128 devices in a mesh: ctx: 8 (over y, core), exp: 16 (over x, z).
Axes of the slice: x: 4, y: 4, z: 4, core: 2. Of those that a mesh axis runs over, the one named last changes fastest.
Arguments:
- mixer_input: bfloat16 [1024, 2, 8192], P('ctx', None, 'exp'), may hold values from -6 to 6
- gate_in: bfloat16 [1024, 2, 8192], P('ctx', None, 'exp'), may hold values from -6 to 6
- step_size: float32 [1024, 2, 8192], P('ctx', None, 'exp'), may hold values from 0.004 to 10
- decay_rate: float32 [16, 8192], P(None, 'exp'), may hold values from 0.03 to 2.5
- state_in: float32 [1024, 2, 16], P('ctx'), may hold values from -6 to 6
- state_out: float32 [1024, 2, 16], P('ctx'), may hold values from -6 to 6
- skip: float32 [8192], P('exp'), may hold values from 0.5 to 1.5
- out_proj: bfloat16 [8192, 4096], P('exp', 'ctx'), may hold values from -0.0625 to 0.0625
- hidden_in: bfloat16 [1024, 2, 4096], P('ctx', None, 'exp'), may hold values from -14 to 14
- norm_gain: float32 [4096], replicated, may hold values from 0.4 to 2.5
- w_gate: bfloat16 [16, 4096, 7168], P('exp', None, 'ctx'), may hold values from -0.09375 to 0.09375
- w_up: bfloat16 [16, 4096, 7168], P('exp', None, 'ctx'), may hold values from -0.09375 to 0.09375
- w_down: bfloat16 [16, 7168, 4096], P('exp', 'ctx'), may hold values from -0.0625 to 0.0625
- route_ids: int32 [1024, 2, 2], P('ctx'), may hold values from 0 to 15, all different within a row; in each aligned block of 256 rows (0 to 255, 256 to 511, ..., all dimensions but the last counted through in order) at most 64 rows name the same one
- route_weight: float32 [1024, 2, 2], P('ctx'), may hold values from 0.1 to 0.9
Outputs:
- layer_out: bfloat16 [1024, 2, 4096], P('ctx', None, 'exp')
The draws below stay inside these ranges and needn't reach their ends.
Inputs may be any that keep to these rules, and one draw needn't show every extreme that they name: `route_ids`: the 2 experts of a token differ; within the rows of one index of ctx no expert is named by more than 64 rows.
All inputs are finite; a program needn't handle non-finite values.
Results may differ from the reference program's by a relative error of at most 0.009.
Values may be sent and summed in bfloat16 or wider, within the bound.
No kernel may reach another device: no remote copies, remote signals or barrier semaphores. Data moves between devices by JAX's collectives and lax.ppermute only.
A program may use at most 192 MiB of HBM per device.

```python
import math
import jax
import jax.numpy as jnp
import numpy as np
from jax import lax

D = 4096
STATE = 16
TOP = 2
INNER = 8192
HID = 7168
BATCH = 2
EXPERTS = 16
TOK_DEV = 256
LEN = 1024
CAP = 64
N_CTX = 8


def draw_step_size(key, part):
    key_base, key_where, key_height = jax.random.split(key, 3)
    shape = (LEN, BATCH, INNER)
    baseline = 0.01 * jnp.exp(jax.random.uniform(key_base, shape, jnp.float32, -0.7, 0.7))
    spots = jax.random.randint(key_where, (2, BATCH), 0, LEN)
    places = jnp.arange(LEN)[:, None]
    bursting = jnp.any(places[None, :, :] == spots[:, None, :], axis=0)
    heights = jnp.exp(jax.random.uniform(key_height, shape, jnp.float32, math.log(5.0), math.log(10.0)))
    return jnp.where(bursting[:, :, None], heights, baseline)


def draw_decay_rate(key, part):
    shape = (STATE, INNER)
    expo = jax.random.uniform(key, shape, jnp.float32, math.log(0.03), math.log(2.5))
    return jnp.exp(expo)


def draw_hidden_in(key, part):
    key_value, key_rough = jax.random.split(jax.random.fold_in(key, 7), 2)
    shape = (LEN, BATCH, D)
    place = jnp.arange(D, dtype=jnp.float32) / max(D - 1, 1)
    rough = jnp.exp(jax.random.uniform(key_rough, (D,), jnp.float32, math.log(0.7), math.log(1.4)))
    profile = jnp.exp(math.log(0.3) + (math.log(3.0) - math.log(0.3)) * place) * rough
    values = jnp.clip(jax.random.normal(key_value, shape, jnp.float32), -3.0, 3.0)
    return (values * profile).astype(jnp.bfloat16)


def shard_levels(rng, shape, cuts, smallest, largest):
    loudness = 1.0
    for axis_at, parts in cuts:
        draws = jax.random.uniform(jax.random.fold_in(jax.random.fold_in(rng, 6), axis_at), (parts,), jnp.float32, smallest / len(cuts), largest / len(cuts))
        loudness = loudness * jnp.repeat(jnp.exp(draws), shape[axis_at] // parts).reshape((-1,) + (1,) * (len(shape) - 1 - axis_at))
    return loudness


def deal_out(own_key, own, number, rows, number_of, top, bound, slope):
    ranking = jax.random.permutation(own_key, number_of)
    packed, common = shares(number_of, rows * top, bound, slope, True), shares(number_of, rows * top, bound, slope, False)
    places = jnp.arange(number_of)

    def named(sizes, offset_by):
        used = int((sizes > 0).sum())
        fixed = max(1, used // 4)
        passed = fixed + (places - fixed + offset_by * (used - fixed)) % max(1, number_of - fixed)
        return jnp.zeros((number_of,), jnp.int32).at[ranking[jnp.where(places < fixed, places, passed)]].set(jnp.asarray(sizes, jnp.int32))

    sizes = jnp.where(number % 4 == 0, named(packed, number // 4), named(common, number - number // 4 - 1))
    mixed = jax.random.permutation(jax.random.fold_in(own, 3), number_of)
    donor, receiver = mixed[0:number_of // 2 * 2:2], mixed[1:number_of // 2 * 2:2]
    room = jnp.minimum(sizes[donor] - 1, bound - sizes[receiver]) // 2
    room = jnp.where((donor == ranking[0]) | (receiver == ranking[0]) | (sizes[receiver] == 0), 0, jnp.maximum(room, 0))
    passed = jax.random.randint(jax.random.fold_in(own, 4), (number_of // 2,), 0, 1 << 20) % (room + 1)
    sizes = sizes.at[donor].add(-passed).at[receiver].add(passed)
    items = jnp.searchsorted(jnp.cumsum(sizes), jnp.arange(rows * top), side="right").astype(jnp.int32)
    listing = items.reshape(top, rows).T
    listing = listing[jax.random.permutation(jax.random.fold_in(own, 1), rows)]
    offset_by = jax.random.randint(jax.random.fold_in(own, 2), (rows, 1), 0, top)
    return jnp.take_along_axis(listing, (jnp.arange(top)[None, :] + offset_by) % top, axis=1)


def shares(amount, total, most, skew, full):
    weights = [(1 << 20) // math.isqrt(grade ** skew) + 1 for grade in range(1, amount + 1)]
    largest = most if full else min(most, max(-(-total // amount), total * weights[0] // sum(weights)))
    least = 1 if total - largest >= amount - 1 else 0
    holding, spare = [largest] + [least] * (amount - 1), total - largest - least * (amount - 1)
    while spare > 0:
        candidates = [i for i in range(1, amount) if holding[i] < largest] or [i for i in range(1, amount) if holding[i] < most]
        mass, budget = sum([weights[i] for i in candidates]), spare
        for i in candidates:
            more = min(most - holding[i], max(1, budget * weights[i] // mass), spare)
            holding[i] = holding[i] + more
            spare = spare - more
    return np.array(holding)


def scatter_about(rng, extent, spread, limit, pieces=(), held_as=jnp.bfloat16):
    level = shard_levels(rng, extent, pieces, -0.22, 0.18) if pieces else 1.0
    values = jax.random.normal(rng, extent, jnp.float32) * spread * level
    return jnp.minimum(jnp.maximum(values, -limit), limit).astype(held_as)


def setup_inputs(seed: int = 0) -> dict:
    streams_of = jax.random.split(jax.random.key(seed), 16)
    mixer_input = scatter_about(streams_of[0], (LEN, BATCH, INNER), 1.0, 6.0, ((0, 8), (2, 16)))
    gate_in = scatter_about(streams_of[1], (LEN, BATCH, INNER), 1.0, 6.0, ((0, 8), (2, 16)))
    step_size = draw_step_size(jax.random.fold_in(streams_of[15], 71), 0)
    decay_rate = draw_decay_rate(jax.random.fold_in(streams_of[15], 71), 0)
    state_in = scatter_about(streams_of[4], (LEN, BATCH, STATE), 1.0, 6.0, ((0, 8),), jnp.float32)
    state_out = scatter_about(streams_of[5], (LEN, BATCH, STATE), 1.0, 6.0, ((0, 8),), jnp.float32)
    skip = jnp.clip(0.5 + 1.0 * jax.random.uniform(streams_of[6], (INNER,), jnp.float32) ** shard_levels(streams_of[6], (INNER,), ((0, 16),), -0.2, 0.2), 0.5, 1.5)
    out_proj = scatter_about(streams_of[7], (INNER, D), INNER ** -0.5, 0.0625, ((0, 16), (1, 8)))
    hidden_in = draw_hidden_in(jax.random.fold_in(streams_of[15], 71), 0)
    norm_gain = jnp.clip(jnp.exp(jax.random.uniform(streams_of[9], (D,), jnp.float32, math.log(0.4), math.log(2.5))), 0.4, 2.5)
    w_gate = scatter_about(streams_of[10], (EXPERTS, D, HID), D ** -0.5, 0.09375, ((0, 16), (2, 8)))
    w_up = scatter_about(streams_of[11], (EXPERTS, D, HID), D ** -0.5, 0.09375, ((0, 16), (2, 8)))
    w_down = scatter_about(streams_of[12], (EXPERTS, HID, D), HID ** -0.5, 0.0625, ((0, 16), (1, 8)))
    route_ids_keys = jax.random.split(jax.random.fold_in(streams_of[13], 1), LEN * BATCH // TOK_DEV)
    route_ids_turns = jax.random.permutation(jax.random.fold_in(streams_of[13], 3), LEN * BATCH // TOK_DEV)
    route_ids = jax.vmap(lambda own, number: deal_out(jax.random.fold_in(streams_of[13], 2), own, number, TOK_DEV, EXPERTS, TOP, CAP, 2))(route_ids_keys, route_ids_turns).reshape((LEN, BATCH, TOP))
    route_weight = jnp.clip(0.1 + 0.79999997 * jax.random.uniform(streams_of[14], (LEN, BATCH, TOP), jnp.float32) ** shard_levels(streams_of[14], (LEN, BATCH, TOP), ((0, 8),), -0.2, 0.2), 0.1, 0.9)
    return dict(mixer_input=mixer_input, gate_in=gate_in, step_size=step_size, decay_rate=decay_rate, state_in=state_in, state_out=state_out, skip=skip, out_proj=out_proj, hidden_in=hidden_in, norm_gain=norm_gain, w_gate=w_gate, w_up=w_up, w_down=w_down, route_ids=route_ids, route_weight=route_weight)


epsilon = 1e-06

def reference(mixer_input, gate_in, step_size, decay_rate, state_in, state_out, skip, out_proj, hidden_in, norm_gain, w_gate, w_up, w_down, route_ids, route_weight):
    signal = mixer_input.astype(jnp.float32)

    def advance(carried, inputs):
        sig_now, step_now, into_now, outof_now = inputs
        factor = jnp.exp(-step_now[:, None, :] * decay_rate[None, :, :])
        carried = factor * carried + (step_now * sig_now)[:, None, :] * into_now[:, :, None]
        return (carried, lax.optimization_barrier(jnp.sum(outof_now[:, :, None] * carried, axis=1)))
    start_state = jnp.zeros((BATCH, STATE, INNER), jnp.float32)
    _, scanned = lax.scan(advance, start_state, (signal, step_size, state_in, state_out))
    mixed = ((scanned + skip * signal) * jax.nn.silu(gate_in.astype(jnp.float32))).astype(jnp.bfloat16)
    all_rows = LEN * BATCH
    mixer_proj = jnp.dot(mixed.reshape(all_rows, INNER), out_proj, preferred_element_type=jnp.float32)
    residual = hidden_in.reshape(all_rows, D).astype(jnp.float32) + mixer_proj
    scale_rows = lax.rsqrt(lax.optimization_barrier(jnp.mean(residual * residual, axis=1)) + epsilon)
    normed = (residual * scale_rows[:, None] * norm_gain).astype(jnp.bfloat16)
    routed = route_ids.reshape(all_rows, TOP)
    weights = route_weight.reshape(all_rows, TOP)
    group = HID // N_CTX
    total_slots = N_CTX * CAP
    row_ids = jnp.arange(all_rows, dtype=jnp.int32)
    block_ids = row_ids // TOK_DEV

    def expert_term(expert, accum):
        matches = routed == expert
        chosen = jnp.any(matches, axis=1)
        strength = lax.optimization_barrier(jnp.sum(jnp.where(matches, weights, 0.0), axis=1))
        position = jnp.cumsum(chosen.astype(jnp.int32).reshape(N_CTX, TOK_DEV), axis=1).reshape(all_rows) - 1
        slot_of = jnp.where(chosen, block_ids * CAP + position, total_slots).astype(jnp.int32)
        slot_token = jnp.zeros((total_slots,), jnp.int32).at[slot_of].set(row_ids, mode='drop')
        filled = jnp.zeros((total_slots,), jnp.bool_).at[slot_of].set(True, mode='drop')
        gathered = jnp.where(filled[:, None], normed[slot_token], jnp.zeros((), jnp.bfloat16)).astype(jnp.bfloat16)
        gate_part = jnp.dot(gathered, w_gate[expert], preferred_element_type=jnp.float32)
        up_part = jnp.dot(gathered, w_up[expert], preferred_element_type=jnp.float32)
        activ = (jax.nn.silu(gate_part) * up_part).astype(jnp.bfloat16)
        down_all = w_down[expert]
        returned = jnp.zeros((total_slots, D), jnp.float32)
        for grp in range(N_CTX):
            partial_value = jnp.dot(activ[:, grp * group:(grp + 1) * group], down_all[grp * group:(grp + 1) * group], preferred_element_type=jnp.float32).astype(jnp.bfloat16)
            partial_value = lax.optimization_barrier(partial_value)
            returned = returned + partial_value.astype(jnp.float32)
        picked = returned[jnp.clip(slot_of, 0, total_slots - 1)]
        return accum + jnp.where(chosen, strength, 0.0)[:, None] * picked
    experts_sum = lax.fori_loop(0, EXPERTS, expert_term, jnp.zeros((all_rows, D), jnp.float32))
    return (residual + experts_sum).astype(jnp.bfloat16).reshape(LEN, BATCH, D)
```

```python
import functools

import jax
import jax.numpy as jnp
from jax import lax
from jax.experimental import pallas as pl
from jax.experimental.pallas import tpu as pltpu
from jax.sharding import PartitionSpec as P

epsilon = 1e-06
LOG2E = 1.4426950408889634
SUBS = 8
LANES = 128
MIB = 1 << 20
f32, bf16 = jnp.float32, jnp.bfloat16


def params(mib):
    return pltpu.CompilerParams(vmem_limit_bytes=mib * MIB)


def vmem():
    return pl.BlockSpec(memory_space=pltpu.VMEM)


def smem():
    return pl.BlockSpec(memory_space=pltpu.SMEM)


def anywhere():
    return pl.BlockSpec(memory_space=pl.ANY)


def spread(table_ref, out_ref):
    turns, _, columns = table_ref.shape

    def turn(t, _):
        row = table_ref[t]
        for i in range(columns):
            out_ref[t, i] = jnp.broadcast_to(row[:, i : i + 1], (SUBS, LANES))
        return 0

    lax.fori_loop(0, turns, turn, 0)


def split_lanes(step_ref, sig_ref, st4, v4):
    for q in range(st4.shape[0]):
        lanes = slice(q * LANES, (q + 1) * LANES)
        st = step_ref[:, lanes]
        st4[q] = st
        v4[q] = st * sig_ref[:, lanes].astype(f32)


def first_pass(step_ref, sig_ref, into_ref, rate_ref, fin_ref, before_ref, pre_ref, st4, v4, into_b):
    states, channels = rate_ref.shape
    prompts = fin_ref.shape[0]
    turns = into_ref.shape[0]
    hop = turns * prompts
    spread(into_ref, into_b)
    split_lanes(step_ref, sig_ref, st4, v4)
    sub = lax.broadcasted_iota(jnp.int32, (SUBS, LANES), 0)
    for q in range(channels // LANES):
        lanes = slice(q * LANES, (q + 1) * LANES)
        rates = [
            jnp.broadcast_to(rate_ref[n : n + 1, lanes] * -LOG2E, (SUBS, LANES)) for n in range(states)
        ]
        for b in range(prompts):

            def turn(t, held, q=q, b=b, rates=rates):
                total, hs = held
                st = st4[q, pl.ds(t * prompts + b, SUBS, stride=hop), :]
                v = v4[q, pl.ds(t * prompts + b, SUBS, stride=hop), :]
                new = []
                for n in range(states):
                    new.append(jnp.exp2(st * rates[n]) * hs[n] + v * into_b[t, b * states + n])
                return total + st, tuple(new)

            zero = jnp.zeros((SUBS, LANES), f32)
            width, hs = lax.fori_loop(0, turns, turn, (zero, (zero,) * states))
            hs = list(hs)
            for d in (1, 2, 4):
                live = sub >= d
                for n in range(states):
                    moved = jnp.where(live, pltpu.roll(hs[n], d, 0), 0.0)
                    hs[n] = hs[n] + jnp.exp2(rates[n] * width) * moved
                width = width + jnp.where(live, pltpu.roll(width, d, 0), 0.0)
            for n in range(states):
                fin_ref[b, n : n + 1, lanes] = hs[n][SUBS - 1 :]
                before_ref[b, n, :, lanes] = jnp.where(sub >= 1, pltpu.roll(hs[n], 1, 0), 0.0)
            fin_ref[b, states : states + 1, lanes] = width[SUBS - 1 :]
            pre_ref[b, :, lanes] = jnp.where(sub >= 1, pltpu.roll(width, 1, 0), 0.0)


def second_pass(
    mine_ref, step_ref, sig_ref, gate_ref, into_ref, outof_ref, rate_ref, skip_ref, before_ref, pre_ref,
    ends_ref, proj_hbm, out_ref, st4, v4, y4, into_b, outof_b, enter, mixed, proj, sem,
):
    states, channels = rate_ref.shape
    prompts = pre_ref.shape[0]
    turns = into_ref.shape[0]
    hop = turns * prompts
    fetch = pltpu.make_async_copy(proj_hbm, proj, sem)
    fetch.start()
    spread(into_ref, into_b)
    spread(outof_ref, outof_b)
    split_lanes(step_ref, sig_ref, st4, v4)
    mine = mine_ref[0]
    for q in range(channels // LANES):
        lanes = slice(q * LANES, (q + 1) * LANES)
        rate_q = rate_ref[:, lanes] * -LOG2E
        rates = [jnp.broadcast_to(rate_q[n : n + 1], (SUBS, LANES)) for n in range(states)]
        for b in range(prompts):
            h0 = jnp.zeros((states, LANES), f32)
            for c in range(ends_ref.shape[0] - 1):
                live = jnp.where(c < mine, 1.0, 0.0).astype(f32)
                decay = jnp.exp2(rate_q * (ends_ref[c, b, states : states + 1, lanes] * live))
                h0 = decay * h0 + ends_ref[c, b, :states, lanes] * live
            enter[...] = h0
            pre = pre_ref[b, :, lanes]
            hs = tuple(
                before_ref[b, n, :, lanes]
                + jnp.exp2(rates[n] * pre) * jnp.broadcast_to(enter[n : n + 1], (SUBS, LANES))
                for n in range(states)
            )

            def turn(t, hs, q=q, b=b, rates=rates):
                rows = pl.ds(t * prompts + b, SUBS, stride=hop)
                st = st4[q, rows, :]
                v = v4[q, rows, :]
                new, sums = [], [None] * 4
                for n in range(states):
                    h = jnp.exp2(st * rates[n]) * hs[n] + v * into_b[t, b * states + n]
                    new.append(h)
                    term = h * outof_b[t, b * states + n]
                    sums[n % 4] = term if sums[n % 4] is None else sums[n % 4] + term
                y4[q, rows, :] = (sums[0] + sums[1]) + (sums[2] + sums[3])
                return tuple(new)

            lax.fori_loop(0, turns, turn, hs)
        sig = sig_ref[:, lanes].astype(f32)
        gate = gate_ref[:, lanes].astype(f32)
        y = y4[q] + skip_ref[:, lanes] * sig
        mixed[:, lanes] = (y * (gate / (1.0 + jnp.exp(-gate)))).astype(bf16)
    fetch.wait()
    width = out_ref.shape[2]
    blocks, _, columns = proj.shape
    for c in range(blocks):
        part = jnp.dot(mixed[...], proj[c], preferred_element_type=f32).astype(bf16)
        for i in range(columns // width):
            out_ref[c * (columns // width) + i] = part[:, i * width : (i + 1) * width]


def dispatch(recv_ref, hidden_ref, ids_ref, res_ref, slots_ref, pick):
    experts, slots, width = slots_ref.shape
    tokens = hidden_ref.shape[0]
    total = hidden_ref[...].astype(f32)
    for i in range(recv_ref.shape[0]):
        total = total + recv_ref[i].astype(f32)
    res_ref[...] = total
    expert = lax.broadcasted_iota(jnp.int32, (experts, tokens), 0)
    chosen = jnp.zeros((experts, tokens), f32)
    for k in range(ids_ref.shape[0]):
        chosen = jnp.where(ids_ref[k : k + 1, :] == expert, 1.0, chosen)
    row = lax.broadcasted_iota(jnp.int32, (tokens, tokens), 0)
    col = lax.broadcasted_iota(jnp.int32, (tokens, tokens), 1)
    earlier = jnp.where(row < col, 1.0, 0.0).astype(bf16)
    place = jnp.dot(chosen.astype(bf16), earlier, preferred_element_type=f32)
    place = jnp.where(chosen > 0.5, place, -1.0)
    slot = lax.broadcasted_iota(jnp.int32, (slots, tokens), 0).astype(f32)
    for e in range(experts):
        pick[e * slots : (e + 1) * slots] = jnp.where(place[e : e + 1] == slot, 1.0, 0.0).astype(bf16)
    rows = jnp.dot(pick[...], total.astype(bf16), preferred_element_type=f32).astype(bf16)
    slots_ref[...] = rows.reshape(experts, slots, width)


def normalize(recv_ref, gain_ref, out_ref):
    blocks, slots, width = recv_ref.shape
    square = jnp.zeros((slots, width), f32)
    for i in range(blocks):
        part = recv_ref[i].astype(f32)
        square = square + part * part
    mean = jnp.sum(square, axis=1, keepdims=True) / (blocks * width)
    scale = lax.rsqrt(mean + epsilon)
    for i in range(blocks):
        lanes = slice(i * width, (i + 1) * width)
        out_ref[:, lanes] = (recv_ref[i].astype(f32) * scale * gain_ref[:, lanes]).astype(bf16)


def feed_forward(x_ref, gate_hbm, up_hbm, down_hbm, out_ref, gates, ups, downs, act, gate_sem, up_sem, down_sem):
    pieces, _, wide = gates.shape
    blocks, _, width = downs.shape
    slabs, _, slots, _ = out_ref.shape

    def gate_copy(i):
        return pltpu.make_async_copy(gate_hbm.at[:, pl.ds(i * wide, wide)], gates.at[i], gate_sem.at[i])

    def up_copy(i):
        return pltpu.make_async_copy(up_hbm.at[:, pl.ds(i * wide, wide)], ups.at[i], up_sem.at[i])

    def down_copy(i):
        return pltpu.make_async_copy(down_hbm.at[:, pl.ds(i * width, width)], downs.at[i], down_sem.at[i])

    for i in range(pieces):
        gate_copy(i).start()
        up_copy(i).start()
    for i in range(blocks):
        down_copy(i).start()
    for i in range(pieces):
        gate_copy(i).wait()
        up_copy(i).wait()
        both = jnp.concatenate([gates[i], ups[i]], axis=1)
        part = jnp.dot(x_ref[...], both, preferred_element_type=f32)
        g, u = part[:, :wide], part[:, wide:]
        act[:, i * wide : (i + 1) * wide] = (g / (1.0 + jnp.exp(-g)) * u).astype(bf16)
    for i in range(blocks):
        down_copy(i).wait()

    @pl.loop(0, blocks)
    def _(i):
        part = jnp.dot(act[...], downs[i], preferred_element_type=f32).astype(bf16)
        for s in range(slabs):
            out_ref[s, i] = part[s * slots : (s + 1) * slots]


def combine(recv_ref, ids_ref, weight_ref, res_ref, out_ref):
    experts, slots, width = recv_ref.shape
    tokens, top = ids_ref.shape
    rows = recv_ref[...].reshape(experts * slots, width)
    expert = lax.broadcasted_iota(jnp.int32, (tokens, experts), 1)
    named = [ids_ref[:, k : k + 1] == expert for k in range(top)]
    chosen = jnp.zeros((tokens, experts), f32)
    for k in range(top):
        chosen = jnp.where(named[k], 1.0, chosen)
    row = lax.broadcasted_iota(jnp.int32, (tokens, tokens), 0)
    col = lax.broadcasted_iota(jnp.int32, (tokens, tokens), 1)
    earlier = jnp.where(col < row, 1.0, 0.0).astype(bf16)
    place = jnp.dot(earlier, chosen.astype(bf16), preferred_element_type=f32)
    place = place + (expert * slots).astype(f32)
    slot = lax.broadcasted_iota(jnp.int32, (tokens, experts * slots), 1)
    total = res_ref[...]
    for k in range(top):
        at = jnp.sum(jnp.where(named[k], place, 0.0), axis=1, keepdims=True).astype(jnp.int32)
        pick = jnp.where(slot == at, 1.0, 0.0).astype(bf16)
        total = total + weight_ref[:, k : k + 1] * jnp.dot(pick, rows, preferred_element_type=f32)
    out_ref[...] = total.astype(out_ref.dtype)


def scan_tables(table, turns):
    return table.reshape(SUBS, turns, -1).transpose(1, 0, 2)


def run_first(step, sig, into, rate, prompts):
    tokens, channels = step.shape
    states = rate.shape[0]
    turns = into.shape[0]
    tiles = channels // LANES
    return pl.pallas_call(
        first_pass,
        out_shape=(
            jax.ShapeDtypeStruct((prompts, states + 1, channels), f32),
            jax.ShapeDtypeStruct((prompts, states, SUBS, channels), f32),
            jax.ShapeDtypeStruct((prompts, SUBS, channels), f32),
        ),
        in_specs=[vmem()] * 4,
        out_specs=(vmem(),) * 3,
        scratch_shapes=[
            pltpu.VMEM((tiles, tokens, LANES), f32),
            pltpu.VMEM((tiles, tokens, LANES), f32),
            pltpu.VMEM((turns, prompts * states, SUBS, LANES), f32),
        ],
        compiler_params=params(24),
        name="scan_first",
    )(step, sig, into, rate)


def run_second(mine, step, sig, gate, into, outof, rate, skip, before, pre, ends, proj, share):
    tokens, channels = step.shape
    prompts, states = before.shape[:2]
    turns = into.shape[0]
    tiles = channels // LANES
    return pl.pallas_call(
        second_pass,
        out_shape=jax.ShapeDtypeStruct((proj.shape[0] * proj.shape[2] // share, tokens, share), bf16),
        in_specs=[smem()] + [vmem()] * 10 + [anywhere()],
        out_specs=vmem(),
        scratch_shapes=[
            pltpu.VMEM((tiles, tokens, LANES), f32),
            pltpu.VMEM((tiles, tokens, LANES), f32),
            pltpu.VMEM((tiles, tokens, LANES), f32),
            pltpu.VMEM((turns, prompts * states, SUBS, LANES), f32),
            pltpu.VMEM((turns, prompts * states, SUBS, LANES), f32),
            pltpu.VMEM((states, LANES), f32),
            pltpu.VMEM((tokens, channels), bf16),
            pltpu.VMEM(proj.shape, bf16),
            pltpu.SemaphoreType.DMA,
        ],
        compiler_params=params(32),
        name="scan_second",
    )(mine, step, sig, gate, into, outof, rate, skip, before, pre, ends, proj)


def run_dispatch(recv, hidden, ids, experts, slots):
    tokens, share = hidden.shape
    return pl.pallas_call(
        dispatch,
        out_shape=(
            jax.ShapeDtypeStruct((tokens, share), f32),
            jax.ShapeDtypeStruct((experts, slots, share), bf16),
        ),
        in_specs=[vmem()] * 3,
        out_specs=(vmem(),) * 2,
        scratch_shapes=[pltpu.VMEM((experts * slots, tokens), bf16)],
        compiler_params=params(16),
        name="dispatch",
    )(recv, hidden, ids)


def run_normalize(recv, gain):
    blocks, slots, width = recv.shape
    return pl.pallas_call(
        normalize,
        out_shape=jax.ShapeDtypeStruct((slots, blocks * width), bf16),
        in_specs=[vmem()] * 2,
        out_specs=vmem(),
        compiler_params=params(8),
        name="normalize",
    )(recv, gain)


def run_ffn(x, w_gate, w_up, w_down, slabs, share):
    rows, depth = x.shape
    hidden = w_gate.shape[1]
    wide = LANES
    pieces, blocks = hidden // wide, w_down.shape[1] // share
    return pl.pallas_call(
        feed_forward,
        out_shape=jax.ShapeDtypeStruct((slabs, blocks, rows // slabs, share), bf16),
        in_specs=[vmem()] + [anywhere()] * 3,
        out_specs=vmem(),
        scratch_shapes=[
            pltpu.VMEM((pieces, depth, wide), bf16),
            pltpu.VMEM((pieces, depth, wide), bf16),
            pltpu.VMEM((blocks, hidden, share), bf16),
            pltpu.VMEM((rows, hidden), bf16),
            pltpu.SemaphoreType.DMA((pieces,)),
            pltpu.SemaphoreType.DMA((pieces,)),
            pltpu.SemaphoreType.DMA((blocks,)),
        ],
        compiler_params=params(48),
        name="feed_forward",
    )(x, w_gate, w_up, w_down)


def run_combine(recv, ids, weights, res):
    return pl.pallas_call(
        combine,
        out_shape=jax.ShapeDtypeStruct(res.shape, bf16),
        in_specs=[vmem()] * 4,
        out_specs=vmem(),
        compiler_params=params(16),
        name="combine",
    )(recv, ids, weights, res)


def on_device(
    mixer_input, gate_in, step_size, decay_rate, state_in, state_out, skip, out_proj, hidden_in, norm_gain,
    w_gate, w_up, w_down, route_ids, route_weight,
):
    slab_len, prompts, channels = mixer_input.shape
    tokens = slab_len * prompts
    share = hidden_in.shape[2]
    slabs = lax.axis_size("ctx")
    experts = lax.axis_size("exp") * w_gate.shape[0]
    slots = 4 * tokens // experts
    turns = slab_len // SUBS
    proj = lax.all_gather(out_proj, "ctx")
    sig = mixer_input.reshape(tokens, channels)
    step = step_size.reshape(tokens, channels)
    into = scan_tables(state_in, turns)
    outof = scan_tables(state_out, turns)
    end, before, pre = run_first(step, sig, into, decay_rate, prompts)
    ends = lax.all_gather(end, "ctx")
    mine = lax.axis_index("ctx").astype(jnp.int32).reshape(1)
    gate = gate_in.reshape(tokens, channels)
    partial_value = run_second(
        mine, step, sig, gate, into, outof, decay_rate, skip.reshape(1, channels), before, pre, ends, proj, share
    )
    recv = lax.all_to_all(partial_value, "exp", 0, 0, tiled=True)
    ids = route_ids.reshape(tokens, -1)
    residual, slot_rows = run_dispatch(recv, hidden_in.reshape(tokens, share), ids.T, experts, slots)
    whole = lax.all_to_all(slot_rows, "exp", 0, 0, tiled=True)
    normed = run_normalize(whole, norm_gain.reshape(1, -1))
    segment = lax.all_gather(normed, "ctx", axis=0, tiled=True)
    part = run_ffn(segment, w_gate[0], w_up[0], w_down[0], slabs, share)
    returned = lax.psum_scatter(part, "ctx", scatter_dimension=0, tiled=True)[0]
    back = lax.all_to_all(returned, "exp", 0, 0, tiled=True)
    out = run_combine(back, ids, route_weight.reshape(tokens, -1), residual)
    return out.reshape(slab_len, prompts, share)


def solution(mesh):
    placed = (
        P("ctx", None, "exp"),
        P("ctx", None, "exp"),
        P("ctx", None, "exp"),
        P(None, "exp"),
        P("ctx", None, None),
        P("ctx", None, None),
        P("exp"),
        P("exp", "ctx"),
        P("ctx", None, "exp"),
        P(),
        P("exp", None, "ctx"),
        P("exp", None, "ctx"),
        P("exp", "ctx", None),
        P("ctx", None, None),
        P("ctx", None, None),
    )
    return jax.shard_map(
        on_device, mesh=mesh, in_specs=placed, out_specs=P("ctx", None, "exp"), check_vma=False
    )
```

```python
import functools

import jax
import jax.numpy as jnp
from jax import lax
from jax.experimental import pallas as pl
from jax.experimental.pallas import tpu as pltpu
from jax.sharding import Mesh
from jax.sharding import PartitionSpec as P

epsilon = 1e-06
LOG2E = 1.4426950408889634
SUBS = 8
LANES = 128
MIB = 1 << 20
f32, bf16 = jnp.float32, jnp.bfloat16


def params(mib):
    return pltpu.CompilerParams(vmem_limit_bytes=mib * MIB)


def vmem():
    return pl.BlockSpec(memory_space=pltpu.VMEM)


def smem():
    return pl.BlockSpec(memory_space=pltpu.SMEM)


def anywhere():
    return pl.BlockSpec(memory_space=pl.ANY)


def spread(table_ref, out_ref):
    turns, _, columns = table_ref.shape

    def turn(t, _):
        row = table_ref[t]
        for i in range(columns):
            out_ref[t, i] = jnp.broadcast_to(row[:, i : i + 1], (SUBS, LANES))
        return 0

    lax.fori_loop(0, turns, turn, 0)


def split_lanes(step_ref, sig_ref, st4, v4):
    for q in range(st4.shape[0]):
        lanes = slice(q * LANES, (q + 1) * LANES)
        st = step_ref[:, lanes]
        st4[q] = st
        v4[q] = st * sig_ref[:, lanes].astype(f32)


def first_pass(step_ref, sig_ref, into_ref, rate_ref, fin_ref, before_ref, pre_ref, st4, v4, into_b):
    states, channels = rate_ref.shape
    prompts = fin_ref.shape[0]
    turns = into_ref.shape[0]
    hop = turns * prompts
    spread(into_ref, into_b)
    split_lanes(step_ref, sig_ref, st4, v4)
    sub = lax.broadcasted_iota(jnp.int32, (SUBS, LANES), 0)
    for q in range(channels // LANES):
        lanes = slice(q * LANES, (q + 1) * LANES)
        rates = [
            jnp.broadcast_to(rate_ref[n : n + 1, lanes] * -LOG2E, (SUBS, LANES)) for n in range(states)
        ]
        for b in range(prompts):

            def turn(t, held, q=q, b=b, rates=rates):
                total, hs = held
                st = st4[q, pl.ds(t * prompts + b, SUBS, stride=hop), :]
                v = v4[q, pl.ds(t * prompts + b, SUBS, stride=hop), :]
                new = []
                for n in range(states):
                    new.append(jnp.exp2(st * rates[n]) * hs[n] + v * into_b[t, b * states + n])
                return total + st, tuple(new)

            zero = jnp.zeros((SUBS, LANES), f32)
            width, hs = lax.fori_loop(0, turns, turn, (zero, (zero,) * states))
            hs = list(hs)
            for d in (1, 2, 4):
                live = sub >= d
                for n in range(states):
                    moved = jnp.where(live, pltpu.roll(hs[n], d, 0), 0.0)
                    hs[n] = hs[n] + jnp.exp2(rates[n] * width) * moved
                width = width + jnp.where(live, pltpu.roll(width, d, 0), 0.0)
            for n in range(states):
                fin_ref[b, n : n + 1, lanes] = hs[n][SUBS - 1 :]
                before_ref[b, n, :, lanes] = jnp.where(sub >= 1, pltpu.roll(hs[n], 1, 0), 0.0)
            fin_ref[b, states : states + 1, lanes] = width[SUBS - 1 :]
            pre_ref[b, :, lanes] = jnp.where(sub >= 1, pltpu.roll(width, 1, 0), 0.0)


def pair_up(core_ref, own_ref, sib_ref, rate_ref, out_ref):
    states = rate_ref.shape[0]
    low = core_ref[0] == 0
    rate = rate_ref[...] * -LOG2E
    for b in range(own_ref.shape[0]):
        first = jnp.where(low, own_ref[b], sib_ref[b])
        second = jnp.where(low, sib_ref[b], own_ref[b])
        decay = jnp.exp2(rate * second[states:])
        out_ref[b, :states] = decay * first[:states] + second[:states]
        out_ref[b, states:] = first[states:] + second[states:]


def second_pass(
    core_ref, step_ref, sig_ref, gate_ref, into_ref, outof_ref, rate_ref, skip_ref, before_ref, pre_ref,
    *rest, earlier,
):
    sib_ref, *pair_refs = rest[: earlier + 1]
    mixed_ref, st4, v4, y4, into_b, outof_b, enter = rest[earlier + 1 :]
    states, channels = rate_ref.shape
    prompts = pre_ref.shape[0]
    turns = into_ref.shape[0]
    hop = turns * prompts
    spread(into_ref, into_b)
    spread(outof_ref, outof_b)
    split_lanes(step_ref, sig_ref, st4, v4)
    live = jnp.where(core_ref[0] > 0, 1.0, 0.0).astype(f32)
    for q in range(channels // LANES):
        lanes = slice(q * LANES, (q + 1) * LANES)
        rate_q = rate_ref[:, lanes] * -LOG2E
        rates = [jnp.broadcast_to(rate_q[n : n + 1], (SUBS, LANES)) for n in range(states)]
        for b in range(prompts):
            h0 = jnp.zeros((states, LANES), f32)
            for pair in pair_refs:
                h0 = jnp.exp2(rate_q * pair[b, states : states + 1, lanes]) * h0 + pair[b, :states, lanes]
            decay = jnp.exp2(rate_q * (sib_ref[b, states : states + 1, lanes] * live))
            enter[...] = decay * h0 + sib_ref[b, :states, lanes] * live
            pre = pre_ref[b, :, lanes]
            hs = tuple(
                before_ref[b, n, :, lanes]
                + jnp.exp2(rates[n] * pre) * jnp.broadcast_to(enter[n : n + 1], (SUBS, LANES))
                for n in range(states)
            )

            def turn(t, hs, q=q, b=b, rates=rates):
                rows = pl.ds(t * prompts + b, SUBS, stride=hop)
                st = st4[q, rows, :]
                v = v4[q, rows, :]
                new, sums = [], [None] * 4
                for n in range(states):
                    h = jnp.exp2(st * rates[n]) * hs[n] + v * into_b[t, b * states + n]
                    new.append(h)
                    term = h * outof_b[t, b * states + n]
                    sums[n % 4] = term if sums[n % 4] is None else sums[n % 4] + term
                y4[q, rows, :] = (sums[0] + sums[1]) + (sums[2] + sums[3])
                return tuple(new)

            lax.fori_loop(0, turns, turn, hs)
        sig = sig_ref[:, lanes].astype(f32)
        gate = gate_ref[:, lanes].astype(f32)
        y = y4[q] + skip_ref[:, lanes] * sig
        mixed_ref[:, lanes] = (y * (gate / (1.0 + jnp.exp(-gate)))).astype(bf16)


def project(mixed_ref, proj_hbm, out_ref, proj, sem):
    width = out_ref.shape[2]
    blocks, _, columns = proj.shape
    for c in range(blocks):
        pltpu.make_async_copy(proj_hbm.at[c], proj.at[c], sem.at[c]).start()
    for c in range(blocks):
        pltpu.make_async_copy(proj_hbm.at[c], proj.at[c], sem.at[c]).wait()
        part = jnp.dot(mixed_ref[...], proj[c], preferred_element_type=f32).astype(bf16)
        for i in range(columns // width):
            out_ref[c * (columns // width) + i] = part[:, i * width : (i + 1) * width]


def dispatch(recv_ref, hidden_ref, ids_ref, res_ref, slots_ref, pick):
    experts, slots, width = slots_ref.shape
    tokens = hidden_ref.shape[0]
    total = hidden_ref[...].astype(f32)
    for i in range(recv_ref.shape[0]):
        total = total + recv_ref[i].astype(f32)
    res_ref[...] = total
    expert = lax.broadcasted_iota(jnp.int32, (experts, tokens), 0)
    chosen = jnp.zeros((experts, tokens), f32)
    for k in range(ids_ref.shape[0]):
        chosen = jnp.where(ids_ref[k : k + 1, :] == expert, 1.0, chosen)
    row = lax.broadcasted_iota(jnp.int32, (tokens, tokens), 0)
    col = lax.broadcasted_iota(jnp.int32, (tokens, tokens), 1)
    earlier = jnp.where(row < col, 1.0, 0.0).astype(bf16)
    place = jnp.dot(chosen.astype(bf16), earlier, preferred_element_type=f32)
    place = jnp.where(chosen > 0.5, place, -1.0)
    slot = lax.broadcasted_iota(jnp.int32, (slots, tokens), 0).astype(f32)
    for e in range(experts):
        pick[e * slots : (e + 1) * slots] = jnp.where(place[e : e + 1] == slot, 1.0, 0.0).astype(bf16)
    rows = jnp.dot(pick[...], total.astype(bf16), preferred_element_type=f32).astype(bf16)
    slots_ref[...] = rows.reshape(experts, slots, width)


def normalize(recv_ref, gain_ref, out_ref):
    blocks, slots, width = recv_ref.shape
    square = jnp.zeros((slots, width), f32)
    for i in range(blocks):
        part = recv_ref[i].astype(f32)
        square = square + part * part
    mean = jnp.sum(square, axis=1, keepdims=True) / (blocks * width)
    scale = lax.rsqrt(mean + epsilon)
    for i in range(blocks):
        lanes = slice(i * width, (i + 1) * width)
        out_ref[:, lanes] = (recv_ref[i].astype(f32) * scale * gain_ref[:, lanes]).astype(bf16)


def load_weights(after_ref, *refs):
    count = (len(refs) - 2) // 2
    sources, targets, turn_out, sem = refs[:count], refs[count : 2 * count], refs[-2], refs[-1]
    copies = [pltpu.make_async_copy(s, t, sem.at[i]) for i, (s, t) in enumerate(zip(sources, targets))]
    for c in copies:
        c.start()
    turn_out[...] = after_ref[: turn_out.shape[0], : turn_out.shape[1]].astype(f32) * 0.0
    for c in copies:
        c.wait()


def feed_forward(*refs, groups):
    count = sum(sum(g) for g in groups)
    pieces, (w_gate, w_up, w_down, turn_ref) = refs[:count], refs[count : count + 4]
    *outs, turn_out, x, act = refs[count + 4 :]
    at = 0
    for p in pieces:
        x[at : at + p.shape[0]] = p[...]
        at += p.shape[0]
    blocks, rows, width = outs[0].shape
    wide = 2 * LANES
    hidden = w_gate.shape[1]
    for i in range(0, hidden, wide):
        size = min(wide, hidden - i)
        lanes = slice(i, i + size)
        both = jnp.concatenate([w_gate[:, lanes], w_up[:, lanes]], axis=1)
        part = jnp.dot(x[...], both, preferred_element_type=f32)
        g, u = part[:, :size], part[:, size:]
        act[:, lanes] = (g / (1.0 + jnp.exp(-g)) * u).astype(bf16)
    for i in range(blocks):
        part = jnp.dot(act[...], w_down[:, i * width : (i + 1) * width], preferred_element_type=f32)
        part = part.astype(bf16)
        for j, out in enumerate(outs):
            out[i] = part[j * rows : (j + 1) * rows]
    turn_out[...] = turn_ref[...]


def add_up(*refs):
    *parts, out_ref = refs
    for i in range(out_ref.shape[0]):
        total = parts[0][i].astype(f32)
        for p in parts[1:]:
            total = total + p[i].astype(f32)
        out_ref[i] = total.astype(bf16)


def combine(recv_ref, ids_ref, weight_ref, res_ref, out_ref):
    experts, slots, width = recv_ref.shape
    tokens, top = ids_ref.shape
    rows = recv_ref[...].reshape(experts * slots, width)
    expert = lax.broadcasted_iota(jnp.int32, (tokens, experts), 1)
    named = [ids_ref[:, k : k + 1] == expert for k in range(top)]
    chosen = jnp.zeros((tokens, experts), f32)
    for k in range(top):
        chosen = jnp.where(named[k], 1.0, chosen)
    row = lax.broadcasted_iota(jnp.int32, (tokens, tokens), 0)
    col = lax.broadcasted_iota(jnp.int32, (tokens, tokens), 1)
    earlier = jnp.where(col < row, 1.0, 0.0).astype(bf16)
    place = jnp.dot(earlier, chosen.astype(bf16), preferred_element_type=f32)
    place = place + (expert * slots).astype(f32)
    slot = lax.broadcasted_iota(jnp.int32, (tokens, experts * slots), 1)
    total = res_ref[...]
    for k in range(top):
        at = jnp.sum(jnp.where(named[k], place, 0.0), axis=1, keepdims=True).astype(jnp.int32)
        pick = jnp.where(slot == at, 1.0, 0.0).astype(bf16)
        total = total + weight_ref[:, k : k + 1] * jnp.dot(pick, rows, preferred_element_type=f32)
    out_ref[...] = total.astype(out_ref.dtype)


def scan_tables(table, turns):
    return table.reshape(SUBS, turns, -1).transpose(1, 0, 2)


def run_first(step, sig, into, rate, prompts):
    tokens, channels = step.shape
    states = rate.shape[0]
    turns = into.shape[0]
    tiles = channels // LANES
    return pl.pallas_call(
        first_pass,
        out_shape=(
            jax.ShapeDtypeStruct((prompts, states + 1, channels), f32),
            jax.ShapeDtypeStruct((prompts, states, SUBS, channels), f32),
            jax.ShapeDtypeStruct((prompts, SUBS, channels), f32),
        ),
        in_specs=[vmem()] * 4,
        out_specs=(vmem(),) * 3,
        scratch_shapes=[
            pltpu.VMEM((tiles, tokens, LANES), f32),
            pltpu.VMEM((tiles, tokens, LANES), f32),
            pltpu.VMEM((turns, prompts * states, SUBS, LANES), f32),
        ],
        compiler_params=params(24),
        name="scan_first",
    )(step, sig, into, rate)


def run_pair(core, own, sib, rate):
    return pl.pallas_call(
        pair_up,
        out_shape=jax.ShapeDtypeStruct(own.shape, f32),
        in_specs=[smem()] + [vmem()] * 3,
        out_specs=vmem(),
        compiler_params=params(8),
        name="pair_up",
    )(core, own, sib, rate)


def run_second(core, step, sig, gate, into, outof, rate, skip, before, pre, sib, pairs):
    tokens, channels = step.shape
    prompts, states = before.shape[:2]
    turns = into.shape[0]
    tiles = channels // LANES
    return pl.pallas_call(
        functools.partial(second_pass, earlier=len(pairs)),
        out_shape=jax.ShapeDtypeStruct((tokens, channels), bf16),
        in_specs=[smem()] + [vmem()] * (10 + len(pairs)),
        out_specs=vmem(),
        scratch_shapes=[
            pltpu.VMEM((tiles, tokens, LANES), f32),
            pltpu.VMEM((tiles, tokens, LANES), f32),
            pltpu.VMEM((tiles, tokens, LANES), f32),
            pltpu.VMEM((turns, prompts * states, SUBS, LANES), f32),
            pltpu.VMEM((turns, prompts * states, SUBS, LANES), f32),
            pltpu.VMEM((states, LANES), f32),
        ],
        compiler_params=params(16),
        cost_estimate=pl.CostEstimate(flops=2 * 10**9, bytes_accessed=2 * MIB, transcendentals=0),
        name="scan_second",
    )(core, step, sig, gate, into, outof, rate, skip, before, pre, sib, *pairs)


def run_project(mixed, proj, share):
    tokens = mixed.shape[0]
    return pl.pallas_call(
        project,
        out_shape=jax.ShapeDtypeStruct((proj.shape[0] * proj.shape[2] // share, tokens, share), bf16),
        in_specs=[vmem(), anywhere()],
        out_specs=vmem(),
        scratch_shapes=[pltpu.VMEM(proj.shape, bf16), pltpu.SemaphoreType.DMA((proj.shape[0],))],
        compiler_params=params(16),
        name="project",
    )(mixed, proj)


def run_dispatch(recv, hidden, ids, experts, slots):
    tokens, share = hidden.shape
    return pl.pallas_call(
        dispatch,
        out_shape=(
            jax.ShapeDtypeStruct((tokens, share), f32),
            jax.ShapeDtypeStruct((experts, slots, share), bf16),
        ),
        in_specs=[vmem()] * 3,
        out_specs=(vmem(),) * 2,
        scratch_shapes=[pltpu.VMEM((experts * slots, tokens), bf16)],
        compiler_params=params(16),
        name="dispatch",
    )(recv, hidden, ids)


def run_normalize(recv, gain):
    blocks, slots, width = recv.shape
    return pl.pallas_call(
        normalize,
        out_shape=jax.ShapeDtypeStruct((slots, blocks * width), bf16),
        in_specs=[vmem()] * 2,
        out_specs=vmem(),
        compiler_params=params(8),
        name="normalize",
    )(recv, gain)


def run_load(after, *weights):
    return pl.pallas_call(
        load_weights,
        out_shape=[pltpu.VMEM(w.shape, w.dtype) for w in weights] + [jax.ShapeDtypeStruct((8, LANES), f32)],
        in_specs=[vmem()] + [pl.BlockSpec(memory_space=pltpu.HBM)] * len(weights),
        out_specs=[vmem()] * (len(weights) + 1),
        scratch_shapes=[pltpu.SemaphoreType.DMA((len(weights),))],
        compiler_params=params(8),
        cost_estimate=pl.CostEstimate(flops=0, bytes_accessed=2 * sum(w.nbytes for w in weights), transcendentals=0),
        name="load_weights",
    )(after, *[pltpu.with_memory_space_constraint(w, pltpu.HBM) for w in weights])


def run_ffn(groups, weights, turn, share):
    pieces = [p for own, other in groups for p in (*own, *other)]
    rows = sum(p.shape[0] for p in groups[0][0])
    depth, hidden = weights[0].shape
    total = 2 * rows * len(groups)
    part = jax.ShapeDtypeStruct((depth // share, rows, share), bf16)
    weights = [pltpu.with_memory_space_constraint(w, pltpu.VMEM) for w in weights]
    return pl.pallas_call(
        functools.partial(feed_forward, groups=tuple((len(own), len(other)) for own, other in groups)),
        out_shape=(part,) * (2 * len(groups)) + (jax.ShapeDtypeStruct(turn.shape, turn.dtype),),
        in_specs=[vmem()] * (len(pieces) + 4),
        out_specs=(vmem(),) * (2 * len(groups) + 1),
        scratch_shapes=[pltpu.VMEM((total, depth), bf16), pltpu.VMEM((total, hidden), bf16)],
        compiler_params=params(12),
        cost_estimate=pl.CostEstimate(
            flops=6 * total * depth * hidden, bytes_accessed=4 * total * depth, transcendentals=0
        ),
        name="feed_forward",
    )(*pieces, *weights, turn)


def run_add(*parts):
    return pl.pallas_call(
        add_up,
        out_shape=jax.ShapeDtypeStruct(parts[0].shape, bf16),
        in_specs=[vmem()] * len(parts),
        out_specs=vmem(),
        compiler_params=params(8),
        name="add_up",
    )(*parts)


def run_combine(recv, ids, weights, res):
    return pl.pallas_call(
        combine,
        out_shape=jax.ShapeDtypeStruct(res.shape, bf16),
        in_specs=[vmem()] * 4,
        out_specs=vmem(),
        compiler_params=params(16),
        name="combine",
    )(recv, ids, weights, res)


def on_device(
    mixer_input, gate_in, step_size, decay_rate, state_in, state_out, skip, out_proj, hidden_in, norm_gain,
    w_gate, w_up, w_down, route_ids, route_weight,
):
    slab_len, prompts, channels = mixer_input.shape
    tokens = slab_len * prompts
    share = hidden_in.shape[2]
    chips = lax.axis_size("y")
    exp = ("x", "z")
    experts = lax.axis_size(exp) * w_gate.shape[0]
    slots = 4 * tokens // experts
    turns = slab_len // SUBS

    def swap(value):
        return lax.ppermute(value, "core", [(0, 1), (1, 0)])

    def ring(value, d):
        return lax.ppermute(value, "y", [(i, (i + d) % chips) for i in range(chips)])

    proj = lax.all_gather(out_proj, ("y", "core"))
    sig = mixer_input.reshape(tokens, channels)
    step = step_size.reshape(tokens, channels)
    into = scan_tables(state_in, turns)
    end, before, pre = run_first(step, sig, into, decay_rate, prompts)
    core = lax.axis_index("core").astype(jnp.int32).reshape(1)
    sib = swap(end)
    pair = run_pair(core, end, sib, decay_rate)
    pairs = [
        lax.ppermute(pair, "y", [(i, i + d) for i in range(chips - d)]) for d in range(chips - 1, 0, -1)
    ]
    gate = gate_in.reshape(tokens, channels)
    outof = scan_tables(state_out, turns)
    mixed = run_second(
        core, step, sig, gate, into, outof, decay_rate, skip.reshape(1, channels), before, pre, sib, pairs
    )
    partial_value = run_project(mixed, proj, share)
    recv = lax.all_to_all(partial_value, exp, 0, 0, tiled=True)
    ids = route_ids.reshape(tokens, -1)
    residual, slot_rows = run_dispatch(recv, hidden_in.reshape(tokens, share), ids.T, experts, slots)
    whole = lax.all_to_all(slot_rows, exp, 0, 0, tiled=True)
    own = run_normalize(whole, norm_gain.reshape(1, -1))

    half = slots // 2
    own_sib = swap(own)
    low = ring(own, 1)
    high = ring(own, -1)
    *weights, turn = run_load(own, w_gate[0], w_up[0], w_down[0])
    low, high, own_sib, turn = lax.optimization_barrier((low, high, own_sib, turn))
    far_low, far_high = ring(low[:half], 1), ring(high[half:], -1)
    low_sib, high_sib = swap(low), swap(high)
    mine0, other0, turn = run_ffn([([own], [own_sib])], weights, turn, share)
    from0 = swap(other0)
    low_sib, high_sib, turn = lax.optimization_barrier((low_sib, high_sib, turn))
    mine1, other1, mine3, other3, turn = run_ffn([([low], [low_sib]), ([high], [high_sib])], weights, turn, share)
    far_low, far_high, turn = lax.optimization_barrier((far_low, far_high, turn))
    mine2, other2, turn = run_ffn(
        [([far_low, far_high], [swap(far_low), swap(far_high)])], weights, turn, share
    )
    back1 = ring(run_add(mine1, swap(other1)), -1)
    back3 = ring(run_add(mine3, swap(other3)), 1)
    back2 = ring(run_add(mine2, swap(other2)), 2)
    returned = run_add(mine0, from0, back1, back3, back2)

    back = lax.all_to_all(returned, exp, 0, 0, tiled=True)
    out = run_combine(back, ids, route_weight.reshape(tokens, -1), residual)
    return out.reshape(slab_len, prompts, share)


def solution(mesh):
    ctx, exp = ("y", "core"), ("x", "z")
    n_ctx, n_exp = mesh.devices.shape
    side = int(round(n_exp**0.5))
    mesh = Mesh(mesh.devices.reshape(n_ctx // 2, 2, side, n_exp // side), ctx + exp)
    placed = (
        P(ctx, None, exp),
        P(ctx, None, exp),
        P(ctx, None, exp),
        P(None, exp),
        P(ctx, None, None),
        P(ctx, None, None),
        P(exp),
        P(exp, ctx),
        P(ctx, None, exp),
        P(),
        P(exp, None, ctx),
        P(exp, None, ctx),
        P(exp, ctx, None),
        P(ctx, None, None),
        P(ctx, None, None),
    )
    return jax.shard_map(on_device, mesh=mesh, in_specs=placed, out_specs=P(ctx, None, exp), check_vma=False)
```

```python
import functools

import jax
import jax.numpy as jnp
from jax import lax
from jax.experimental import pallas as pl
from jax.experimental.pallas import tpu as pltpu
from jax.sharding import Mesh
from jax.sharding import PartitionSpec as P

epsilon = 1e-06
LOG2E = 1.4426950408889634
SUBS = 8
LANES = 128
UNROLL = 16
MIB = 1 << 20
f32, bf16 = jnp.float32, jnp.bfloat16


def params(mib):
    return pltpu.CompilerParams(vmem_limit_bytes=mib * MIB)


def vmem():
    return pl.BlockSpec(memory_space=pltpu.VMEM)


def smem():
    return pl.BlockSpec(memory_space=pltpu.SMEM)


def anywhere():
    return pl.BlockSpec(memory_space=pl.ANY)


def spread(table_ref, out_ref):
    turns, _, columns = table_ref.shape

    def turn(t, _):
        row = table_ref[t]
        for i in range(columns):
            out_ref[t, i] = jnp.broadcast_to(row[:, i : i + 1], (SUBS, LANES))
        return 0

    lax.fori_loop(0, turns, turn, 0)


def split_lanes(step_ref, sig_ref, st4, v4):
    for q in range(st4.shape[0]):
        lanes = slice(q * LANES, (q + 1) * LANES)
        st = step_ref[:, lanes]
        st4[q] = st
        v4[q] = st * sig_ref[:, lanes].astype(f32)


def first_pass(step_ref, sig_ref, into_ref, rate_ref, fin_ref, before_ref, pre_ref, st4, v4, into_b):
    states, channels = rate_ref.shape
    prompts = fin_ref.shape[0]
    turns = into_ref.shape[0]
    hop = turns * prompts
    spread(into_ref, into_b)
    split_lanes(step_ref, sig_ref, st4, v4)
    sub = lax.broadcasted_iota(jnp.int32, (SUBS, LANES), 0)
    for q in range(channels // LANES):
        lanes = slice(q * LANES, (q + 1) * LANES)
        rates = [
            jnp.broadcast_to(rate_ref[n : n + 1, lanes] * -LOG2E, (SUBS, LANES)) for n in range(states)
        ]
        for b in range(prompts):

            def turn(t, held, q=q, b=b, rates=rates):
                total, hs = held
                st = st4[q, pl.ds(t * prompts + b, SUBS, stride=hop), :]
                v = v4[q, pl.ds(t * prompts + b, SUBS, stride=hop), :]
                new = []
                for n in range(states):
                    new.append(jnp.exp2(st * rates[n]) * hs[n] + v * into_b[t, b * states + n])
                return total + st, tuple(new)

            zero = jnp.zeros((SUBS, LANES), f32)
            width, hs = lax.fori_loop(0, turns, turn, (zero, (zero,) * states))
            hs = list(hs)
            for d in (1, 2, 4):
                live = sub >= d
                for n in range(states):
                    moved = jnp.where(live, pltpu.roll(hs[n], d, 0), 0.0)
                    hs[n] = hs[n] + jnp.exp2(rates[n] * width) * moved
                width = width + jnp.where(live, pltpu.roll(width, d, 0), 0.0)
            for n in range(states):
                fin_ref[b, n : n + 1, lanes] = hs[n][SUBS - 1 :]
                before_ref[b, n, :, lanes] = jnp.where(sub >= 1, pltpu.roll(hs[n], 1, 0), 0.0)
            fin_ref[b, states : states + 1, lanes] = width[SUBS - 1 :]
            pre_ref[b, :, lanes] = jnp.where(sub >= 1, pltpu.roll(width, 1, 0), 0.0)


def pair_up(core_ref, own_ref, sib_ref, rate_ref, out_ref):
    states = rate_ref.shape[0]
    low = core_ref[0] == 0
    rate = rate_ref[...] * -LOG2E
    for b in range(own_ref.shape[0]):
        first = jnp.where(low, own_ref[b], sib_ref[b])
        second = jnp.where(low, sib_ref[b], own_ref[b])
        decay = jnp.exp2(rate * second[states:])
        out_ref[b, :states] = decay * first[:states] + second[:states]
        out_ref[b, states:] = first[states:] + second[states:]


def second_pass(
    core_ref, step_ref, sig_ref, gate_ref, into_ref, outof_ref, rate_ref, skip_ref, before_ref, pre_ref,
    *rest, earlier,
):
    sib_ref, *pair_refs = rest[: earlier + 1]
    mixed_ref, st4, v4, y4, into_b, outof_b, enter = rest[earlier + 1 :]
    states, channels = rate_ref.shape
    prompts = pre_ref.shape[0]
    turns = into_ref.shape[0]
    hop = turns * prompts
    spread(into_ref, into_b)
    spread(outof_ref, outof_b)
    split_lanes(step_ref, sig_ref, st4, v4)
    live = jnp.where(core_ref[0] > 0, 1.0, 0.0).astype(f32)
    for q in range(channels // LANES):
        lanes = slice(q * LANES, (q + 1) * LANES)
        rate_q = rate_ref[:, lanes] * -LOG2E
        rates = [jnp.broadcast_to(rate_q[n : n + 1], (SUBS, LANES)) for n in range(states)]
        for b in range(prompts):
            h0 = jnp.zeros((states, LANES), f32)
            for pair in pair_refs:
                h0 = jnp.exp2(rate_q * pair[b, states : states + 1, lanes]) * h0 + pair[b, :states, lanes]
            decay = jnp.exp2(rate_q * (sib_ref[b, states : states + 1, lanes] * live))
            enter[...] = decay * h0 + sib_ref[b, :states, lanes] * live
            pre = pre_ref[b, :, lanes]
            hs = tuple(
                before_ref[b, n, :, lanes]
                + jnp.exp2(rates[n] * pre) * jnp.broadcast_to(enter[n : n + 1], (SUBS, LANES))
                for n in range(states)
            )

            def turn(t, hs, q=q, b=b, rates=rates):
                rows = pl.ds(t * prompts + b, SUBS, stride=hop)
                st = st4[q, rows, :]
                v = v4[q, rows, :]
                new, sums = [], [None] * 4
                for n in range(states):
                    h = jnp.exp2(st * rates[n]) * hs[n] + v * into_b[t, b * states + n]
                    new.append(h)
                    term = h * outof_b[t, b * states + n]
                    sums[n % 4] = term if sums[n % 4] is None else sums[n % 4] + term
                y4[q, rows, :] = (sums[0] + sums[1]) + (sums[2] + sums[3])
                return tuple(new)

            lax.fori_loop(0, turns, turn, hs, unroll=UNROLL)
        sig = sig_ref[:, lanes].astype(f32)
        gate = gate_ref[:, lanes].astype(f32)
        y = y4[q] + skip_ref[:, lanes] * sig
        mixed_ref[:, lanes] = (y * (gate / (1.0 + jnp.exp(-gate)))).astype(bf16)


def project(coords_ref, mixed_ref, ids_ref, proj_hbm, *rest, sides):
    nx, nz = sides
    z_refs, x_refs = rest[:nz], rest[nz : nz + nx]
    ids_out, turn_out, whole, proj, sem = rest[nz + nx :]
    _, half, width = z_refs[0].shape
    blocks, _, columns = proj.shape
    for c in range(blocks):
        pltpu.make_async_copy(proj_hbm.at[c], proj.at[c], sem.at[c]).start()
    for c in range(blocks):
        pltpu.make_async_copy(proj_hbm.at[c], proj.at[c], sem.at[c]).wait()
        part = jnp.dot(mixed_ref[...], proj[c], preferred_element_type=f32).astype(bf16)
        for i in range(columns // width):
            whole[c * (columns // width) + i] = part[:, i * width : (i + 1) * width]
    x, z = coords_ref[1], coords_ref[2]
    for d, out in enumerate(z_refs):
        for i in range(nx):
            out[i] = whole[i * nz + lax.rem(z + d, nz), :half]
    for d, out in enumerate(x_refs):
        for i in range(nz):
            out[i] = whole[lax.rem(x + d, nx) * nz + i, half:]
    ids_out[...] = ids_ref[...]
    turn_out[...] = jnp.zeros_like(turn_out)


def fold(coords_ref, *rest, sides):
    nx, nz = sides
    z_refs, x_refs = rest[:nz], rest[nz : nz + nx]
    first_refs, last_refs = rest[nz + nx : nz + 2 * nx], rest[nz + 2 * nx :]
    x, z = coords_ref[1], coords_ref[2]
    for parts, outs, at, count in ((z_refs, first_refs, x, nx), (x_refs, last_refs, z, nz)):
        for d, out in enumerate(outs):
            block = lax.rem(at + d, count)
            total = parts[0][block].astype(f32)
            for p in parts[1:]:
                total = total + p[block].astype(f32)
            out[...] = total.astype(bf16)


def dispatch(*refs, sides):
    *recvs, hidden_ref, ids_ref, res_ref, slots_ref, pick = refs
    experts, slots, width = slots_ref.shape
    tokens = hidden_ref.shape[0]
    half = tokens // 2
    for rows, parts in ((slice(0, half), recvs[: sides[0]]), (slice(half, tokens), recvs[sides[0] :])):
        part = hidden_ref[rows].astype(f32)
        for p in parts:
            part = part + p[...].astype(f32)
        res_ref[rows] = part
    total = res_ref[...]
    expert = lax.broadcasted_iota(jnp.int32, (experts, tokens), 0)
    chosen = jnp.zeros((experts, tokens), f32)
    for k in range(ids_ref.shape[0]):
        chosen = jnp.where(ids_ref[k : k + 1, :] == expert, 1.0, chosen)
    row = lax.broadcasted_iota(jnp.int32, (tokens, tokens), 0)
    col = lax.broadcasted_iota(jnp.int32, (tokens, tokens), 1)
    earlier = jnp.where(row < col, 1.0, 0.0).astype(bf16)
    place = jnp.dot(chosen.astype(bf16), earlier, preferred_element_type=f32)
    place = jnp.where(chosen > 0.5, place, -1.0)
    slot = lax.broadcasted_iota(jnp.int32, (slots, tokens), 0).astype(f32)
    for e in range(experts):
        pick[e * slots : (e + 1) * slots] = jnp.where(place[e : e + 1] == slot, 1.0, 0.0).astype(bf16)
    rows = jnp.dot(pick[...], total.astype(bf16), preferred_element_type=f32).astype(bf16)
    slots_ref[...] = rows.reshape(experts, slots, width)


def normalize(recv_ref, gain_ref, out_ref):
    blocks, slots, width = recv_ref.shape
    square = jnp.zeros((slots, width), f32)
    for i in range(blocks):
        part = recv_ref[i].astype(f32)
        square = square + part * part
    mean = jnp.sum(square, axis=1, keepdims=True) / (blocks * width)
    scale = lax.rsqrt(mean + epsilon)
    for i in range(blocks):
        lanes = slice(i * width, (i + 1) * width)
        out_ref[:, lanes] = (recv_ref[i].astype(f32) * scale * gain_ref[:, lanes]).astype(bf16)


def load_weights(after_ref, *refs):
    count = (len(refs) - 2) // 2
    sources, targets, turn_out, sem = refs[:count], refs[count : 2 * count], refs[-2], refs[-1]
    copies = [pltpu.make_async_copy(s, t, sem.at[i]) for i, (s, t) in enumerate(zip(sources, targets))]
    for c in copies:
        c.start()
    turn_out[...] = after_ref[...]
    for c in copies:
        c.wait()


def feed_forward(*refs, groups):
    count = sum(sum(g) for g in groups)
    pieces, (w_gate, w_up, w_down, turn_ref) = refs[:count], refs[count : count + 4]
    *outs, turn_out, x, act = refs[count + 4 :]
    at = 0
    for p in pieces:
        x[at : at + p.shape[0]] = p[...]
        at += p.shape[0]
    blocks, rows, width = outs[0].shape
    wide = 2 * LANES
    hidden = w_gate.shape[1]
    for i in range(0, hidden, wide):
        size = min(wide, hidden - i)
        lanes = slice(i, i + size)
        both = jnp.concatenate([w_gate[:, lanes], w_up[:, lanes]], axis=1)
        part = jnp.dot(x[...], both, preferred_element_type=f32)
        g, u = part[:, :size], part[:, size:]
        act[:, lanes] = (g / (1.0 + jnp.exp(-g)) * u).astype(bf16)
    for i in range(blocks):
        part = jnp.dot(act[...], w_down[:, i * width : (i + 1) * width], preferred_element_type=f32)
        part = part.astype(bf16)
        for j, out in enumerate(outs):
            out[i] = part[j * rows : (j + 1) * rows]
    turn_out[...] = turn_ref[...]


def add_up(*refs):
    *parts, out_ref = refs
    for i in range(out_ref.shape[0]):
        total = parts[0][i].astype(f32)
        for p in parts[1:]:
            total = total + p[i].astype(f32)
        out_ref[i] = total.astype(bf16)


def combine(recv_ref, ids_ref, weight_ref, res_ref, out_ref):
    experts, slots, width = recv_ref.shape
    tokens, top = ids_ref.shape
    rows = recv_ref[...].reshape(experts * slots, width)
    expert = lax.broadcasted_iota(jnp.int32, (tokens, experts), 1)
    named = [ids_ref[:, k : k + 1] == expert for k in range(top)]
    chosen = jnp.zeros((tokens, experts), f32)
    for k in range(top):
        chosen = jnp.where(named[k], 1.0, chosen)
    row = lax.broadcasted_iota(jnp.int32, (tokens, tokens), 0)
    col = lax.broadcasted_iota(jnp.int32, (tokens, tokens), 1)
    earlier = jnp.where(col < row, 1.0, 0.0).astype(bf16)
    place = jnp.dot(earlier, chosen.astype(bf16), preferred_element_type=f32)
    place = place + (expert * slots).astype(f32)
    slot = lax.broadcasted_iota(jnp.int32, (tokens, experts * slots), 1)
    total = res_ref[...]
    for k in range(top):
        at = jnp.sum(jnp.where(named[k], place, 0.0), axis=1, keepdims=True).astype(jnp.int32)
        pick = jnp.where(slot == at, 1.0, 0.0).astype(bf16)
        total = total + weight_ref[:, k : k + 1] * jnp.dot(pick, rows, preferred_element_type=f32)
    out_ref[...] = total.astype(out_ref.dtype)


def scan_tables(table, turns):
    return table.reshape(SUBS, turns, -1).transpose(1, 0, 2)


def run_first(step, sig, into, rate, prompts):
    tokens, channels = step.shape
    states = rate.shape[0]
    turns = into.shape[0]
    tiles = channels // LANES
    return pl.pallas_call(
        first_pass,
        out_shape=(
            jax.ShapeDtypeStruct((prompts, states + 1, channels), f32),
            jax.ShapeDtypeStruct((prompts, states, SUBS, channels), f32),
            jax.ShapeDtypeStruct((prompts, SUBS, channels), f32),
        ),
        in_specs=[vmem()] * 4,
        out_specs=(vmem(),) * 3,
        scratch_shapes=[
            pltpu.VMEM((tiles, tokens, LANES), f32),
            pltpu.VMEM((tiles, tokens, LANES), f32),
            pltpu.VMEM((turns, prompts * states, SUBS, LANES), f32),
        ],
        compiler_params=params(24),
        name="scan_first",
    )(step, sig, into, rate)


def run_pair(core, own, sib, rate):
    return pl.pallas_call(
        pair_up,
        out_shape=jax.ShapeDtypeStruct(own.shape, f32),
        in_specs=[smem()] + [vmem()] * 3,
        out_specs=vmem(),
        compiler_params=params(8),
        name="pair_up",
    )(core, own, sib, rate)


def run_second(core, step, sig, gate, into, outof, rate, skip, before, pre, sib, pairs):
    tokens, channels = step.shape
    prompts, states = before.shape[:2]
    turns = into.shape[0]
    tiles = channels // LANES
    return pl.pallas_call(
        functools.partial(second_pass, earlier=len(pairs)),
        out_shape=jax.ShapeDtypeStruct((tokens, channels), bf16),
        in_specs=[smem()] + [vmem()] * (10 + len(pairs)),
        out_specs=vmem(),
        scratch_shapes=[
            pltpu.VMEM((tiles, tokens, LANES), f32),
            pltpu.VMEM((tiles, tokens, LANES), f32),
            pltpu.VMEM((tiles, tokens, LANES), f32),
            pltpu.VMEM((turns, prompts * states, SUBS, LANES), f32),
            pltpu.VMEM((turns, prompts * states, SUBS, LANES), f32),
            pltpu.VMEM((states, LANES), f32),
        ],
        compiler_params=params(16),
        cost_estimate=pl.CostEstimate(flops=2 * 10**9, bytes_accessed=2 * MIB, transcendentals=0),
        name="scan_second",
    )(core, step, sig, gate, into, outof, rate, skip, before, pre, sib, *pairs)


def run_project(coords, mixed, ids, proj, share, sides):
    tokens = mixed.shape[0]
    nx, nz = sides
    blocks = proj.shape[0] * proj.shape[2] // share
    return pl.pallas_call(
        functools.partial(project, sides=sides),
        out_shape=[jax.ShapeDtypeStruct((nx, tokens // 2, share), bf16)] * nz
        + [jax.ShapeDtypeStruct((nz, tokens // 2, share), bf16)] * nx
        + [jax.ShapeDtypeStruct(ids.shape, ids.dtype), jax.ShapeDtypeStruct((8, LANES), f32)],
        in_specs=[smem(), vmem(), vmem(), anywhere()],
        out_specs=[vmem()] * (nx + nz + 2),
        scratch_shapes=[
            pltpu.VMEM((blocks, tokens, share), bf16),
            pltpu.VMEM(proj.shape, bf16),
            pltpu.SemaphoreType.DMA((proj.shape[0],)),
        ],
        compiler_params=params(16),
        name="project",
    )(coords, mixed, ids, pltpu.with_memory_space_constraint(proj, pltpu.HBM))


def run_fold(coords, parts, sides):
    nx, nz = sides
    _, half, share = parts[0].shape
    return pl.pallas_call(
        functools.partial(fold, sides=sides),
        out_shape=[jax.ShapeDtypeStruct((half, share), bf16)] * (nx + nz),
        in_specs=[smem()] + [vmem()] * (nx + nz),
        out_specs=[vmem()] * (nx + nz),
        compiler_params=params(8),
        name="fold",
    )(coords, *parts)


def run_dispatch(recvs, hidden, ids, experts, slots, sides):
    tokens, share = hidden.shape
    return pl.pallas_call(
        functools.partial(dispatch, sides=sides),
        out_shape=(
            jax.ShapeDtypeStruct((tokens, share), f32),
            jax.ShapeDtypeStruct((experts, slots, share), bf16),
        ),
        in_specs=[vmem()] * (len(recvs) + 2),
        out_specs=(vmem(),) * 2,
        scratch_shapes=[pltpu.VMEM((experts * slots, tokens), bf16)],
        compiler_params=params(8),
        name="dispatch",
    )(*recvs, hidden, ids)


def run_normalize(recv, gain):
    blocks, slots, width = recv.shape
    return pl.pallas_call(
        normalize,
        out_shape=jax.ShapeDtypeStruct((slots, blocks * width), bf16),
        in_specs=[vmem()] * 2,
        out_specs=vmem(),
        compiler_params=params(8),
        name="normalize",
    )(recv, gain)


def run_load(after, *weights):
    return pl.pallas_call(
        load_weights,
        out_shape=[pltpu.VMEM(w.shape, w.dtype) for w in weights] + [jax.ShapeDtypeStruct((8, LANES), f32)],
        in_specs=[vmem()] + [pl.BlockSpec(memory_space=pltpu.HBM)] * len(weights),
        out_specs=[vmem()] * (len(weights) + 1),
        scratch_shapes=[pltpu.SemaphoreType.DMA((len(weights),))],
        compiler_params=params(8),
        cost_estimate=pl.CostEstimate(flops=0, bytes_accessed=2 * sum(w.nbytes for w in weights), transcendentals=0),
        name="load_weights",
    )(after, *[pltpu.with_memory_space_constraint(w, pltpu.HBM) for w in weights])


def run_ffn(groups, weights, turn, share):
    pieces = [p for own, other in groups for p in (*own, *other)]
    rows = sum(p.shape[0] for p in groups[0][0])
    depth, hidden = weights[0].shape
    total = 2 * rows * len(groups)
    part = jax.ShapeDtypeStruct((depth // share, rows, share), bf16)
    weights = [pltpu.with_memory_space_constraint(w, pltpu.VMEM) for w in weights]
    return pl.pallas_call(
        functools.partial(feed_forward, groups=tuple((len(own), len(other)) for own, other in groups)),
        out_shape=(part,) * (2 * len(groups)) + (jax.ShapeDtypeStruct(turn.shape, turn.dtype),),
        in_specs=[vmem()] * (len(pieces) + 4),
        out_specs=(vmem(),) * (2 * len(groups) + 1),
        scratch_shapes=[pltpu.VMEM((total, depth), bf16), pltpu.VMEM((total, hidden), bf16)],
        compiler_params=params(12),
        cost_estimate=pl.CostEstimate(
            flops=6 * total * depth * hidden, bytes_accessed=4 * total * depth, transcendentals=0
        ),
        name="feed_forward",
    )(*pieces, *weights, turn)


def run_add(*parts):
    return pl.pallas_call(
        add_up,
        out_shape=jax.ShapeDtypeStruct(parts[0].shape, bf16),
        in_specs=[vmem()] * len(parts),
        out_specs=vmem(),
        compiler_params=params(8),
        name="add_up",
    )(*parts)


def run_combine(recv, ids, weights, res):
    return pl.pallas_call(
        combine,
        out_shape=jax.ShapeDtypeStruct(res.shape, bf16),
        in_specs=[vmem()] * 4,
        out_specs=vmem(),
        compiler_params=params(16),
        name="combine",
    )(recv, ids, weights, res)


def on_device(
    mixer_input, gate_in, step_size, decay_rate, state_in, state_out, skip, out_proj, hidden_in, norm_gain,
    w_gate, w_up, w_down, route_ids, route_weight,
):
    slab_len, prompts, channels = mixer_input.shape
    tokens = slab_len * prompts
    share = hidden_in.shape[2]
    chips = lax.axis_size("y")
    exp = ("x", "z")
    experts = lax.axis_size(exp) * w_gate.shape[0]
    slots = 4 * tokens // experts
    turns = slab_len // SUBS

    def swap(value):
        return lax.ppermute(value, "core", [(0, 1), (1, 0)])

    def ring(value, d):
        return lax.ppermute(value, "y", [(i, (i + d) % chips) for i in range(chips)])

    proj = lax.all_gather(out_proj, ("y", "core"))
    sig = mixer_input.reshape(tokens, channels)
    step = step_size.reshape(tokens, channels)
    into = scan_tables(state_in, turns)
    end, before, pre = run_first(step, sig, into, decay_rate, prompts)
    core = lax.axis_index("core").astype(jnp.int32).reshape(1)
    sib = swap(end)
    pair = run_pair(core, end, sib, decay_rate)
    pairs = [
        lax.ppermute(pair, "y", [(i, i + d) for i in range(chips - d)]) for d in range(chips - 1, 0, -1)
    ]
    gate = gate_in.reshape(tokens, channels)
    outof = scan_tables(state_out, turns)
    mixed = run_second(
        core, step, sig, gate, into, outof, decay_rate, skip.reshape(1, channels), before, pre, sib, pairs
    )
    sides = (lax.axis_size("x"), lax.axis_size("z"))
    coords = jnp.stack([lax.axis_index(a).astype(jnp.int32) for a in ("core", "x", "z")])

    def shift(value, axis, d):
        n = lax.axis_size(axis)
        return lax.ppermute(value, axis, [(i, (i + d) % n) for i in range(n)]) if d else value

    nx, nz = sides
    ids = route_ids.reshape(tokens, -1)
    *parts, by_choice, turn = run_project(coords, mixed, ids.T, proj, share, sides)
    hidden = hidden_in.reshape(tokens, share)
    hidden, ids, turn = lax.optimization_barrier((hidden, ids, turn))
    *weights, turn = run_load(turn, w_gate[0], w_up[0], w_down[0])
    parts = [shift(p, "z", d) for d, p in enumerate(parts[:nz])] + [shift(p, "x", d) for d, p in enumerate(parts[nz:])]
    *parts, turn = lax.optimization_barrier((*parts, turn))
    parts = run_fold(coords, parts, sides)
    parts = [shift(p, "x", d) for d, p in enumerate(parts[:nx])] + [shift(p, "z", d) for d, p in enumerate(parts[nx:])]
    residual, slot_rows = run_dispatch(parts, hidden, by_choice, experts, slots, sides)
    whole = lax.all_to_all(slot_rows, exp, 0, 0, tiled=True)
    own = run_normalize(whole, norm_gain.reshape(1, -1))

    half = slots // 2
    own_sib = swap(own)
    low = ring(own, 1)
    high = ring(own, -1)
    mine0, other0, turn = run_ffn([([own], [own_sib])], weights, turn, share)
    low, high, turn = lax.optimization_barrier((low, high, turn))
    from0 = swap(other0)
    far_low, far_high = ring(low[:half], 1), ring(high[half:], -1)
    low_sib, high_sib = swap(low), swap(high)
    mine1, other1, mine3, other3, turn = run_ffn([([low], [low_sib]), ([high], [high_sib])], weights, turn, share)
    far_low, far_high, turn, other1, other3 = lax.optimization_barrier((far_low, far_high, turn, other1, other3))
    mine2, other2, turn = run_ffn(
        [([far_low, far_high], [swap(far_low), swap(far_high)])], weights, turn, share
    )
    back1 = ring(run_add(mine1, swap(other1)), -1)
    back3 = ring(run_add(mine3, swap(other3)), 1)
    back2 = ring(run_add(mine2, swap(other2)), 2)
    returned = run_add(mine0, from0, back1, back3, back2)

    back = lax.all_to_all(returned, exp, 0, 0, tiled=True)
    out = run_combine(back, ids, route_weight.reshape(tokens, -1), residual)
    return out.reshape(slab_len, prompts, share)


def solution(mesh):
    ctx, exp = ("y", "core"), ("x", "z")
    n_ctx, n_exp = mesh.devices.shape
    side = int(round(n_exp**0.5))
    mesh = Mesh(mesh.devices.reshape(n_ctx // 2, 2, side, n_exp // side), ctx + exp)
    placed = (
        P(ctx, None, exp),
        P(ctx, None, exp),
        P(ctx, None, exp),
        P(None, exp),
        P(ctx, None, None),
        P(ctx, None, None),
        P(exp),
        P(exp, ctx),
        P(ctx, None, exp),
        P(),
        P(exp, None, ctx),
        P(exp, None, ctx),
        P(exp, ctx, None),
        P(ctx, None, None),
        P(ctx, None, None),
    )
    return jax.shard_map(on_device, mesh=mesh, in_specs=placed, out_specs=P(ctx, None, exp), check_vma=False)
```

```python
import functools

import jax
import jax.numpy as jnp
from jax import lax
from jax.experimental import pallas as pl
from jax.experimental.pallas import tpu as pltpu
from jax.sharding import Mesh
from jax.sharding import PartitionSpec as P

epsilon = 1e-06
LOG2E = 1.4426950408889634
SUBS = 8
LANES = 128
CUT = 1
UNROLL = 16
MIB = 1 << 20
f32, bf16 = jnp.float32, jnp.bfloat16


def params(mib):
    return pltpu.CompilerParams(vmem_limit_bytes=mib * MIB)


def vmem():
    return pl.BlockSpec(memory_space=pltpu.VMEM)


def smem():
    return pl.BlockSpec(memory_space=pltpu.SMEM)


def anywhere():
    return pl.BlockSpec(memory_space=pl.ANY)


def spread(table_ref, out_ref):
    turns, _, columns = table_ref.shape

    def turn(t, _):
        row = table_ref[t]
        for i in range(columns):
            out_ref[t, i] = jnp.broadcast_to(row[:, i : i + 1], (SUBS, LANES))
        return 0

    lax.fori_loop(0, turns, turn, 0)


def split_lanes(step_ref, sig_ref, st4, v4):
    for q in range(st4.shape[0]):
        lanes = slice(q * LANES, (q + 1) * LANES)
        st = step_ref[:, lanes]
        st4[q] = st
        v4[q] = st * sig_ref[:, lanes].astype(f32)


def first_pass(step_ref, sig_ref, into_ref, rate_ref, fin_ref, before_ref, pre_ref, st4, v4, into_b):
    states, channels = rate_ref.shape
    prompts = fin_ref.shape[0]
    turns = into_ref.shape[0]
    hop = turns * prompts
    spread(into_ref, into_b)
    split_lanes(step_ref, sig_ref, st4, v4)
    sub = lax.broadcasted_iota(jnp.int32, (SUBS, LANES), 0)
    for q in range(channels // LANES):
        lanes = slice(q * LANES, (q + 1) * LANES)
        rates = [
            jnp.broadcast_to(rate_ref[n : n + 1, lanes] * -LOG2E, (SUBS, LANES)) for n in range(states)
        ]
        for b in range(prompts):

            def turn(t, held, q=q, b=b, rates=rates):
                total, hs = held
                st = st4[q, pl.ds(t * prompts + b, SUBS, stride=hop), :]
                v = v4[q, pl.ds(t * prompts + b, SUBS, stride=hop), :]
                new = []
                for n in range(states):
                    new.append(jnp.exp2(st * rates[n]) * hs[n] + v * into_b[t, b * states + n])
                return total + st, tuple(new)

            zero = jnp.zeros((SUBS, LANES), f32)
            width, hs = lax.fori_loop(0, turns, turn, (zero, (zero,) * states))
            hs = list(hs)
            for d in (1, 2, 4):
                live = sub >= d
                for n in range(states):
                    moved = jnp.where(live, pltpu.roll(hs[n], d, 0), 0.0)
                    hs[n] = hs[n] + jnp.exp2(rates[n] * width) * moved
                width = width + jnp.where(live, pltpu.roll(width, d, 0), 0.0)
            for n in range(states):
                fin_ref[b, n : n + 1, lanes] = hs[n][SUBS - 1 :]
                before_ref[b, n, :, lanes] = jnp.where(sub >= 1, pltpu.roll(hs[n], 1, 0), 0.0)
            fin_ref[b, states : states + 1, lanes] = width[SUBS - 1 :]
            pre_ref[b, :, lanes] = jnp.where(sub >= 1, pltpu.roll(width, 1, 0), 0.0)


def second_pass(
    coords_ref, step_ref, sig_ref, gate_ref, into_ref, outof_ref, rate_ref, skip_ref, before_ref, pre_ref,
    ends_ref, mixed_ref, st4, v4, y4, into_b, outof_b, enter,
):
    states, channels = rate_ref.shape
    prompts = pre_ref.shape[0]
    turns = into_ref.shape[0]
    hop = turns * prompts
    spread(into_ref, into_b)
    spread(outof_ref, outof_b)
    split_lanes(step_ref, sig_ref, st4, v4)
    mine = coords_ref[0]
    for q in range(channels // LANES):
        lanes = slice(q * LANES, (q + 1) * LANES)
        rate_q = rate_ref[:, lanes] * -LOG2E
        rates = [jnp.broadcast_to(rate_q[n : n + 1], (SUBS, LANES)) for n in range(states)]
        for b in range(prompts):
            h0 = jnp.zeros((states, LANES), f32)
            for c in range(ends_ref.shape[0] - 1):
                live = jnp.where(c < mine, 1.0, 0.0).astype(f32)
                decay = jnp.exp2(rate_q * (ends_ref[c, b, states : states + 1, lanes] * live))
                h0 = decay * h0 + ends_ref[c, b, :states, lanes] * live
            enter[...] = h0
            pre = pre_ref[b, :, lanes]
            hs = tuple(
                before_ref[b, n, :, lanes]
                + jnp.exp2(rates[n] * pre) * jnp.broadcast_to(enter[n : n + 1], (SUBS, LANES))
                for n in range(states)
            )

            def turn(t, hs, q=q, b=b, rates=rates):
                rows = pl.ds(t * prompts + b, SUBS, stride=hop)
                st = st4[q, rows, :]
                v = v4[q, rows, :]
                new, sums = [], [None] * 4
                for n in range(states):
                    h = jnp.exp2(st * rates[n]) * hs[n] + v * into_b[t, b * states + n]
                    new.append(h)
                    term = h * outof_b[t, b * states + n]
                    sums[n % 4] = term if sums[n % 4] is None else sums[n % 4] + term
                y4[q, rows, :] = (sums[0] + sums[1]) + (sums[2] + sums[3])
                return tuple(new)

            lax.fori_loop(0, turns, turn, hs, unroll=UNROLL)
        sig = sig_ref[:, lanes].astype(f32)
        gate = gate_ref[:, lanes].astype(f32)
        y = y4[q] + skip_ref[:, lanes] * sig
        mixed_ref[:, lanes] = (y * (gate / (1.0 + jnp.exp(-gate)))).astype(bf16)


def project(coords_ref, mixed_ref, ids_ref, *refs, sides, halves):
    nx, nz = sides
    sources, rest = refs[:halves], refs[halves:]
    z_refs, x_refs = rest[:nz], rest[nz : nz + nx]
    ids_out, proj, sem = rest[nz + nx :]
    _, half, width = z_refs[0].shape
    _, depth, _ = proj.shape
    per = sources[0].shape[2] // width
    piece = depth // halves
    x, z = coords_ref[1], coords_ref[2]
    hops = [(dx, dz) for dx in range(nx) for dz in range(nz)]
    copies = []
    for r, (dx, dz) in enumerate(hops):
        to_x, to_z = lax.rem(x + dx, nx), lax.rem(z + dz, nz)
        block = to_x * nz + to_z
        columns = pl.ds(pl.multiple_of(lax.rem(block, per) * width, width), width)
        copies.append(
            [
                pltpu.make_async_copy(
                    source.at[block // per, :, columns], proj.at[r, i * piece : (i + 1) * piece], sem.at[r, i]
                )
                for i, source in enumerate(sources)
            ]
        )
        for c in copies[-1]:
            c.start()
    ids_out[...] = ids_ref[...]
    for r, (dx, dz) in enumerate(hops):
        for c in copies[r]:
            c.wait()
        part = jnp.dot(mixed_ref[...], proj[r], preferred_element_type=f32).astype(bf16)
        z_refs[dz][lax.rem(x + dx, nx)] = part[:half]
        x_refs[dx][lax.rem(z + dz, nz)] = part[half:]


def fold(coords_ref, *rest, sides):
    nx, nz = sides
    z_refs, x_refs = rest[:nz], rest[nz : nz + nx]
    first_refs, last_refs = rest[nz + nx : nz + 2 * nx], rest[nz + 2 * nx :]
    x, z = coords_ref[1], coords_ref[2]
    for parts, outs, at, count in ((z_refs, first_refs, x, nx), (x_refs, last_refs, z, nz)):
        for d, out in enumerate(outs):
            block = lax.rem(at + d, count)
            total = parts[0][block].astype(f32)
            for p in parts[1:]:
                total = total + p[block].astype(f32)
            out[...] = total.astype(bf16)


def dispatch(*refs, sides):
    *recvs, hidden_ref, ids_ref, res_ref, slots_ref, pick = refs
    experts, slots, width = slots_ref.shape
    tokens = hidden_ref.shape[0]
    half = tokens // 2
    for rows, parts in ((slice(0, half), recvs[: sides[0]]), (slice(half, tokens), recvs[sides[0] :])):
        part = hidden_ref[rows].astype(f32)
        for p in parts:
            part = part + p[...].astype(f32)
        res_ref[rows] = part
    total = res_ref[...]
    expert = lax.broadcasted_iota(jnp.int32, (experts, tokens), 0)
    chosen = jnp.zeros((experts, tokens), f32)
    for k in range(ids_ref.shape[0]):
        chosen = jnp.where(ids_ref[k : k + 1, :] == expert, 1.0, chosen)
    row = lax.broadcasted_iota(jnp.int32, (tokens, tokens), 0)
    col = lax.broadcasted_iota(jnp.int32, (tokens, tokens), 1)
    earlier = jnp.where(row < col, 1.0, 0.0).astype(bf16)
    place = jnp.dot(chosen.astype(bf16), earlier, preferred_element_type=f32)
    place = jnp.where(chosen > 0.5, place, -1.0)
    slot = lax.broadcasted_iota(jnp.int32, (slots, tokens), 0).astype(f32)
    for e in range(experts):
        pick[e * slots : (e + 1) * slots] = jnp.where(place[e : e + 1] == slot, 1.0, 0.0).astype(bf16)
    rows = jnp.dot(pick[...], total.astype(bf16), preferred_element_type=f32).astype(bf16)
    slots_ref[...] = rows.reshape(experts, slots, width)


def normalize(recv_ref, gain_ref, out_ref):
    blocks, slots, width = recv_ref.shape
    square = jnp.zeros((slots, width), f32)
    for i in range(blocks):
        part = recv_ref[i].astype(f32)
        square = square + part * part
    mean = jnp.sum(square, axis=1, keepdims=True) / (blocks * width)
    scale = lax.rsqrt(mean + epsilon)
    for i in range(blocks):
        lanes = slice(i * width, (i + 1) * width)
        out_ref[:, lanes] = (recv_ref[i].astype(f32) * scale * gain_ref[:, lanes]).astype(bf16)


def load_weights(after_ref, *refs):
    count = (len(refs) - 2) // 2
    sources, targets, turn_out, sem = refs[:count], refs[count : 2 * count], refs[-2], refs[-1]
    copies = [pltpu.make_async_copy(s, t, sem.at[i]) for i, (s, t) in enumerate(zip(sources, targets))]
    for c in copies:
        c.start()
    turn_out[...] = after_ref[: turn_out.shape[0], : turn_out.shape[1]].astype(f32)
    for c in copies:
        c.wait()


def feed_forward(*refs, groups, cut):
    count = sum(sum(g) for g in groups)
    pieces, (w_gate, w_up, w_down, turn_ref) = refs[:count], refs[count : count + 4]
    *outs, turn_out, x, act = refs[count + 4 :]
    at = 0
    for p in pieces:
        x[at : at + p.shape[0]] = p[...]
        at += p.shape[0]
    blocks, rows, width = outs[0].shape
    size_out = blocks // cut
    wide = 2 * LANES
    hidden = w_gate.shape[1]
    for i in range(0, hidden, wide):
        size = min(wide, hidden - i)
        lanes = slice(i, i + size)
        both = jnp.concatenate([w_gate[:, lanes], w_up[:, lanes]], axis=1)
        part = jnp.dot(x[...], both, preferred_element_type=f32)
        g, u = part[:, :size], part[:, size:]
        act[:, lanes] = (g / (1.0 + jnp.exp(-g)) * u).astype(bf16)
    for i in range(blocks):
        part = jnp.dot(act[...], w_down[:, i * width : (i + 1) * width], preferred_element_type=f32)
        part = part.astype(bf16)
        for j in range(len(groups)):
            own, *others = outs[j * (cut + 1) : (j + 1) * (cut + 1)]
            own[i] = part[2 * j * rows : (2 * j + 1) * rows]
            others[i // size_out][i % size_out] = part[(2 * j + 1) * rows : (2 * j + 2) * rows]
    turn_out[...] = turn_ref[...]


def add_up(*refs, pieces):
    *parts, out_ref = refs
    for i in range(out_ref.shape[0]):
        total, at = None, 0
        for n in pieces:
            size = out_ref.shape[0] // n
            term = parts[at + i // size][i % size].astype(f32)
            total = term if total is None else total + term
            at += n
        out_ref[i] = total.astype(out_ref.dtype)


def combine(recv_ref, ids_ref, weight_ref, res_ref, out_ref):
    experts, slots, width = recv_ref.shape
    tokens, top = ids_ref.shape
    rows = recv_ref[...].reshape(experts * slots, width)
    expert = lax.broadcasted_iota(jnp.int32, (tokens, experts), 1)
    named = [ids_ref[:, k : k + 1] == expert for k in range(top)]
    chosen = jnp.zeros((tokens, experts), f32)
    for k in range(top):
        chosen = jnp.where(named[k], 1.0, chosen)
    row = lax.broadcasted_iota(jnp.int32, (tokens, tokens), 0)
    col = lax.broadcasted_iota(jnp.int32, (tokens, tokens), 1)
    earlier = jnp.where(col < row, 1.0, 0.0).astype(bf16)
    place = jnp.dot(earlier, chosen.astype(bf16), preferred_element_type=f32)
    place = place + (expert * slots).astype(f32)
    slot = lax.broadcasted_iota(jnp.int32, (tokens, experts * slots), 1)
    total = res_ref[...]
    for k in range(top):
        at = jnp.sum(jnp.where(named[k], place, 0.0), axis=1, keepdims=True).astype(jnp.int32)
        pick = jnp.where(slot == at, 1.0, 0.0).astype(bf16)
        total = total + weight_ref[:, k : k + 1] * jnp.dot(pick, rows, preferred_element_type=f32)
    out_ref[...] = total.astype(out_ref.dtype)


def scan_tables(table, turns):
    return table.reshape(SUBS, turns, -1).transpose(1, 0, 2)


def run_first(step, sig, into, rate, prompts):
    tokens, channels = step.shape
    states = rate.shape[0]
    turns = into.shape[0]
    tiles = channels // LANES
    return pl.pallas_call(
        first_pass,
        out_shape=(
            jax.ShapeDtypeStruct((prompts, states + 1, channels), f32),
            jax.ShapeDtypeStruct((prompts, states, SUBS, channels), f32),
            jax.ShapeDtypeStruct((prompts, SUBS, channels), f32),
        ),
        in_specs=[vmem()] * 4,
        out_specs=(vmem(),) * 3,
        scratch_shapes=[
            pltpu.VMEM((tiles, tokens, LANES), f32),
            pltpu.VMEM((tiles, tokens, LANES), f32),
            pltpu.VMEM((turns, prompts * states, SUBS, LANES), f32),
        ],
        compiler_params=params(24),
        name="scan_first",
    )(step, sig, into, rate)


def run_second(coords, step, sig, gate, into, outof, rate, skip, before, pre, ends):
    tokens, channels = step.shape
    prompts, states = before.shape[:2]
    turns = into.shape[0]
    tiles = channels // LANES
    return pl.pallas_call(
        second_pass,
        out_shape=jax.ShapeDtypeStruct((tokens, channels), bf16),
        in_specs=[smem()] + [vmem()] * 10,
        out_specs=vmem(),
        scratch_shapes=[
            pltpu.VMEM((tiles, tokens, LANES), f32),
            pltpu.VMEM((tiles, tokens, LANES), f32),
            pltpu.VMEM((tiles, tokens, LANES), f32),
            pltpu.VMEM((turns, prompts * states, SUBS, LANES), f32),
            pltpu.VMEM((turns, prompts * states, SUBS, LANES), f32),
            pltpu.VMEM((states, LANES), f32),
        ],
        compiler_params=params(16),
        cost_estimate=pl.CostEstimate(flops=2 * 10**9, bytes_accessed=2 * MIB, transcendentals=0),
        name="scan_second",
    )(coords, step, sig, gate, into, outof, rate, skip, before, pre, ends)


def run_project(coords, mixed, ids, proj, share, sides):
    tokens, depth = mixed.shape
    nx, nz = sides
    return pl.pallas_call(
        functools.partial(project, sides=sides, halves=len(proj)),
        out_shape=[jax.ShapeDtypeStruct((nx, tokens // 2, share), bf16)] * nz
        + [jax.ShapeDtypeStruct((nz, tokens // 2, share), bf16)] * nx
        + [jax.ShapeDtypeStruct(ids.shape, ids.dtype)],
        in_specs=[smem(), vmem(), vmem()] + [anywhere()] * len(proj),
        out_specs=[vmem()] * (nx + nz + 1),
        scratch_shapes=[
            pltpu.VMEM((nx * nz, depth, share), bf16),
            pltpu.SemaphoreType.DMA((nx * nz, len(proj))),
        ],
        compiler_params=params(16),
        name="project",
    )(coords, mixed, ids, *[pltpu.with_memory_space_constraint(p, pltpu.HBM) for p in proj])


def run_fold(coords, parts, sides):
    nx, nz = sides
    _, half, share = parts[0].shape
    return pl.pallas_call(
        functools.partial(fold, sides=sides),
        out_shape=[jax.ShapeDtypeStruct((half, share), bf16)] * (nx + nz),
        in_specs=[smem()] + [vmem()] * (nx + nz),
        out_specs=[vmem()] * (nx + nz),
        compiler_params=params(8),
        name="fold",
    )(coords, *parts)


def run_dispatch(recvs, hidden, ids, experts, slots, sides):
    tokens, share = hidden.shape
    return pl.pallas_call(
        functools.partial(dispatch, sides=sides),
        out_shape=(
            jax.ShapeDtypeStruct((tokens, share), f32),
            jax.ShapeDtypeStruct((experts, slots, share), bf16),
        ),
        in_specs=[vmem()] * (len(recvs) + 2),
        out_specs=(vmem(),) * 2,
        scratch_shapes=[pltpu.VMEM((experts * slots, tokens), bf16)],
        compiler_params=params(8),
        name="dispatch",
    )(*recvs, hidden, ids)


def run_normalize(recv, gain):
    blocks, slots, width = recv.shape
    return pl.pallas_call(
        normalize,
        out_shape=jax.ShapeDtypeStruct((slots, blocks * width), bf16),
        in_specs=[vmem()] * 2,
        out_specs=vmem(),
        compiler_params=params(8),
        name="normalize",
    )(recv, gain)


def run_load(after, *weights):
    return pl.pallas_call(
        load_weights,
        out_shape=[pltpu.VMEM(w.shape, w.dtype) for w in weights] + [jax.ShapeDtypeStruct((8, LANES), f32)],
        in_specs=[vmem()] + [pl.BlockSpec(memory_space=pltpu.HBM)] * len(weights),
        out_specs=[vmem()] * (len(weights) + 1),
        scratch_shapes=[pltpu.SemaphoreType.DMA((len(weights),))],
        compiler_params=params(8),
        cost_estimate=pl.CostEstimate(flops=0, bytes_accessed=2 * sum(w.nbytes for w in weights), transcendentals=0),
        name="load_weights",
    )(after, *[pltpu.with_memory_space_constraint(w, pltpu.HBM) for w in weights])


def run_ffn(groups, weights, turn, share, cut=1):
    pieces = [p for own, other in groups for p in (*own, *other)]
    rows = sum(p.shape[0] for p in groups[0][0])
    depth, hidden = weights[0].shape
    total = 2 * rows * len(groups)
    part = jax.ShapeDtypeStruct((depth // share, rows, share), bf16)
    piece = jax.ShapeDtypeStruct((depth // share // cut, rows, share), bf16)
    weights = [pltpu.with_memory_space_constraint(w, pltpu.VMEM) for w in weights]
    return pl.pallas_call(
        functools.partial(feed_forward, groups=tuple((len(own), len(other)) for own, other in groups), cut=cut),
        out_shape=(part, *(piece,) * cut) * len(groups) + (jax.ShapeDtypeStruct(turn.shape, turn.dtype),),
        in_specs=[vmem()] * (len(pieces) + 4),
        out_specs=(vmem(),) * ((cut + 1) * len(groups) + 1),
        scratch_shapes=[pltpu.VMEM((total, depth), bf16), pltpu.VMEM((total, hidden), bf16)],
        compiler_params=params(12),
        cost_estimate=pl.CostEstimate(
            flops=6 * total * depth * hidden, bytes_accessed=4 * total * depth, transcendentals=0
        ),
        name="feed_forward",
    )(*pieces, *weights, turn)


def run_add(*parts, dtype=bf16, bytes_accessed=MIB):
    parts = [p if isinstance(p, list) else [p] for p in parts]
    flat = [piece for p in parts for piece in p]
    return pl.pallas_call(
        functools.partial(add_up, pieces=tuple(len(p) for p in parts)),
        out_shape=jax.ShapeDtypeStruct((sum(p.shape[0] for p in parts[0]), *flat[0].shape[1:]), dtype),
        in_specs=[vmem()] * len(flat),
        out_specs=vmem(),
        compiler_params=params(8),
        cost_estimate=pl.CostEstimate(flops=0, bytes_accessed=bytes_accessed, transcendentals=0),
        name="add_up",
    )(*flat)


def run_combine(recv, ids, weights, res):
    return pl.pallas_call(
        combine,
        out_shape=jax.ShapeDtypeStruct(res.shape, bf16),
        in_specs=[vmem()] * 4,
        out_specs=vmem(),
        compiler_params=params(16),
        name="combine",
    )(recv, ids, weights, res)


def on_device(
    mixer_input, gate_in, step_size, decay_rate, state_in, state_out, skip, out_proj, hidden_in, norm_gain,
    w_gate, w_up, w_down, route_ids, route_weight,
):
    slab_len, prompts, channels = mixer_input.shape
    tokens = slab_len * prompts
    share = hidden_in.shape[2]
    chips = lax.axis_size("y")
    ctx, exp = ("y", "core"), ("x", "z")
    experts = lax.axis_size(exp) * w_gate.shape[0]
    slots = 4 * tokens // experts
    turns = slab_len // SUBS

    def swap(value):
        return lax.ppermute(value, "core", [(0, 1), (1, 0)])

    def ring(value, d):
        return lax.ppermute(value, "y", [(i, (i + d) % chips) for i in range(chips)])

    proj = [lax.all_gather(p, ctx) for p in jnp.split(out_proj, 2, axis=0)]
    sig = mixer_input.reshape(tokens, channels)
    step = step_size.reshape(tokens, channels)
    into = scan_tables(state_in, turns)
    end, before, pre = run_first(step, sig, into, decay_rate, prompts)
    ends = lax.all_gather(end, ctx)
    coords = jnp.stack([lax.axis_index(a).astype(jnp.int32) for a in (ctx, "x", "z")])
    gate = gate_in.reshape(tokens, channels)
    outof = scan_tables(state_out, turns)
    mixed = run_second(
        coords, step, sig, gate, into, outof, decay_rate, skip.reshape(1, channels), before, pre, ends
    )
    sides = (lax.axis_size("x"), lax.axis_size("z"))

    def shift(value, axis, d):
        n = lax.axis_size(axis)
        return lax.ppermute(value, axis, [(i, (i + d) % n) for i in range(n)]) if d else value

    nx, nz = sides
    ids = route_ids.reshape(tokens, -1)
    *parts, by_choice = run_project(coords, mixed, ids.T, proj, share, sides)
    hidden = hidden_in.reshape(tokens, share)
    parts = [shift(p, "z", d) for d, p in enumerate(parts[:nz])] + [shift(p, "x", d) for d, p in enumerate(parts[nz:])]
    parts = run_fold(coords, parts, sides)
    parts = [shift(p, "x", d) for d, p in enumerate(parts[:nx])] + [shift(p, "z", d) for d, p in enumerate(parts[nx:])]
    residual, slot_rows = run_dispatch(parts, hidden, by_choice, experts, slots, sides)
    whole = lax.all_to_all(slot_rows, exp, 0, 0, tiled=True)
    own = run_normalize(whole, norm_gain.reshape(1, -1))

    half = slots // 2
    own_sib = swap(own)
    low = ring(own, 1)
    high = ring(own, -1)
    *weights, turn = run_load(own, w_gate[0], w_up[0], w_down[0])
    own_sib, turn = lax.optimization_barrier((own_sib, turn))
    mine0, other0, turn = run_ffn([([own], [own_sib])], weights, turn, share)
    low, high, turn = lax.optimization_barrier((low, high, turn))
    from0 = swap(other0)
    far_low, far_high = ring(low[:half], 1), ring(high[half:], -1)
    low_sib, high_sib = swap(low), swap(high)
    low_sib, from0 = lax.optimization_barrier((low_sib, from0))
    mine1, other1, mine3, other3, turn = run_ffn([([low], [low_sib]), ([high], [high_sib])], weights, turn, share)
    far_low, far_high, turn, other1, other3 = lax.optimization_barrier((far_low, far_high, turn, other1, other3))
    far_low_sib, far_high_sib = swap(far_low), swap(far_high)
    low_sum, high_sum = run_add(mine1, swap(other1)), run_add(mine3, swap(other3))
    low_sum, high_sum, turn = lax.optimization_barrier((low_sum, high_sum, turn))
    back1, back3 = ring(low_sum, -1), ring(high_sum, 1)
    mine2, *other2, turn = run_ffn(
        [([far_low, far_high], [far_low_sib, far_high_sib])], weights, turn, share, cut=CUT
    )
    back2 = ring(run_add(mine2, [swap(p) for p in other2]), 2)
    near = run_add(mine0, from0, back1, back3, dtype=f32, bytes_accessed=64 * MIB)
    returned = run_add(near, back2)

    back = lax.all_to_all(returned, exp, 0, 0, tiled=True)
    out = run_combine(back, ids, route_weight.reshape(tokens, -1), residual)
    return out.reshape(slab_len, prompts, share)


def solution(mesh):
    ctx, exp = ("y", "core"), ("x", "z")
    n_ctx, n_exp = mesh.devices.shape
    side = int(round(n_exp**0.5))
    mesh = Mesh(mesh.devices.reshape(n_ctx // 2, 2, side, n_exp // side), ctx + exp)
    placed = (
        P(ctx, None, exp),
        P(ctx, None, exp),
        P(ctx, None, exp),
        P(None, exp),
        P(ctx, None, None),
        P(ctx, None, None),
        P(exp),
        P(exp, ctx),
        P(ctx, None, exp),
        P(),
        P(exp, None, ctx),
        P(exp, None, ctx),
        P(exp, ctx, None),
        P(ctx, None, None),
        P(ctx, None, None),
    )
    return jax.shard_map(on_device, mesh=mesh, in_specs=placed, out_specs=P(ctx, None, exp), check_vma=False)
```

```python
import functools

import jax
import jax.numpy as jnp
from jax import lax
from jax.experimental import pallas as pl
from jax.experimental.pallas import tpu as pltpu
from jax.sharding import Mesh
from jax.sharding import PartitionSpec as P

epsilon = 1e-06
LOG2E = 1.4426950408889634
SUBS = 8
LANES = 128
CUT = 1
UNROLL = 16
MIB = 1 << 20
f32, bf16 = jnp.float32, jnp.bfloat16


def params(mib):
    return pltpu.CompilerParams(vmem_limit_bytes=mib * MIB)


def vmem():
    return pl.BlockSpec(memory_space=pltpu.VMEM)


def smem():
    return pl.BlockSpec(memory_space=pltpu.SMEM)


def anywhere():
    return pl.BlockSpec(memory_space=pl.ANY)


def spread(table_ref, out_ref):
    turns, _, columns = table_ref.shape

    def turn(t, _):
        row = table_ref[t]
        for i in range(columns):
            out_ref[t, i] = jnp.broadcast_to(row[:, i : i + 1], (SUBS, LANES))
        return 0

    lax.fori_loop(0, turns, turn, 0)


def split_lanes(step_ref, sig_ref, st4, v4):
    for q in range(st4.shape[0]):
        lanes = slice(q * LANES, (q + 1) * LANES)
        st = step_ref[:, lanes]
        st4[q] = st
        v4[q] = st * sig_ref[:, lanes].astype(f32)


def first_pass(step_ref, sig_ref, into_ref, rate_ref, fin_ref, before_ref, pre_ref, st4, v4, into_b):
    states, channels = rate_ref.shape
    prompts = fin_ref.shape[0]
    turns = into_ref.shape[0]
    hop = turns * prompts
    spread(into_ref, into_b)
    split_lanes(step_ref, sig_ref, st4, v4)
    sub = lax.broadcasted_iota(jnp.int32, (SUBS, LANES), 0)
    for q in range(channels // LANES):
        lanes = slice(q * LANES, (q + 1) * LANES)
        rates = [
            jnp.broadcast_to(rate_ref[n : n + 1, lanes] * -LOG2E, (SUBS, LANES)) for n in range(states)
        ]
        for b in range(prompts):

            def turn(t, held, q=q, b=b, rates=rates):
                total, hs = held
                st = st4[q, pl.ds(t * prompts + b, SUBS, stride=hop), :]
                v = v4[q, pl.ds(t * prompts + b, SUBS, stride=hop), :]
                new = []
                for n in range(states):
                    new.append(jnp.exp2(st * rates[n]) * hs[n] + v * into_b[t, b * states + n])
                return total + st, tuple(new)

            zero = jnp.zeros((SUBS, LANES), f32)
            width, hs = lax.fori_loop(0, turns, turn, (zero, (zero,) * states))
            hs = list(hs)
            for d in (1, 2, 4):
                live = sub >= d
                for n in range(states):
                    moved = jnp.where(live, pltpu.roll(hs[n], d, 0), 0.0)
                    hs[n] = hs[n] + jnp.exp2(rates[n] * width) * moved
                width = width + jnp.where(live, pltpu.roll(width, d, 0), 0.0)
            for n in range(states):
                fin_ref[b, n : n + 1, lanes] = hs[n][SUBS - 1 :]
                before_ref[b, n, :, lanes] = jnp.where(sub >= 1, pltpu.roll(hs[n], 1, 0), 0.0)
            fin_ref[b, states : states + 1, lanes] = width[SUBS - 1 :]
            pre_ref[b, :, lanes] = jnp.where(sub >= 1, pltpu.roll(width, 1, 0), 0.0)


def second_pass(
    coords_ref, step_ref, sig_ref, gate_ref, into_ref, outof_ref, rate_ref, skip_ref, before_ref, pre_ref,
    ends_ref, mixed_ref, st4, v4, y4, into_b, outof_b, enter,
):
    states, channels = rate_ref.shape
    prompts = pre_ref.shape[0]
    turns = into_ref.shape[0]
    hop = turns * prompts
    spread(into_ref, into_b)
    spread(outof_ref, outof_b)
    split_lanes(step_ref, sig_ref, st4, v4)
    mine = coords_ref[0]
    for q in range(channels // LANES):
        lanes = slice(q * LANES, (q + 1) * LANES)
        rate_q = rate_ref[:, lanes] * -LOG2E
        rates = [jnp.broadcast_to(rate_q[n : n + 1], (SUBS, LANES)) for n in range(states)]
        for b in range(prompts):
            h0 = jnp.zeros((states, LANES), f32)
            for c in range(ends_ref.shape[0] - 1):
                live = jnp.where(c < mine, 1.0, 0.0).astype(f32)
                decay = jnp.exp2(rate_q * (ends_ref[c, b, states : states + 1, lanes] * live))
                h0 = decay * h0 + ends_ref[c, b, :states, lanes] * live
            enter[...] = h0
            pre = pre_ref[b, :, lanes]
            hs = tuple(
                before_ref[b, n, :, lanes]
                + jnp.exp2(rates[n] * pre) * jnp.broadcast_to(enter[n : n + 1], (SUBS, LANES))
                for n in range(states)
            )

            def turn(t, hs, q=q, b=b, rates=rates):
                rows = pl.ds(t * prompts + b, SUBS, stride=hop)
                st = st4[q, rows, :]
                v = v4[q, rows, :]
                new, sums = [], [None] * 4
                for n in range(states):
                    h = jnp.exp2(st * rates[n]) * hs[n] + v * into_b[t, b * states + n]
                    new.append(h)
                    term = h * outof_b[t, b * states + n]
                    sums[n % 4] = term if sums[n % 4] is None else sums[n % 4] + term
                y4[q, rows, :] = (sums[0] + sums[1]) + (sums[2] + sums[3])
                return tuple(new)

            lax.fori_loop(0, turns, turn, hs, unroll=UNROLL)
        sig = sig_ref[:, lanes].astype(f32)
        gate = gate_ref[:, lanes].astype(f32)
        y = y4[q] + skip_ref[:, lanes] * sig
        mixed_ref[:, lanes] = (y * (gate / (1.0 + jnp.exp(-gate)))).astype(bf16)


def project(coords_ref, mixed_ref, ids_ref, proj_hbm, *rest, sides):
    nx, nz = sides
    z_refs, x_refs = rest[:nz], rest[nz : nz + nx]
    ids_out, whole, proj, sem = rest[nz + nx :]
    _, half, width = z_refs[0].shape
    blocks, _, columns = proj.shape
    for c in range(blocks):
        pltpu.make_async_copy(proj_hbm.at[c], proj.at[c], sem.at[c]).start()
    for c in range(blocks):
        pltpu.make_async_copy(proj_hbm.at[c], proj.at[c], sem.at[c]).wait()
        part = jnp.dot(mixed_ref[...], proj[c], preferred_element_type=f32).astype(bf16)
        for i in range(columns // width):
            whole[c * (columns // width) + i] = part[:, i * width : (i + 1) * width]
    x, z = coords_ref[1], coords_ref[2]
    for d, out in enumerate(z_refs):
        for i in range(nx):
            out[i] = whole[i * nz + lax.rem(z + d, nz), :half]
    for d, out in enumerate(x_refs):
        for i in range(nz):
            out[i] = whole[lax.rem(x + d, nx) * nz + i, half:]
    ids_out[...] = ids_ref[...]


def fold(coords_ref, *rest, sides):
    nx, nz = sides
    z_refs, x_refs = rest[:nz], rest[nz : nz + nx]
    first_refs, last_refs = rest[nz + nx : nz + 2 * nx], rest[nz + 2 * nx :]
    x, z = coords_ref[1], coords_ref[2]
    for parts, outs, at, count in ((z_refs, first_refs, x, nx), (x_refs, last_refs, z, nz)):
        for d, out in enumerate(outs):
            block = lax.rem(at + d, count)
            total = parts[0][block].astype(f32)
            for p in parts[1:]:
                total = total + p[block].astype(f32)
            out[...] = total.astype(bf16)


def dispatch(*refs, sides):
    *recvs, hidden_ref, ids_ref, res_ref, slots_ref, pick = refs
    experts, slots, width = slots_ref.shape
    tokens = hidden_ref.shape[0]
    half = tokens // 2
    for rows, parts in ((slice(0, half), recvs[: sides[0]]), (slice(half, tokens), recvs[sides[0] :])):
        part = hidden_ref[rows].astype(f32)
        for p in parts:
            part = part + p[...].astype(f32)
        res_ref[rows] = part
    total = res_ref[...]
    expert = lax.broadcasted_iota(jnp.int32, (experts, tokens), 0)
    chosen = jnp.zeros((experts, tokens), f32)
    for k in range(ids_ref.shape[0]):
        chosen = jnp.where(ids_ref[k : k + 1, :] == expert, 1.0, chosen)
    row = lax.broadcasted_iota(jnp.int32, (tokens, tokens), 0)
    col = lax.broadcasted_iota(jnp.int32, (tokens, tokens), 1)
    earlier = jnp.where(row < col, 1.0, 0.0).astype(bf16)
    place = jnp.dot(chosen.astype(bf16), earlier, preferred_element_type=f32)
    place = jnp.where(chosen > 0.5, place, -1.0)
    slot = lax.broadcasted_iota(jnp.int32, (slots, tokens), 0).astype(f32)
    for e in range(experts):
        pick[e * slots : (e + 1) * slots] = jnp.where(place[e : e + 1] == slot, 1.0, 0.0).astype(bf16)
    rows = jnp.dot(pick[...], total.astype(bf16), preferred_element_type=f32).astype(bf16)
    slots_ref[...] = rows.reshape(experts, slots, width)


def normalize(recv_ref, gain_ref, out_ref):
    blocks, slots, width = recv_ref.shape
    square = jnp.zeros((slots, width), f32)
    for i in range(blocks):
        part = recv_ref[i].astype(f32)
        square = square + part * part
    mean = jnp.sum(square, axis=1, keepdims=True) / (blocks * width)
    scale = lax.rsqrt(mean + epsilon)
    for i in range(blocks):
        lanes = slice(i * width, (i + 1) * width)
        out_ref[:, lanes] = (recv_ref[i].astype(f32) * scale * gain_ref[:, lanes]).astype(bf16)


def load_weights(after_ref, *refs):
    count = (len(refs) - 2) // 2
    sources, targets, turn_out, sem = refs[:count], refs[count : 2 * count], refs[-2], refs[-1]
    copies = [pltpu.make_async_copy(s, t, sem.at[i]) for i, (s, t) in enumerate(zip(sources, targets))]
    for c in copies:
        c.start()
    turn_out[...] = after_ref[: turn_out.shape[0], : turn_out.shape[1]].astype(f32)
    for c in copies:
        c.wait()


def feed_forward(*refs, groups, cut):
    count = sum(sum(g) for g in groups)
    pieces, (w_gate, w_up, w_down, turn_ref) = refs[:count], refs[count : count + 4]
    *outs, turn_out, x, act = refs[count + 4 :]
    at = 0
    for p in pieces:
        x[at : at + p.shape[0]] = p[...]
        at += p.shape[0]
    blocks, rows, width = outs[0].shape
    size_out = blocks // cut
    wide = 2 * LANES
    hidden = w_gate.shape[1]
    for i in range(0, hidden, wide):
        size = min(wide, hidden - i)
        lanes = slice(i, i + size)
        both = jnp.concatenate([w_gate[:, lanes], w_up[:, lanes]], axis=1)
        part = jnp.dot(x[...], both, preferred_element_type=f32)
        g, u = part[:, :size], part[:, size:]
        act[:, lanes] = (g / (1.0 + jnp.exp(-g)) * u).astype(bf16)
    for i in range(blocks):
        part = jnp.dot(act[...], w_down[:, i * width : (i + 1) * width], preferred_element_type=f32)
        part = part.astype(bf16)
        for j in range(len(groups)):
            own, *others = outs[j * (cut + 1) : (j + 1) * (cut + 1)]
            own[i] = part[2 * j * rows : (2 * j + 1) * rows]
            others[i // size_out][i % size_out] = part[(2 * j + 1) * rows : (2 * j + 2) * rows]
    turn_out[...] = turn_ref[...]


def add_up(*refs, pieces):
    *parts, out_ref = refs
    for i in range(out_ref.shape[0]):
        total, at = None, 0
        for n in pieces:
            size = out_ref.shape[0] // n
            term = parts[at + i // size][i % size].astype(f32)
            total = term if total is None else total + term
            at += n
        out_ref[i] = total.astype(out_ref.dtype)


def combine(recv_ref, ids_ref, weight_ref, res_ref, out_ref):
    experts, slots, width = recv_ref.shape
    tokens, top = ids_ref.shape
    rows = recv_ref[...].reshape(experts * slots, width)
    expert = lax.broadcasted_iota(jnp.int32, (tokens, experts), 1)
    named = [ids_ref[:, k : k + 1] == expert for k in range(top)]
    chosen = jnp.zeros((tokens, experts), f32)
    for k in range(top):
        chosen = jnp.where(named[k], 1.0, chosen)
    row = lax.broadcasted_iota(jnp.int32, (tokens, tokens), 0)
    col = lax.broadcasted_iota(jnp.int32, (tokens, tokens), 1)
    earlier = jnp.where(col < row, 1.0, 0.0).astype(bf16)
    place = jnp.dot(earlier, chosen.astype(bf16), preferred_element_type=f32)
    place = place + (expert * slots).astype(f32)
    slot = lax.broadcasted_iota(jnp.int32, (tokens, experts * slots), 1)
    total = res_ref[...]
    for k in range(top):
        at = jnp.sum(jnp.where(named[k], place, 0.0), axis=1, keepdims=True).astype(jnp.int32)
        pick = jnp.where(slot == at, 1.0, 0.0).astype(bf16)
        total = total + weight_ref[:, k : k + 1] * jnp.dot(pick, rows, preferred_element_type=f32)
    out_ref[...] = total.astype(out_ref.dtype)


def scan_tables(table, turns):
    return table.reshape(SUBS, turns, -1).transpose(1, 0, 2)


def run_first(step, sig, into, rate, prompts):
    tokens, channels = step.shape
    states = rate.shape[0]
    turns = into.shape[0]
    tiles = channels // LANES
    return pl.pallas_call(
        first_pass,
        out_shape=(
            jax.ShapeDtypeStruct((prompts, states + 1, channels), f32),
            jax.ShapeDtypeStruct((prompts, states, SUBS, channels), f32),
            jax.ShapeDtypeStruct((prompts, SUBS, channels), f32),
        ),
        in_specs=[vmem()] * 4,
        out_specs=(vmem(),) * 3,
        scratch_shapes=[
            pltpu.VMEM((tiles, tokens, LANES), f32),
            pltpu.VMEM((tiles, tokens, LANES), f32),
            pltpu.VMEM((turns, prompts * states, SUBS, LANES), f32),
        ],
        compiler_params=params(24),
        name="scan_first",
    )(step, sig, into, rate)


def run_second(coords, step, sig, gate, into, outof, rate, skip, before, pre, ends):
    tokens, channels = step.shape
    prompts, states = before.shape[:2]
    turns = into.shape[0]
    tiles = channels // LANES
    return pl.pallas_call(
        second_pass,
        out_shape=jax.ShapeDtypeStruct((tokens, channels), bf16),
        in_specs=[smem()] + [vmem()] * 10,
        out_specs=vmem(),
        scratch_shapes=[
            pltpu.VMEM((tiles, tokens, LANES), f32),
            pltpu.VMEM((tiles, tokens, LANES), f32),
            pltpu.VMEM((tiles, tokens, LANES), f32),
            pltpu.VMEM((turns, prompts * states, SUBS, LANES), f32),
            pltpu.VMEM((turns, prompts * states, SUBS, LANES), f32),
            pltpu.VMEM((states, LANES), f32),
        ],
        compiler_params=params(16),
        cost_estimate=pl.CostEstimate(flops=2 * 10**9, bytes_accessed=2 * MIB, transcendentals=0),
        name="scan_second",
    )(coords, step, sig, gate, into, outof, rate, skip, before, pre, ends)


def run_project(coords, mixed, ids, proj, share, sides):
    tokens = mixed.shape[0]
    nx, nz = sides
    blocks = proj.shape[0] * proj.shape[2] // share
    return pl.pallas_call(
        functools.partial(project, sides=sides),
        out_shape=[jax.ShapeDtypeStruct((nx, tokens // 2, share), bf16)] * nz
        + [jax.ShapeDtypeStruct((nz, tokens // 2, share), bf16)] * nx
        + [jax.ShapeDtypeStruct(ids.shape, ids.dtype)],
        in_specs=[smem(), vmem(), vmem(), anywhere()],
        out_specs=[vmem()] * (nx + nz + 1),
        scratch_shapes=[
            pltpu.VMEM((blocks, tokens, share), bf16),
            pltpu.VMEM(proj.shape, bf16),
            pltpu.SemaphoreType.DMA((proj.shape[0],)),
        ],
        compiler_params=params(16),
        name="project",
    )(coords, mixed, ids, pltpu.with_memory_space_constraint(proj, pltpu.HBM))


def run_fold(coords, parts, sides):
    nx, nz = sides
    _, half, share = parts[0].shape
    return pl.pallas_call(
        functools.partial(fold, sides=sides),
        out_shape=[jax.ShapeDtypeStruct((half, share), bf16)] * (nx + nz),
        in_specs=[smem()] + [vmem()] * (nx + nz),
        out_specs=[vmem()] * (nx + nz),
        compiler_params=params(8),
        name="fold",
    )(coords, *parts)


def run_dispatch(recvs, hidden, ids, experts, slots, sides):
    tokens, share = hidden.shape
    return pl.pallas_call(
        functools.partial(dispatch, sides=sides),
        out_shape=(
            jax.ShapeDtypeStruct((tokens, share), f32),
            jax.ShapeDtypeStruct((experts, slots, share), bf16),
        ),
        in_specs=[vmem()] * (len(recvs) + 2),
        out_specs=(vmem(),) * 2,
        scratch_shapes=[pltpu.VMEM((experts * slots, tokens), bf16)],
        compiler_params=params(8),
        name="dispatch",
    )(*recvs, hidden, ids)


def run_normalize(recv, gain):
    blocks, slots, width = recv.shape
    return pl.pallas_call(
        normalize,
        out_shape=jax.ShapeDtypeStruct((slots, blocks * width), bf16),
        in_specs=[vmem()] * 2,
        out_specs=vmem(),
        compiler_params=params(8),
        name="normalize",
    )(recv, gain)


def run_load(after, *weights):
    return pl.pallas_call(
        load_weights,
        out_shape=[pltpu.VMEM(w.shape, w.dtype) for w in weights] + [jax.ShapeDtypeStruct((8, LANES), f32)],
        in_specs=[vmem()] + [pl.BlockSpec(memory_space=pltpu.HBM)] * len(weights),
        out_specs=[vmem()] * (len(weights) + 1),
        scratch_shapes=[pltpu.SemaphoreType.DMA((len(weights),))],
        compiler_params=params(8),
        cost_estimate=pl.CostEstimate(flops=0, bytes_accessed=2 * sum(w.nbytes for w in weights), transcendentals=0),
        name="load_weights",
    )(after, *[pltpu.with_memory_space_constraint(w, pltpu.HBM) for w in weights])


def run_ffn(groups, weights, turn, share, cut=1):
    pieces = [p for own, other in groups for p in (*own, *other)]
    rows = sum(p.shape[0] for p in groups[0][0])
    depth, hidden = weights[0].shape
    total = 2 * rows * len(groups)
    part = jax.ShapeDtypeStruct((depth // share, rows, share), bf16)
    piece = jax.ShapeDtypeStruct((depth // share // cut, rows, share), bf16)
    weights = [pltpu.with_memory_space_constraint(w, pltpu.VMEM) for w in weights]
    return pl.pallas_call(
        functools.partial(feed_forward, groups=tuple((len(own), len(other)) for own, other in groups), cut=cut),
        out_shape=(part, *(piece,) * cut) * len(groups) + (jax.ShapeDtypeStruct(turn.shape, turn.dtype),),
        in_specs=[vmem()] * (len(pieces) + 4),
        out_specs=(vmem(),) * ((cut + 1) * len(groups) + 1),
        scratch_shapes=[pltpu.VMEM((total, depth), bf16), pltpu.VMEM((total, hidden), bf16)],
        compiler_params=params(12),
        cost_estimate=pl.CostEstimate(
            flops=6 * total * depth * hidden, bytes_accessed=4 * total * depth, transcendentals=0
        ),
        name="feed_forward",
    )(*pieces, *weights, turn)


def run_add(*parts, dtype=bf16, bytes_accessed=MIB):
    parts = [p if isinstance(p, list) else [p] for p in parts]
    flat = [piece for p in parts for piece in p]
    return pl.pallas_call(
        functools.partial(add_up, pieces=tuple(len(p) for p in parts)),
        out_shape=jax.ShapeDtypeStruct((sum(p.shape[0] for p in parts[0]), *flat[0].shape[1:]), dtype),
        in_specs=[vmem()] * len(flat),
        out_specs=vmem(),
        compiler_params=params(8),
        cost_estimate=pl.CostEstimate(flops=0, bytes_accessed=bytes_accessed, transcendentals=0),
        name="add_up",
    )(*flat)


def run_combine(recv, ids, weights, res):
    return pl.pallas_call(
        combine,
        out_shape=jax.ShapeDtypeStruct(res.shape, bf16),
        in_specs=[vmem()] * 4,
        out_specs=vmem(),
        compiler_params=params(16),
        name="combine",
    )(recv, ids, weights, res)


def on_device(
    mixer_input, gate_in, step_size, decay_rate, state_in, state_out, skip, out_proj, hidden_in, norm_gain,
    w_gate, w_up, w_down, route_ids, route_weight,
):
    slab_len, prompts, channels = mixer_input.shape
    tokens = slab_len * prompts
    share = hidden_in.shape[2]
    chips = lax.axis_size("y")
    ctx, exp = ("y", "core"), ("x", "z")
    experts = lax.axis_size(exp) * w_gate.shape[0]
    slots = 4 * tokens // experts
    turns = slab_len // SUBS

    def swap(value):
        return lax.ppermute(value, "core", [(0, 1), (1, 0)])

    def ring(value, d):
        return lax.ppermute(value, "y", [(i, (i + d) % chips) for i in range(chips)])

    proj = lax.all_gather(out_proj, ctx)
    sig = mixer_input.reshape(tokens, channels)
    step = step_size.reshape(tokens, channels)
    into = scan_tables(state_in, turns)
    end, before, pre = run_first(step, sig, into, decay_rate, prompts)
    ends = lax.all_gather(end, ctx)
    coords = jnp.stack([lax.axis_index(a).astype(jnp.int32) for a in (ctx, "x", "z")])
    gate = gate_in.reshape(tokens, channels)
    outof = scan_tables(state_out, turns)
    mixed = run_second(
        coords, step, sig, gate, into, outof, decay_rate, skip.reshape(1, channels), before, pre, ends
    )
    sides = (lax.axis_size("x"), lax.axis_size("z"))

    def shift(value, axis, d):
        n = lax.axis_size(axis)
        return lax.ppermute(value, axis, [(i, (i + d) % n) for i in range(n)]) if d else value

    nx, nz = sides
    ids = route_ids.reshape(tokens, -1)
    *parts, by_choice = run_project(coords, mixed, ids.T, proj, share, sides)
    hidden = hidden_in.reshape(tokens, share)
    parts = [shift(p, "z", d) for d, p in enumerate(parts[:nz])] + [shift(p, "x", d) for d, p in enumerate(parts[nz:])]
    parts = run_fold(coords, parts, sides)
    parts = [shift(p, "x", d) for d, p in enumerate(parts[:nx])] + [shift(p, "z", d) for d, p in enumerate(parts[nx:])]
    residual, slot_rows = run_dispatch(parts, hidden, by_choice, experts, slots, sides)
    whole = lax.all_to_all(slot_rows, exp, 0, 0, tiled=True)
    own = run_normalize(whole, norm_gain.reshape(1, -1))

    half = slots // 2
    own_sib = swap(own)
    low = ring(own, 1)
    high = ring(own, -1)
    *weights, turn = run_load(own, w_gate[0], w_up[0], w_down[0])
    own_sib, turn = lax.optimization_barrier((own_sib, turn))
    mine0, other0, turn = run_ffn([([own], [own_sib])], weights, turn, share)
    low, high, turn = lax.optimization_barrier((low, high, turn))
    from0 = swap(other0)
    far_low, far_high = ring(low[:half], 1), ring(high[half:], -1)
    low_sib, high_sib = swap(low), swap(high)
    low_sib, from0 = lax.optimization_barrier((low_sib, from0))
    mine1, other1, mine3, other3, turn = run_ffn([([low], [low_sib]), ([high], [high_sib])], weights, turn, share)
    far_low, far_high, turn, other1, other3 = lax.optimization_barrier((far_low, far_high, turn, other1, other3))
    far_low_sib, far_high_sib = swap(far_low), swap(far_high)
    low_sum, high_sum = run_add(mine1, swap(other1)), run_add(mine3, swap(other3))
    low_sum, high_sum, turn = lax.optimization_barrier((low_sum, high_sum, turn))
    back1, back3 = ring(low_sum, -1), ring(high_sum, 1)
    mine2, *other2, turn = run_ffn(
        [([far_low, far_high], [far_low_sib, far_high_sib])], weights, turn, share, cut=CUT
    )
    back2 = ring(run_add(mine2, [swap(p) for p in other2]), 2)
    near = run_add(mine0, from0, back1, back3, dtype=f32, bytes_accessed=64 * MIB)
    returned = run_add(near, back2)

    back = lax.all_to_all(returned, exp, 0, 0, tiled=True)
    out = run_combine(back, ids, route_weight.reshape(tokens, -1), residual)
    return out.reshape(slab_len, prompts, share)


def solution(mesh):
    ctx, exp = ("y", "core"), ("x", "z")
    n_ctx, n_exp = mesh.devices.shape
    side = int(round(n_exp**0.5))
    mesh = Mesh(mesh.devices.reshape(n_ctx // 2, 2, side, n_exp // side), ctx + exp)
    placed = (
        P(ctx, None, exp),
        P(ctx, None, exp),
        P(ctx, None, exp),
        P(None, exp),
        P(ctx, None, None),
        P(ctx, None, None),
        P(exp),
        P(exp, ctx),
        P(ctx, None, exp),
        P(),
        P(exp, None, ctx),
        P(exp, None, ctx),
        P(exp, ctx, None),
        P(ctx, None, None),
        P(ctx, None, None),
    )
    return jax.shard_map(on_device, mesh=mesh, in_specs=placed, out_specs=P(ctx, None, exp), check_vma=False)
```

```python
import functools

import jax
import jax.numpy as jnp
from jax import lax
from jax.experimental import pallas as pl
from jax.experimental.pallas import tpu as pltpu
from jax.sharding import Mesh
from jax.sharding import PartitionSpec as P

epsilon = 1e-06
LOG2E = 1.4426950408889634
SUBS = 8
LANES = 128
CUT = 1
UNROLL = 16
MIB = 1 << 20
f32, bf16 = jnp.float32, jnp.bfloat16


def params(mib):
    return pltpu.CompilerParams(vmem_limit_bytes=mib * MIB)


def vmem():
    return pl.BlockSpec(memory_space=pltpu.VMEM)


def smem():
    return pl.BlockSpec(memory_space=pltpu.SMEM)


def anywhere():
    return pl.BlockSpec(memory_space=pl.ANY)


def spread(table_ref, out_ref):
    turns, _, columns = table_ref.shape

    def turn(t, _):
        row = table_ref[t]
        for i in range(columns):
            out_ref[t, i] = jnp.broadcast_to(row[:, i : i + 1], (SUBS, LANES))
        return 0

    lax.fori_loop(0, turns, turn, 0)


def split_lanes(step_ref, sig_ref, st4, v4):
    for q in range(st4.shape[0]):
        lanes = slice(q * LANES, (q + 1) * LANES)
        st = step_ref[:, lanes]
        st4[q] = st
        v4[q] = st * sig_ref[:, lanes].astype(f32)


def first_pass(step_ref, sig_ref, into_ref, rate_ref, fin_ref, before_ref, pre_ref, st4, v4, into_b):
    states, channels = rate_ref.shape
    prompts = fin_ref.shape[0]
    turns = into_ref.shape[0]
    hop = turns * prompts
    spread(into_ref, into_b)
    split_lanes(step_ref, sig_ref, st4, v4)
    sub = lax.broadcasted_iota(jnp.int32, (SUBS, LANES), 0)
    for q in range(channels // LANES):
        lanes = slice(q * LANES, (q + 1) * LANES)
        rates = [
            jnp.broadcast_to(rate_ref[n : n + 1, lanes] * -LOG2E, (SUBS, LANES)) for n in range(states)
        ]
        for b in range(prompts):

            def turn(t, held, q=q, b=b, rates=rates):
                total, hs = held
                st = st4[q, pl.ds(t * prompts + b, SUBS, stride=hop), :]
                v = v4[q, pl.ds(t * prompts + b, SUBS, stride=hop), :]
                new = []
                for n in range(states):
                    new.append(jnp.exp2(st * rates[n]) * hs[n] + v * into_b[t, b * states + n])
                return total + st, tuple(new)

            zero = jnp.zeros((SUBS, LANES), f32)
            width, hs = lax.fori_loop(0, turns, turn, (zero, (zero,) * states))
            hs = list(hs)
            for d in (1, 2, 4):
                live = sub >= d
                for n in range(states):
                    moved = jnp.where(live, pltpu.roll(hs[n], d, 0), 0.0)
                    hs[n] = hs[n] + jnp.exp2(rates[n] * width) * moved
                width = width + jnp.where(live, pltpu.roll(width, d, 0), 0.0)
            for n in range(states):
                fin_ref[b, n : n + 1, lanes] = hs[n][SUBS - 1 :]
                before_ref[b, n, :, lanes] = jnp.where(sub >= 1, pltpu.roll(hs[n], 1, 0), 0.0)
            fin_ref[b, states : states + 1, lanes] = width[SUBS - 1 :]
            pre_ref[b, :, lanes] = jnp.where(sub >= 1, pltpu.roll(width, 1, 0), 0.0)


def second_pass(
    coords_ref, step_ref, sig_ref, gate_ref, into_ref, outof_ref, rate_ref, skip_ref, before_ref, pre_ref,
    ends_ref, mixed_ref, st4, v4, y4, into_b, outof_b, enter,
):
    states, channels = rate_ref.shape
    prompts = pre_ref.shape[0]
    turns = into_ref.shape[0]
    hop = turns * prompts
    spread(into_ref, into_b)
    spread(outof_ref, outof_b)
    split_lanes(step_ref, sig_ref, st4, v4)
    mine = coords_ref[0]
    for q in range(channels // LANES):
        lanes = slice(q * LANES, (q + 1) * LANES)
        rate_q = rate_ref[:, lanes] * -LOG2E
        rates = [jnp.broadcast_to(rate_q[n : n + 1], (SUBS, LANES)) for n in range(states)]
        for b in range(prompts):
            h0 = jnp.zeros((states, LANES), f32)
            for c in range(ends_ref.shape[0] - 1):
                live = jnp.where(c < mine, 1.0, 0.0).astype(f32)
                decay = jnp.exp2(rate_q * (ends_ref[c, b, states : states + 1, lanes] * live))
                h0 = decay * h0 + ends_ref[c, b, :states, lanes] * live
            enter[...] = h0
            pre = pre_ref[b, :, lanes]
            hs = tuple(
                before_ref[b, n, :, lanes]
                + jnp.exp2(rates[n] * pre) * jnp.broadcast_to(enter[n : n + 1], (SUBS, LANES))
                for n in range(states)
            )

            def turn(t, hs, q=q, b=b, rates=rates):
                rows = pl.ds(t * prompts + b, SUBS, stride=hop)
                st = st4[q, rows, :]
                v = v4[q, rows, :]
                new, sums = [], [None] * 4
                for n in range(states):
                    h = jnp.exp2(st * rates[n]) * hs[n] + v * into_b[t, b * states + n]
                    new.append(h)
                    term = h * outof_b[t, b * states + n]
                    sums[n % 4] = term if sums[n % 4] is None else sums[n % 4] + term
                y4[q, rows, :] = (sums[0] + sums[1]) + (sums[2] + sums[3])
                return tuple(new)

            lax.fori_loop(0, turns, turn, hs, unroll=UNROLL)
        sig = sig_ref[:, lanes].astype(f32)
        gate = gate_ref[:, lanes].astype(f32)
        y = y4[q] + skip_ref[:, lanes] * sig
        mixed_ref[:, lanes] = (y * (gate / (1.0 + jnp.exp(-gate)))).astype(bf16)


def project(coords_ref, mixed_ref, ids_ref, proj_hbm, *rest, sides):
    nx, nz = sides
    z_refs, x_refs = rest[:nz], rest[nz : nz + nx]
    ids_out, whole, proj, sem = rest[nz + nx :]
    _, half, width = z_refs[0].shape
    blocks, _, columns = proj.shape
    for c in range(blocks):
        pltpu.make_async_copy(proj_hbm.at[c], proj.at[c], sem.at[c]).start()
    for c in range(blocks):
        pltpu.make_async_copy(proj_hbm.at[c], proj.at[c], sem.at[c]).wait()
        part = jnp.dot(mixed_ref[...], proj[c], preferred_element_type=f32).astype(bf16)
        for i in range(columns // width):
            whole[c * (columns // width) + i] = part[:, i * width : (i + 1) * width]
    x, z = coords_ref[1], coords_ref[2]
    for d, out in enumerate(z_refs):
        for i in range(nx):
            out[i] = whole[i * nz + lax.rem(z + d, nz), :half]
    for d, out in enumerate(x_refs):
        for i in range(nz):
            out[i] = whole[lax.rem(x + d, nx) * nz + i, half:]
    ids_out[...] = ids_ref[...]


def fold(coords_ref, *rest, sides, ways):
    nx, nz = sides
    parts, outs = rest[: len(ways)], rest[len(ways) :]
    groups = [[p for p, (i, _) in zip(parts, ways) if i == group] for group in (0, 1)]
    x, z = coords_ref[1], coords_ref[2]
    for parts, outs, at, count in ((groups[0], outs[:nx], x, nx), (groups[1], outs[nx:], z, nz)):
        for d, out in enumerate(outs):
            block = lax.rem(at + d, count)
            total = parts[0][block].astype(f32)
            for p in parts[1:]:
                total = total + p[block].astype(f32)
            out[...] = total.astype(bf16)


def dispatch(*refs, ways):
    *recvs, hidden_ref, ids_ref, res_ref, slots_ref, pick = refs
    experts, slots, width = slots_ref.shape
    tokens = hidden_ref.shape[0]
    half = tokens // 2
    groups = [[p for p, (i, _) in zip(recvs, ways) if i == group] for group in (0, 1)]
    for rows, parts in ((slice(0, half), groups[0]), (slice(half, tokens), groups[1])):
        part = hidden_ref[rows].astype(f32)
        for p in parts:
            part = part + p[...].astype(f32)
        res_ref[rows] = part
    total = res_ref[...]
    expert = lax.broadcasted_iota(jnp.int32, (experts, tokens), 0)
    chosen = jnp.zeros((experts, tokens), f32)
    for k in range(ids_ref.shape[0]):
        chosen = jnp.where(ids_ref[k : k + 1, :] == expert, 1.0, chosen)
    row = lax.broadcasted_iota(jnp.int32, (tokens, tokens), 0)
    col = lax.broadcasted_iota(jnp.int32, (tokens, tokens), 1)
    earlier = jnp.where(row < col, 1.0, 0.0).astype(bf16)
    place = jnp.dot(chosen.astype(bf16), earlier, preferred_element_type=f32)
    place = jnp.where(chosen > 0.5, place, -1.0)
    slot = lax.broadcasted_iota(jnp.int32, (slots, tokens), 0).astype(f32)
    for e in range(experts):
        pick[e * slots : (e + 1) * slots] = jnp.where(place[e : e + 1] == slot, 1.0, 0.0).astype(bf16)
    rows = jnp.dot(pick[...], total.astype(bf16), preferred_element_type=f32).astype(bf16)
    slots_ref[...] = rows.reshape(experts, slots, width)


def normalize(recv_ref, gain_ref, out_ref):
    blocks, slots, width = recv_ref.shape
    square = jnp.zeros((slots, width), f32)
    for i in range(blocks):
        part = recv_ref[i].astype(f32)
        square = square + part * part
    mean = jnp.sum(square, axis=1, keepdims=True) / (blocks * width)
    scale = lax.rsqrt(mean + epsilon)
    for i in range(blocks):
        lanes = slice(i * width, (i + 1) * width)
        out_ref[:, lanes] = (recv_ref[i].astype(f32) * scale * gain_ref[:, lanes]).astype(bf16)


def load_weights(after_ref, *refs):
    count = (len(refs) - 2) // 2
    sources, targets, turn_out, sem = refs[:count], refs[count : 2 * count], refs[-2], refs[-1]
    copies = [pltpu.make_async_copy(s, t, sem.at[i]) for i, (s, t) in enumerate(zip(sources, targets))]
    for c in copies:
        c.start()
    turn_out[...] = after_ref[: turn_out.shape[0], : turn_out.shape[1]].astype(f32)
    for c in copies:
        c.wait()


def feed_forward(*refs, groups, cut):
    count = sum(sum(g) for g in groups)
    pieces, (w_gate, w_up, w_down, turn_ref) = refs[:count], refs[count : count + 4]
    *outs, turn_out, x, act = refs[count + 4 :]
    at = 0
    for p in pieces:
        x[at : at + p.shape[0]] = p[...]
        at += p.shape[0]
    blocks, rows, width = outs[0].shape
    size_out = blocks // cut
    wide = 2 * LANES
    hidden = w_gate.shape[1]
    for i in range(0, hidden, wide):
        size = min(wide, hidden - i)
        lanes = slice(i, i + size)
        both = jnp.concatenate([w_gate[:, lanes], w_up[:, lanes]], axis=1)
        part = jnp.dot(x[...], both, preferred_element_type=f32)
        g, u = part[:, :size], part[:, size:]
        act[:, lanes] = (g / (1.0 + jnp.exp(-g)) * u).astype(bf16)
    for i in range(blocks):
        part = jnp.dot(act[...], w_down[:, i * width : (i + 1) * width], preferred_element_type=f32)
        part = part.astype(bf16)
        for j in range(len(groups)):
            own, *others = outs[j * (cut + 1) : (j + 1) * (cut + 1)]
            own[i] = part[2 * j * rows : (2 * j + 1) * rows]
            others[i // size_out][i % size_out] = part[(2 * j + 1) * rows : (2 * j + 2) * rows]
    turn_out[...] = turn_ref[...]


def add_up(*refs, pieces):
    *parts, out_ref = refs
    for i in range(out_ref.shape[0]):
        total, at = None, 0
        for n in pieces:
            size = out_ref.shape[0] // n
            term = parts[at + i // size][i % size].astype(f32)
            total = term if total is None else total + term
            at += n
        out_ref[i] = total.astype(out_ref.dtype)


def combine(recv_ref, ids_ref, weight_ref, res_ref, out_ref):
    experts, slots, width = recv_ref.shape
    tokens, top = ids_ref.shape
    rows = recv_ref[...].reshape(experts * slots, width)
    expert = lax.broadcasted_iota(jnp.int32, (tokens, experts), 1)
    named = [ids_ref[:, k : k + 1] == expert for k in range(top)]
    chosen = jnp.zeros((tokens, experts), f32)
    for k in range(top):
        chosen = jnp.where(named[k], 1.0, chosen)
    row = lax.broadcasted_iota(jnp.int32, (tokens, tokens), 0)
    col = lax.broadcasted_iota(jnp.int32, (tokens, tokens), 1)
    earlier = jnp.where(col < row, 1.0, 0.0).astype(bf16)
    place = jnp.dot(earlier, chosen.astype(bf16), preferred_element_type=f32)
    place = place + (expert * slots).astype(f32)
    slot = lax.broadcasted_iota(jnp.int32, (tokens, experts * slots), 1)
    total = res_ref[...]
    for k in range(top):
        at = jnp.sum(jnp.where(named[k], place, 0.0), axis=1, keepdims=True).astype(jnp.int32)
        pick = jnp.where(slot == at, 1.0, 0.0).astype(bf16)
        total = total + weight_ref[:, k : k + 1] * jnp.dot(pick, rows, preferred_element_type=f32)
    out_ref[...] = total.astype(out_ref.dtype)


def scan_tables(table, turns):
    return table.reshape(SUBS, turns, -1).transpose(1, 0, 2)


def run_first(step, sig, into, rate, prompts):
    tokens, channels = step.shape
    states = rate.shape[0]
    turns = into.shape[0]
    tiles = channels // LANES
    return pl.pallas_call(
        first_pass,
        out_shape=(
            jax.ShapeDtypeStruct((prompts, states + 1, channels), f32),
            jax.ShapeDtypeStruct((prompts, states, SUBS, channels), f32),
            jax.ShapeDtypeStruct((prompts, SUBS, channels), f32),
        ),
        in_specs=[vmem()] * 4,
        out_specs=(vmem(),) * 3,
        scratch_shapes=[
            pltpu.VMEM((tiles, tokens, LANES), f32),
            pltpu.VMEM((tiles, tokens, LANES), f32),
            pltpu.VMEM((turns, prompts * states, SUBS, LANES), f32),
        ],
        compiler_params=params(24),
        name="scan_first",
    )(step, sig, into, rate)


def run_second(coords, step, sig, gate, into, outof, rate, skip, before, pre, ends):
    tokens, channels = step.shape
    prompts, states = before.shape[:2]
    turns = into.shape[0]
    tiles = channels // LANES
    return pl.pallas_call(
        second_pass,
        out_shape=jax.ShapeDtypeStruct((tokens, channels), bf16),
        in_specs=[smem()] + [vmem()] * 10,
        out_specs=vmem(),
        scratch_shapes=[
            pltpu.VMEM((tiles, tokens, LANES), f32),
            pltpu.VMEM((tiles, tokens, LANES), f32),
            pltpu.VMEM((tiles, tokens, LANES), f32),
            pltpu.VMEM((turns, prompts * states, SUBS, LANES), f32),
            pltpu.VMEM((turns, prompts * states, SUBS, LANES), f32),
            pltpu.VMEM((states, LANES), f32),
        ],
        compiler_params=params(16),
        cost_estimate=pl.CostEstimate(flops=2 * 10**9, bytes_accessed=2 * MIB, transcendentals=0),
        name="scan_second",
    )(coords, step, sig, gate, into, outof, rate, skip, before, pre, ends)


def run_project(coords, mixed, ids, proj, share, sides):
    tokens = mixed.shape[0]
    nx, nz = sides
    blocks = proj.shape[0] * proj.shape[2] // share
    return pl.pallas_call(
        functools.partial(project, sides=sides),
        out_shape=[jax.ShapeDtypeStruct((nx, tokens // 2, share), bf16)] * nz
        + [jax.ShapeDtypeStruct((nz, tokens // 2, share), bf16)] * nx
        + [jax.ShapeDtypeStruct(ids.shape, ids.dtype)],
        in_specs=[smem(), vmem(), vmem(), anywhere()],
        out_specs=[vmem()] * (nx + nz + 1),
        scratch_shapes=[
            pltpu.VMEM((blocks, tokens, share), bf16),
            pltpu.VMEM(proj.shape, bf16),
            pltpu.SemaphoreType.DMA((proj.shape[0],)),
        ],
        compiler_params=params(16),
        name="project",
    )(coords, mixed, ids, pltpu.with_memory_space_constraint(proj, pltpu.HBM))


def run_fold(coords, parts, sides, ways):
    nx, nz = sides
    _, half, share = parts[0].shape
    return pl.pallas_call(
        functools.partial(fold, sides=sides, ways=ways),
        out_shape=[jax.ShapeDtypeStruct((half, share), bf16)] * (nx + nz),
        in_specs=[smem()] + [vmem()] * (nx + nz),
        out_specs=[vmem()] * (nx + nz),
        compiler_params=params(8),
        name="fold",
    )(coords, *parts)


def run_dispatch(recvs, hidden, ids, experts, slots, ways):
    tokens, share = hidden.shape
    return pl.pallas_call(
        functools.partial(dispatch, ways=ways),
        out_shape=(
            jax.ShapeDtypeStruct((tokens, share), f32),
            jax.ShapeDtypeStruct((experts, slots, share), bf16),
        ),
        in_specs=[vmem()] * (len(recvs) + 2),
        out_specs=(vmem(),) * 2,
        scratch_shapes=[pltpu.VMEM((experts * slots, tokens), bf16)],
        compiler_params=params(8),
        name="dispatch",
    )(*recvs, hidden, ids)


def run_normalize(recv, gain):
    blocks, slots, width = recv.shape
    return pl.pallas_call(
        normalize,
        out_shape=jax.ShapeDtypeStruct((slots, blocks * width), bf16),
        in_specs=[vmem()] * 2,
        out_specs=vmem(),
        compiler_params=params(8),
        name="normalize",
    )(recv, gain)


def run_load(after, *weights):
    return pl.pallas_call(
        load_weights,
        out_shape=[pltpu.VMEM(w.shape, w.dtype) for w in weights] + [jax.ShapeDtypeStruct((8, LANES), f32)],
        in_specs=[vmem()] + [pl.BlockSpec(memory_space=pltpu.HBM)] * len(weights),
        out_specs=[vmem()] * (len(weights) + 1),
        scratch_shapes=[pltpu.SemaphoreType.DMA((len(weights),))],
        compiler_params=params(8),
        cost_estimate=pl.CostEstimate(flops=0, bytes_accessed=2 * sum(w.nbytes for w in weights), transcendentals=0),
        name="load_weights",
    )(after, *[pltpu.with_memory_space_constraint(w, pltpu.HBM) for w in weights])


def run_ffn(groups, weights, turn, share, cut=1):
    pieces = [p for own, other in groups for p in (*own, *other)]
    rows = sum(p.shape[0] for p in groups[0][0])
    depth, hidden = weights[0].shape
    total = 2 * rows * len(groups)
    part = jax.ShapeDtypeStruct((depth // share, rows, share), bf16)
    piece = jax.ShapeDtypeStruct((depth // share // cut, rows, share), bf16)
    weights = [pltpu.with_memory_space_constraint(w, pltpu.VMEM) for w in weights]
    return pl.pallas_call(
        functools.partial(feed_forward, groups=tuple((len(own), len(other)) for own, other in groups), cut=cut),
        out_shape=(part, *(piece,) * cut) * len(groups) + (jax.ShapeDtypeStruct(turn.shape, turn.dtype),),
        in_specs=[vmem()] * (len(pieces) + 4),
        out_specs=(vmem(),) * ((cut + 1) * len(groups) + 1),
        scratch_shapes=[pltpu.VMEM((total, depth), bf16), pltpu.VMEM((total, hidden), bf16)],
        compiler_params=params(12),
        cost_estimate=pl.CostEstimate(
            flops=6 * total * depth * hidden, bytes_accessed=4 * total * depth, transcendentals=0
        ),
        name="feed_forward",
    )(*pieces, *weights, turn)


def run_add(*parts, dtype=bf16, bytes_accessed=MIB):
    parts = [p if isinstance(p, list) else [p] for p in parts]
    flat = [piece for p in parts for piece in p]
    return pl.pallas_call(
        functools.partial(add_up, pieces=tuple(len(p) for p in parts)),
        out_shape=jax.ShapeDtypeStruct((sum(p.shape[0] for p in parts[0]), *flat[0].shape[1:]), dtype),
        in_specs=[vmem()] * len(flat),
        out_specs=vmem(),
        compiler_params=params(8),
        cost_estimate=pl.CostEstimate(flops=0, bytes_accessed=bytes_accessed, transcendentals=0),
        name="add_up",
    )(*flat)


def run_combine(recv, ids, weights, res):
    return pl.pallas_call(
        combine,
        out_shape=jax.ShapeDtypeStruct(res.shape, bf16),
        in_specs=[vmem()] * 4,
        out_specs=vmem(),
        compiler_params=params(16),
        name="combine",
    )(recv, ids, weights, res)


def on_device(
    mixer_input, gate_in, step_size, decay_rate, state_in, state_out, skip, out_proj, hidden_in, norm_gain,
    w_gate, w_up, w_down, route_ids, route_weight,
):
    slab_len, prompts, channels = mixer_input.shape
    tokens = slab_len * prompts
    share = hidden_in.shape[2]
    chips = lax.axis_size("y")
    ctx, exp = ("y", "core"), ("x", "z")
    experts = lax.axis_size(exp) * w_gate.shape[0]
    slots = 4 * tokens // experts
    turns = slab_len // SUBS

    def swap(value):
        return lax.ppermute(value, "core", [(0, 1), (1, 0)])

    def ring(value, d):
        return lax.ppermute(value, "y", [(i, (i + d) % chips) for i in range(chips)])

    proj = lax.all_gather(out_proj, ctx)
    sig = mixer_input.reshape(tokens, channels)
    step = step_size.reshape(tokens, channels)
    into = scan_tables(state_in, turns)
    end, before, pre = run_first(step, sig, into, decay_rate, prompts)
    ends = lax.all_gather(end, ctx)
    coords = jnp.stack([lax.axis_index(a).astype(jnp.int32) for a in (ctx, "x", "z")])
    gate = gate_in.reshape(tokens, channels)
    outof = scan_tables(state_out, turns)
    mixed = run_second(
        coords, step, sig, gate, into, outof, decay_rate, skip.reshape(1, channels), before, pre, ends
    )
    sides = (lax.axis_size("x"), lax.axis_size("z"))

    def shift(value, axis, d):
        n = lax.axis_size(axis)
        return lax.ppermute(value, axis, [(i, (i + d) % n) for i in range(n)]) if d else value

    def spread_out(one, one_axis, two, two_axis):
        sides = ((one, one_axis), (two, two_axis))
        ways = [(i, d) for i, (parts, _) in enumerate(sides) for d in range(len(parts))]
        hops = {(i, d): min(d, len(sides[i][0]) - d) for i, d in ways}
        lead = (0, 1)
        ways = sorted(ways, key=lambda w: (w != lead, -hops[w], w[1], w[0]))
        return [shift(sides[i][0][d], sides[i][1], d) for i, d in ways], tuple(ways)

    nx, nz = sides
    ids = route_ids.reshape(tokens, -1)
    *parts, by_choice = run_project(coords, mixed, ids.T, proj, share, sides)
    hidden = hidden_in.reshape(tokens, share)
    parts, ways = spread_out(parts[:nz], "z", parts[nz:], "x")
    parts = run_fold(coords, parts, sides, ways)
    parts, ways = spread_out(parts[:nx], "x", parts[nx:], "z")
    residual, slot_rows = run_dispatch(parts, hidden, by_choice, experts, slots, ways)
    whole = lax.all_to_all(slot_rows, exp, 0, 0, tiled=True)
    own = run_normalize(whole, norm_gain.reshape(1, -1))

    half = slots // 2
    own_sib = swap(own)
    low = ring(own, 1)
    high = ring(own, -1)
    *weights, turn = run_load(own, w_gate[0], w_up[0], w_down[0])
    own_sib, turn = lax.optimization_barrier((own_sib, turn))
    mine0, other0, turn = run_ffn([([own], [own_sib])], weights, turn, share)
    low, high, turn = lax.optimization_barrier((low, high, turn))
    from0 = swap(other0)
    far_low, far_high = ring(low[:half], 1), ring(high[half:], -1)
    low_sib, high_sib = swap(low), swap(high)
    low_sib, from0 = lax.optimization_barrier((low_sib, from0))
    mine1, other1, mine3, other3, turn = run_ffn([([low], [low_sib]), ([high], [high_sib])], weights, turn, share)
    far_low, far_high, turn, other1, other3 = lax.optimization_barrier((far_low, far_high, turn, other1, other3))
    far_low_sib, far_high_sib = swap(far_low), swap(far_high)
    low_sum, high_sum = run_add(mine1, swap(other1)), run_add(mine3, swap(other3))
    low_sum, high_sum, turn = lax.optimization_barrier((low_sum, high_sum, turn))
    back1, back3 = ring(low_sum, -1), ring(high_sum, 1)
    mine2, *other2, turn = run_ffn(
        [([far_low, far_high], [far_low_sib, far_high_sib])], weights, turn, share, cut=CUT
    )
    back2 = ring(run_add(mine2, [swap(p) for p in other2]), 2)
    near = run_add(mine0, from0, back1, back3, dtype=f32, bytes_accessed=64 * MIB)
    returned = run_add(near, back2)

    back = lax.all_to_all(returned, exp, 0, 0, tiled=True)
    out = run_combine(back, ids, route_weight.reshape(tokens, -1), residual)
    return out.reshape(slab_len, prompts, share)


def solution(mesh):
    ctx, exp = ("y", "core"), ("x", "z")
    n_ctx, n_exp = mesh.devices.shape
    side = int(round(n_exp**0.5))
    mesh = Mesh(mesh.devices.reshape(n_ctx // 2, 2, side, n_exp // side), ctx + exp)
    placed = (
        P(ctx, None, exp),
        P(ctx, None, exp),
        P(ctx, None, exp),
        P(None, exp),
        P(ctx, None, None),
        P(ctx, None, None),
        P(exp),
        P(exp, ctx),
        P(ctx, None, exp),
        P(),
        P(exp, None, ctx),
        P(exp, None, ctx),
        P(exp, ctx, None),
        P(ctx, None, None),
        P(ctx, None, None),
    )
    return jax.shard_map(on_device, mesh=mesh, in_specs=placed, out_specs=P(ctx, None, exp), check_vma=False)
```

```python
import functools

import jax
import jax.numpy as jnp
from jax import lax
from jax.experimental import pallas as pl
from jax.experimental.pallas import tpu as pltpu
from jax.sharding import Mesh
from jax.sharding import PartitionSpec as P

epsilon = 1e-06
LOG2E = 1.4426950408889634
SUBS = 8
LANES = 128
CUT = 1
UNROLL = 16
MIB = 1 << 20
f32, bf16 = jnp.float32, jnp.bfloat16


def params(mib):
    return pltpu.CompilerParams(vmem_limit_bytes=mib * MIB)


def vmem():
    return pl.BlockSpec(memory_space=pltpu.VMEM)


def smem():
    return pl.BlockSpec(memory_space=pltpu.SMEM)


def anywhere():
    return pl.BlockSpec(memory_space=pl.ANY)


def spread(table_ref, out_ref):
    turns, _, columns = table_ref.shape

    def turn(t, _):
        row = table_ref[t]
        for i in range(columns):
            out_ref[t, i] = jnp.broadcast_to(row[:, i : i + 1], (SUBS, LANES))
        return 0

    lax.fori_loop(0, turns, turn, 0)


def split_lanes(step_ref, sig_ref, st4, v4):
    for q in range(st4.shape[0]):
        lanes = slice(q * LANES, (q + 1) * LANES)
        st = step_ref[:, lanes]
        st4[q] = st
        v4[q] = st * sig_ref[:, lanes].astype(f32)


def first_pass(step_ref, sig_ref, into_ref, rate_ref, fin_ref, before_ref, pre_ref, st4, v4, into_b):
    states, channels = rate_ref.shape
    prompts = fin_ref.shape[0]
    turns = into_ref.shape[0]
    hop = turns * prompts
    spread(into_ref, into_b)
    split_lanes(step_ref, sig_ref, st4, v4)
    sub = lax.broadcasted_iota(jnp.int32, (SUBS, LANES), 0)
    for q in range(channels // LANES):
        lanes = slice(q * LANES, (q + 1) * LANES)
        rates = [
            jnp.broadcast_to(rate_ref[n : n + 1, lanes] * -LOG2E, (SUBS, LANES)) for n in range(states)
        ]
        for b in range(prompts):

            def turn(t, held, q=q, b=b, rates=rates):
                total, hs = held
                st = st4[q, pl.ds(t * prompts + b, SUBS, stride=hop), :]
                v = v4[q, pl.ds(t * prompts + b, SUBS, stride=hop), :]
                new = []
                for n in range(states):
                    new.append(jnp.exp2(st * rates[n]) * hs[n] + v * into_b[t, b * states + n])
                return total + st, tuple(new)

            zero = jnp.zeros((SUBS, LANES), f32)
            width, hs = lax.fori_loop(0, turns, turn, (zero, (zero,) * states))
            hs = list(hs)
            for d in (1, 2, 4):
                live = sub >= d
                for n in range(states):
                    moved = jnp.where(live, pltpu.roll(hs[n], d, 0), 0.0)
                    hs[n] = hs[n] + jnp.exp2(rates[n] * width) * moved
                width = width + jnp.where(live, pltpu.roll(width, d, 0), 0.0)
            for n in range(states):
                fin_ref[b, n : n + 1, lanes] = hs[n][SUBS - 1 :]
                before_ref[b, n, :, lanes] = jnp.where(sub >= 1, pltpu.roll(hs[n], 1, 0), 0.0)
            fin_ref[b, states : states + 1, lanes] = width[SUBS - 1 :]
            pre_ref[b, :, lanes] = jnp.where(sub >= 1, pltpu.roll(width, 1, 0), 0.0)


def pair_up(core_ref, own_ref, sib_ref, rate_ref, out_ref):
    states = rate_ref.shape[0]
    low = core_ref[0] == 0
    rate = rate_ref[...] * -LOG2E
    for b in range(own_ref.shape[0]):
        first = jnp.where(low, own_ref[b], sib_ref[b])
        second = jnp.where(low, sib_ref[b], own_ref[b])
        decay = jnp.exp2(rate * second[states:])
        out_ref[b, :states] = decay * first[:states] + second[:states]
        out_ref[b, states:] = first[states:] + second[states:]


def second_pass(
    core_ref, step_ref, sig_ref, gate_ref, into_ref, outof_ref, rate_ref, skip_ref, before_ref, pre_ref,
    *rest, earlier,
):
    sib_ref, *pair_refs = rest[: earlier + 1]
    mixed_ref, st4, v4, y4, into_b, outof_b, enter = rest[earlier + 1 :]
    states, channels = rate_ref.shape
    prompts = pre_ref.shape[0]
    turns = into_ref.shape[0]
    hop = turns * prompts
    spread(into_ref, into_b)
    spread(outof_ref, outof_b)
    split_lanes(step_ref, sig_ref, st4, v4)
    live = jnp.where(core_ref[0] > 0, 1.0, 0.0).astype(f32)
    for q in range(channels // LANES):
        lanes = slice(q * LANES, (q + 1) * LANES)
        rate_q = rate_ref[:, lanes] * -LOG2E
        rates = [jnp.broadcast_to(rate_q[n : n + 1], (SUBS, LANES)) for n in range(states)]
        for b in range(prompts):
            h0 = jnp.zeros((states, LANES), f32)
            for pair in pair_refs:
                h0 = jnp.exp2(rate_q * pair[b, states : states + 1, lanes]) * h0 + pair[b, :states, lanes]
            decay = jnp.exp2(rate_q * (sib_ref[b, states : states + 1, lanes] * live))
            enter[...] = decay * h0 + sib_ref[b, :states, lanes] * live
            pre = pre_ref[b, :, lanes]
            hs = tuple(
                before_ref[b, n, :, lanes]
                + jnp.exp2(rates[n] * pre) * jnp.broadcast_to(enter[n : n + 1], (SUBS, LANES))
                for n in range(states)
            )

            def turn(t, hs, q=q, b=b, rates=rates):
                rows = pl.ds(t * prompts + b, SUBS, stride=hop)
                st = st4[q, rows, :]
                v = v4[q, rows, :]
                new, sums = [], [None] * 4
                for n in range(states):
                    h = jnp.exp2(st * rates[n]) * hs[n] + v * into_b[t, b * states + n]
                    new.append(h)
                    term = h * outof_b[t, b * states + n]
                    sums[n % 4] = term if sums[n % 4] is None else sums[n % 4] + term
                y4[q, rows, :] = (sums[0] + sums[1]) + (sums[2] + sums[3])
                return tuple(new)

            lax.fori_loop(0, turns, turn, hs, unroll=UNROLL)
        sig = sig_ref[:, lanes].astype(f32)
        gate = gate_ref[:, lanes].astype(f32)
        y = y4[q] + skip_ref[:, lanes] * sig
        mixed_ref[:, lanes] = (y * (gate / (1.0 + jnp.exp(-gate)))).astype(bf16)


def project(coords_ref, mixed_ref, ids_ref, proj_hbm, *rest, sides):
    nx, nz = sides
    z_refs, x_refs = rest[:nz], rest[nz : nz + nx]
    ids_out, whole, proj, sem = rest[nz + nx :]
    _, half, width = z_refs[0].shape
    blocks, _, columns = proj.shape
    for c in range(blocks):
        pltpu.make_async_copy(proj_hbm.at[c], proj.at[c], sem.at[c]).start()
    for c in range(blocks):
        pltpu.make_async_copy(proj_hbm.at[c], proj.at[c], sem.at[c]).wait()
        part = jnp.dot(mixed_ref[...], proj[c], preferred_element_type=f32).astype(bf16)
        for i in range(columns // width):
            whole[c * (columns // width) + i] = part[:, i * width : (i + 1) * width]
    x, z = coords_ref[1], coords_ref[2]
    for d, out in enumerate(z_refs):
        for i in range(nx):
            out[i] = whole[i * nz + lax.rem(z + d, nz), :half]
    for d, out in enumerate(x_refs):
        for i in range(nz):
            out[i] = whole[lax.rem(x + d, nx) * nz + i, half:]
    ids_out[...] = ids_ref[...]


def fold(coords_ref, *rest, sides, ways):
    nx, nz = sides
    parts, outs = rest[: len(ways)], rest[len(ways) :]
    groups = [[p for p, (i, _) in zip(parts, ways) if i == group] for group in (0, 1)]
    x, z = coords_ref[1], coords_ref[2]
    for parts, outs, at, count in ((groups[0], outs[:nx], x, nx), (groups[1], outs[nx:], z, nz)):
        for d, out in enumerate(outs):
            block = lax.rem(at + d, count)
            total = parts[0][block].astype(f32)
            for p in parts[1:]:
                total = total + p[block].astype(f32)
            out[...] = total.astype(bf16)


def dispatch(*refs, ways):
    *recvs, hidden_ref, ids_ref, res_ref, slots_ref, pick = refs
    experts, slots, width = slots_ref.shape
    tokens = hidden_ref.shape[0]
    half = tokens // 2
    groups = [[p for p, (i, _) in zip(recvs, ways) if i == group] for group in (0, 1)]
    for rows, parts in ((slice(0, half), groups[0]), (slice(half, tokens), groups[1])):
        part = hidden_ref[rows].astype(f32)
        for p in parts:
            part = part + p[...].astype(f32)
        res_ref[rows] = part
    total = res_ref[...]
    expert = lax.broadcasted_iota(jnp.int32, (experts, tokens), 0)
    chosen = jnp.zeros((experts, tokens), f32)
    for k in range(ids_ref.shape[0]):
        chosen = jnp.where(ids_ref[k : k + 1, :] == expert, 1.0, chosen)
    row = lax.broadcasted_iota(jnp.int32, (tokens, tokens), 0)
    col = lax.broadcasted_iota(jnp.int32, (tokens, tokens), 1)
    earlier = jnp.where(row < col, 1.0, 0.0).astype(bf16)
    place = jnp.dot(chosen.astype(bf16), earlier, preferred_element_type=f32)
    place = jnp.where(chosen > 0.5, place, -1.0)
    slot = lax.broadcasted_iota(jnp.int32, (slots, tokens), 0).astype(f32)
    for e in range(experts):
        pick[e * slots : (e + 1) * slots] = jnp.where(place[e : e + 1] == slot, 1.0, 0.0).astype(bf16)
    rows = jnp.dot(pick[...], total.astype(bf16), preferred_element_type=f32).astype(bf16)
    slots_ref[...] = rows.reshape(experts, slots, width)


def normalize(recv_ref, gain_ref, out_ref):
    blocks, slots, width = recv_ref.shape
    square = jnp.zeros((slots, width), f32)
    for i in range(blocks):
        part = recv_ref[i].astype(f32)
        square = square + part * part
    mean = jnp.sum(square, axis=1, keepdims=True) / (blocks * width)
    scale = lax.rsqrt(mean + epsilon)
    for i in range(blocks):
        lanes = slice(i * width, (i + 1) * width)
        out_ref[:, lanes] = (recv_ref[i].astype(f32) * scale * gain_ref[:, lanes]).astype(bf16)


def load_weights(after_ref, *refs):
    count = (len(refs) - 2) // 2
    sources, targets, turn_out, sem = refs[:count], refs[count : 2 * count], refs[-2], refs[-1]
    copies = [pltpu.make_async_copy(s, t, sem.at[i]) for i, (s, t) in enumerate(zip(sources, targets))]
    for c in copies:
        c.start()
    turn_out[...] = after_ref[: turn_out.shape[0], : turn_out.shape[1]].astype(f32)
    for c in copies:
        c.wait()


def feed_forward(*refs, groups, cut):
    count = sum(sum(g) for g in groups)
    pieces, (w_gate, w_up, w_down, turn_ref) = refs[:count], refs[count : count + 4]
    *outs, turn_out, x, act = refs[count + 4 :]
    at = 0
    for p in pieces:
        x[at : at + p.shape[0]] = p[...]
        at += p.shape[0]
    blocks, rows, width = outs[0].shape
    size_out = blocks // cut
    wide = 2 * LANES
    hidden = w_gate.shape[1]
    for i in range(0, hidden, wide):
        size = min(wide, hidden - i)
        lanes = slice(i, i + size)
        both = jnp.concatenate([w_gate[:, lanes], w_up[:, lanes]], axis=1)
        part = jnp.dot(x[...], both, preferred_element_type=f32)
        g, u = part[:, :size], part[:, size:]
        act[:, lanes] = (g / (1.0 + jnp.exp(-g)) * u).astype(bf16)
    for i in range(blocks):
        part = jnp.dot(act[...], w_down[:, i * width : (i + 1) * width], preferred_element_type=f32)
        part = part.astype(bf16)
        for j in range(len(groups)):
            own, *others = outs[j * (cut + 1) : (j + 1) * (cut + 1)]
            own[i] = part[2 * j * rows : (2 * j + 1) * rows]
            others[i // size_out][i % size_out] = part[(2 * j + 1) * rows : (2 * j + 2) * rows]
    turn_out[...] = turn_ref[...]


def add_up(*refs, pieces):
    *parts, out_ref = refs
    for i in range(out_ref.shape[0]):
        total, at = None, 0
        for n in pieces:
            size = out_ref.shape[0] // n
            term = parts[at + i // size][i % size].astype(f32)
            total = term if total is None else total + term
            at += n
        out_ref[i] = total.astype(out_ref.dtype)


def combine(recv_ref, ids_ref, weight_ref, res_ref, out_ref):
    experts, slots, width = recv_ref.shape
    tokens, top = ids_ref.shape
    rows = recv_ref[...].reshape(experts * slots, width)
    expert = lax.broadcasted_iota(jnp.int32, (tokens, experts), 1)
    named = [ids_ref[:, k : k + 1] == expert for k in range(top)]
    chosen = jnp.zeros((tokens, experts), f32)
    for k in range(top):
        chosen = jnp.where(named[k], 1.0, chosen)
    row = lax.broadcasted_iota(jnp.int32, (tokens, tokens), 0)
    col = lax.broadcasted_iota(jnp.int32, (tokens, tokens), 1)
    earlier = jnp.where(col < row, 1.0, 0.0).astype(bf16)
    place = jnp.dot(earlier, chosen.astype(bf16), preferred_element_type=f32)
    place = place + (expert * slots).astype(f32)
    slot = lax.broadcasted_iota(jnp.int32, (tokens, experts * slots), 1)
    total = res_ref[...]
    for k in range(top):
        at = jnp.sum(jnp.where(named[k], place, 0.0), axis=1, keepdims=True).astype(jnp.int32)
        pick = jnp.where(slot == at, 1.0, 0.0).astype(bf16)
        total = total + weight_ref[:, k : k + 1] * jnp.dot(pick, rows, preferred_element_type=f32)
    out_ref[...] = total.astype(out_ref.dtype)


def scan_tables(table, turns):
    return table.reshape(SUBS, turns, -1).transpose(1, 0, 2)


def run_first(step, sig, into, rate, prompts):
    tokens, channels = step.shape
    states = rate.shape[0]
    turns = into.shape[0]
    tiles = channels // LANES
    return pl.pallas_call(
        first_pass,
        out_shape=(
            jax.ShapeDtypeStruct((prompts, states + 1, channels), f32),
            jax.ShapeDtypeStruct((prompts, states, SUBS, channels), f32),
            jax.ShapeDtypeStruct((prompts, SUBS, channels), f32),
        ),
        in_specs=[vmem()] * 4,
        out_specs=(vmem(),) * 3,
        scratch_shapes=[
            pltpu.VMEM((tiles, tokens, LANES), f32),
            pltpu.VMEM((tiles, tokens, LANES), f32),
            pltpu.VMEM((turns, prompts * states, SUBS, LANES), f32),
        ],
        compiler_params=params(24),
        name="scan_first",
    )(step, sig, into, rate)


def run_pair(core, own, sib, rate):
    return pl.pallas_call(
        pair_up,
        out_shape=jax.ShapeDtypeStruct(own.shape, f32),
        in_specs=[smem()] + [vmem()] * 3,
        out_specs=vmem(),
        compiler_params=params(8),
        name="pair_up",
    )(core, own, sib, rate)


def run_second(core, step, sig, gate, into, outof, rate, skip, before, pre, sib, pairs):
    tokens, channels = step.shape
    prompts, states = before.shape[:2]
    turns = into.shape[0]
    tiles = channels // LANES
    return pl.pallas_call(
        functools.partial(second_pass, earlier=len(pairs)),
        out_shape=jax.ShapeDtypeStruct((tokens, channels), bf16),
        in_specs=[smem()] + [vmem()] * (10 + len(pairs)),
        out_specs=vmem(),
        scratch_shapes=[
            pltpu.VMEM((tiles, tokens, LANES), f32),
            pltpu.VMEM((tiles, tokens, LANES), f32),
            pltpu.VMEM((tiles, tokens, LANES), f32),
            pltpu.VMEM((turns, prompts * states, SUBS, LANES), f32),
            pltpu.VMEM((turns, prompts * states, SUBS, LANES), f32),
            pltpu.VMEM((states, LANES), f32),
        ],
        compiler_params=params(16),
        cost_estimate=pl.CostEstimate(flops=2 * 10**9, bytes_accessed=2 * MIB, transcendentals=0),
        name="scan_second",
    )(core, step, sig, gate, into, outof, rate, skip, before, pre, sib, *pairs)


def run_project(coords, mixed, ids, proj, share, sides):
    tokens = mixed.shape[0]
    nx, nz = sides
    blocks = proj.shape[0] * proj.shape[2] // share
    return pl.pallas_call(
        functools.partial(project, sides=sides),
        out_shape=[jax.ShapeDtypeStruct((nx, tokens // 2, share), bf16)] * nz
        + [jax.ShapeDtypeStruct((nz, tokens // 2, share), bf16)] * nx
        + [jax.ShapeDtypeStruct(ids.shape, ids.dtype)],
        in_specs=[smem(), vmem(), vmem(), anywhere()],
        out_specs=[vmem()] * (nx + nz + 1),
        scratch_shapes=[
            pltpu.VMEM((blocks, tokens, share), bf16),
            pltpu.VMEM(proj.shape, bf16),
            pltpu.SemaphoreType.DMA((proj.shape[0],)),
        ],
        compiler_params=params(16),
        name="project",
    )(coords, mixed, ids, pltpu.with_memory_space_constraint(proj, pltpu.HBM))


def run_fold(coords, parts, sides, ways):
    nx, nz = sides
    _, half, share = parts[0].shape
    return pl.pallas_call(
        functools.partial(fold, sides=sides, ways=ways),
        out_shape=[jax.ShapeDtypeStruct((half, share), bf16)] * (nx + nz),
        in_specs=[smem()] + [vmem()] * (nx + nz),
        out_specs=[vmem()] * (nx + nz),
        compiler_params=params(8),
        name="fold",
    )(coords, *parts)


def run_dispatch(recvs, hidden, ids, experts, slots, ways):
    tokens, share = hidden.shape
    return pl.pallas_call(
        functools.partial(dispatch, ways=ways),
        out_shape=(
            jax.ShapeDtypeStruct((tokens, share), f32),
            jax.ShapeDtypeStruct((experts, slots, share), bf16),
        ),
        in_specs=[vmem()] * (len(recvs) + 2),
        out_specs=(vmem(),) * 2,
        scratch_shapes=[pltpu.VMEM((experts * slots, tokens), bf16)],
        compiler_params=params(8),
        name="dispatch",
    )(*recvs, hidden, ids)


def run_normalize(recv, gain):
    blocks, slots, width = recv.shape
    return pl.pallas_call(
        normalize,
        out_shape=jax.ShapeDtypeStruct((slots, blocks * width), bf16),
        in_specs=[vmem()] * 2,
        out_specs=vmem(),
        compiler_params=params(8),
        name="normalize",
    )(recv, gain)


def run_load(after, *weights):
    return pl.pallas_call(
        load_weights,
        out_shape=[pltpu.VMEM(w.shape, w.dtype) for w in weights] + [jax.ShapeDtypeStruct((8, LANES), f32)],
        in_specs=[vmem()] + [pl.BlockSpec(memory_space=pltpu.HBM)] * len(weights),
        out_specs=[vmem()] * (len(weights) + 1),
        scratch_shapes=[pltpu.SemaphoreType.DMA((len(weights),))],
        compiler_params=params(8),
        cost_estimate=pl.CostEstimate(flops=0, bytes_accessed=2 * sum(w.nbytes for w in weights), transcendentals=0),
        name="load_weights",
    )(after, *[pltpu.with_memory_space_constraint(w, pltpu.HBM) for w in weights])


def run_ffn(groups, weights, turn, share, cut=1):
    pieces = [p for own, other in groups for p in (*own, *other)]
    rows = sum(p.shape[0] for p in groups[0][0])
    depth, hidden = weights[0].shape
    total = 2 * rows * len(groups)
    part = jax.ShapeDtypeStruct((depth // share, rows, share), bf16)
    piece = jax.ShapeDtypeStruct((depth // share // cut, rows, share), bf16)
    weights = [pltpu.with_memory_space_constraint(w, pltpu.VMEM) for w in weights]
    return pl.pallas_call(
        functools.partial(feed_forward, groups=tuple((len(own), len(other)) for own, other in groups), cut=cut),
        out_shape=(part, *(piece,) * cut) * len(groups) + (jax.ShapeDtypeStruct(turn.shape, turn.dtype),),
        in_specs=[vmem()] * (len(pieces) + 4),
        out_specs=(vmem(),) * ((cut + 1) * len(groups) + 1),
        scratch_shapes=[pltpu.VMEM((total, depth), bf16), pltpu.VMEM((total, hidden), bf16)],
        compiler_params=params(12),
        cost_estimate=pl.CostEstimate(
            flops=6 * total * depth * hidden, bytes_accessed=4 * total * depth, transcendentals=0
        ),
        name="feed_forward",
    )(*pieces, *weights, turn)


def run_add(*parts, dtype=bf16, bytes_accessed=MIB):
    parts = [p if isinstance(p, list) else [p] for p in parts]
    flat = [piece for p in parts for piece in p]
    return pl.pallas_call(
        functools.partial(add_up, pieces=tuple(len(p) for p in parts)),
        out_shape=jax.ShapeDtypeStruct((sum(p.shape[0] for p in parts[0]), *flat[0].shape[1:]), dtype),
        in_specs=[vmem()] * len(flat),
        out_specs=vmem(),
        compiler_params=params(8),
        cost_estimate=pl.CostEstimate(flops=0, bytes_accessed=bytes_accessed, transcendentals=0),
        name="add_up",
    )(*flat)


def run_combine(recv, ids, weights, res):
    return pl.pallas_call(
        combine,
        out_shape=jax.ShapeDtypeStruct(res.shape, bf16),
        in_specs=[vmem()] * 4,
        out_specs=vmem(),
        compiler_params=params(16),
        name="combine",
    )(recv, ids, weights, res)


def on_device(
    mixer_input, gate_in, step_size, decay_rate, state_in, state_out, skip, out_proj, hidden_in, norm_gain,
    w_gate, w_up, w_down, route_ids, route_weight,
):
    slab_len, prompts, channels = mixer_input.shape
    tokens = slab_len * prompts
    share = hidden_in.shape[2]
    chips = lax.axis_size("y")
    ctx, exp = ("y", "core"), ("x", "z")
    experts = lax.axis_size(exp) * w_gate.shape[0]
    slots = 4 * tokens // experts
    turns = slab_len // SUBS

    def swap(value):
        return lax.ppermute(value, "core", [(0, 1), (1, 0)])

    def ring(value, d):
        return lax.ppermute(value, "y", [(i, (i + d) % chips) for i in range(chips)])

    proj = lax.all_gather(out_proj, ctx)
    sig = mixer_input.reshape(tokens, channels)
    step = step_size.reshape(tokens, channels)
    into = scan_tables(state_in, turns)
    end, before, pre = run_first(step, sig, into, decay_rate, prompts)
    coords = jnp.stack([lax.axis_index(a).astype(jnp.int32) for a in ("core", "x", "z")])
    sib = swap(end)
    pair = run_pair(coords, end, sib, decay_rate)
    gate_in, state_out, pair = lax.optimization_barrier((gate_in, state_out, pair))
    pairs = [
        lax.ppermute(pair, "y", [(i, i + d) for i in range(chips - d)]) for d in range(chips - 1, 0, -1)
    ]
    gate = gate_in.reshape(tokens, channels)
    outof = scan_tables(state_out, turns)
    mixed = run_second(
        coords, step, sig, gate, into, outof, decay_rate, skip.reshape(1, channels), before, pre, sib, pairs
    )
    sides = (lax.axis_size("x"), lax.axis_size("z"))

    def shift(value, axis, d):
        n = lax.axis_size(axis)
        return lax.ppermute(value, axis, [(i, (i + d) % n) for i in range(n)]) if d else value

    def spread_out(one, one_axis, two, two_axis):
        sides = ((one, one_axis), (two, two_axis))
        ways = [(i, d) for i, (parts, _) in enumerate(sides) for d in range(len(parts))]
        hops = {(i, d): min(d, len(sides[i][0]) - d) for i, d in ways}
        lead = (0, 1)
        ways = sorted(ways, key=lambda w: (w != lead, -hops[w], w[1], w[0]))
        return [shift(sides[i][0][d], sides[i][1], d) for i, d in ways], tuple(ways)

    nx, nz = sides
    ids = route_ids.reshape(tokens, -1)
    *parts, by_choice = run_project(coords, mixed, ids.T, proj, share, sides)
    hidden = hidden_in.reshape(tokens, share)
    parts, ways = spread_out(parts[:nz], "z", parts[nz:], "x")
    parts = run_fold(coords, parts, sides, ways)
    parts, ways = spread_out(parts[:nx], "x", parts[nx:], "z")
    residual, slot_rows = run_dispatch(parts, hidden, by_choice, experts, slots, ways)
    whole = lax.all_to_all(slot_rows, exp, 0, 0, tiled=True)
    own = run_normalize(whole, norm_gain.reshape(1, -1))

    half = slots // 2
    own_sib = swap(own)
    low = ring(own, 1)
    high = ring(own, -1)
    *weights, turn = run_load(own, w_gate[0], w_up[0], w_down[0])
    own_sib, turn = lax.optimization_barrier((own_sib, turn))
    mine0, other0, turn = run_ffn([([own], [own_sib])], weights, turn, share)
    low, high, turn = lax.optimization_barrier((low, high, turn))
    from0 = swap(other0)
    far_low, far_high = ring(low[:half], 1), ring(high[half:], -1)
    low_sib, high_sib = swap(low), swap(high)
    low_sib, from0 = lax.optimization_barrier((low_sib, from0))
    mine1, other1, mine3, other3, turn = run_ffn([([low], [low_sib]), ([high], [high_sib])], weights, turn, share)
    far_low, far_high, turn, other1, other3 = lax.optimization_barrier((far_low, far_high, turn, other1, other3))
    far_low_sib, far_high_sib = swap(far_low), swap(far_high)
    low_sum, high_sum = run_add(mine1, swap(other1)), run_add(mine3, swap(other3))
    low_sum, high_sum, turn = lax.optimization_barrier((low_sum, high_sum, turn))
    back1, back3 = ring(low_sum, -1), ring(high_sum, 1)
    mine2, *other2, turn = run_ffn(
        [([far_low, far_high], [far_low_sib, far_high_sib])], weights, turn, share, cut=CUT
    )
    back2 = ring(run_add(mine2, [swap(p) for p in other2]), 2)
    near = run_add(mine0, from0, back1, back3, dtype=f32, bytes_accessed=64 * MIB)
    returned = run_add(near, back2)

    back = lax.all_to_all(returned, exp, 0, 0, tiled=True)
    out = run_combine(back, ids, route_weight.reshape(tokens, -1), residual)
    return out.reshape(slab_len, prompts, share)


def solution(mesh):
    ctx, exp = ("y", "core"), ("x", "z")
    n_ctx, n_exp = mesh.devices.shape
    side = int(round(n_exp**0.5))
    mesh = Mesh(mesh.devices.reshape(n_ctx // 2, 2, side, n_exp // side), ctx + exp)
    placed = (
        P(ctx, None, exp),
        P(ctx, None, exp),
        P(ctx, None, exp),
        P(None, exp),
        P(ctx, None, None),
        P(ctx, None, None),
        P(exp),
        P(exp, ctx),
        P(ctx, None, exp),
        P(),
        P(exp, None, ctx),
        P(exp, None, ctx),
        P(exp, ctx, None),
        P(ctx, None, None),
        P(ctx, None, None),
    )
    return jax.shard_map(on_device, mesh=mesh, in_specs=placed, out_specs=P(ctx, None, exp), check_vma=False)
```

```python
import functools

import jax
import jax.numpy as jnp
from jax import lax
from jax.experimental import pallas as pl
from jax.experimental.pallas import tpu as pltpu
from jax.sharding import Mesh
from jax.sharding import PartitionSpec as P

epsilon = 1e-06
LOG2E = 1.4426950408889634
SUBS = 8
LANES = 128
UNROLL = 16
MIB = 1 << 20
f32, bf16 = jnp.float32, jnp.bfloat16


def params(mib):
    return pltpu.CompilerParams(vmem_limit_bytes=mib * MIB)


def vmem():
    return pl.BlockSpec(memory_space=pltpu.VMEM)


def smem():
    return pl.BlockSpec(memory_space=pltpu.SMEM)


def anywhere():
    return pl.BlockSpec(memory_space=pl.ANY)


def spread(table_ref, out_ref):
    turns, _, columns = table_ref.shape

    def turn(t, _):
        row = table_ref[t]
        for i in range(columns):
            out_ref[t, i] = jnp.broadcast_to(row[:, i : i + 1], (SUBS, LANES))
        return 0

    lax.fori_loop(0, turns, turn, 0)


def split_lanes(step_ref, sig_ref, st4, v4):
    for q in range(st4.shape[0]):
        lanes = slice(q * LANES, (q + 1) * LANES)
        st = step_ref[:, lanes]
        st4[q] = st
        v4[q] = st * sig_ref[:, lanes].astype(f32)


def first_pass(step_ref, sig_ref, into_ref, rate_ref, fin_ref, before_ref, pre_ref, st4, v4, into_b):
    states, channels = rate_ref.shape
    prompts = fin_ref.shape[0]
    turns = into_ref.shape[0]
    hop = turns * prompts
    spread(into_ref, into_b)
    split_lanes(step_ref, sig_ref, st4, v4)
    sub = lax.broadcasted_iota(jnp.int32, (SUBS, LANES), 0)
    for q in range(channels // LANES):
        lanes = slice(q * LANES, (q + 1) * LANES)
        rates = [
            jnp.broadcast_to(rate_ref[n : n + 1, lanes] * -LOG2E, (SUBS, LANES)) for n in range(states)
        ]
        for b in range(prompts):

            def turn(t, held, q=q, b=b, rates=rates):
                total, hs = held
                st = st4[q, pl.ds(t * prompts + b, SUBS, stride=hop), :]
                v = v4[q, pl.ds(t * prompts + b, SUBS, stride=hop), :]
                new = []
                for n in range(states):
                    new.append(jnp.exp2(st * rates[n]) * hs[n] + v * into_b[t, b * states + n])
                return total + st, tuple(new)

            zero = jnp.zeros((SUBS, LANES), f32)
            width, hs = lax.fori_loop(0, turns, turn, (zero, (zero,) * states))
            hs = list(hs)
            for d in (1, 2, 4):
                live = sub >= d
                for n in range(states):
                    moved = jnp.where(live, pltpu.roll(hs[n], d, 0), 0.0)
                    hs[n] = hs[n] + jnp.exp2(rates[n] * width) * moved
                width = width + jnp.where(live, pltpu.roll(width, d, 0), 0.0)
            for n in range(states):
                fin_ref[b, n : n + 1, lanes] = hs[n][SUBS - 1 :]
                before_ref[b, n, :, lanes] = jnp.where(sub >= 1, pltpu.roll(hs[n], 1, 0), 0.0)
            fin_ref[b, states : states + 1, lanes] = width[SUBS - 1 :]
            pre_ref[b, :, lanes] = jnp.where(sub >= 1, pltpu.roll(width, 1, 0), 0.0)


def pair_up(core_ref, own_ref, sib_ref, rate_ref, out_ref):
    states = rate_ref.shape[0]
    low = core_ref[0] == 0
    rate = rate_ref[...] * -LOG2E
    for b in range(own_ref.shape[0]):
        first = jnp.where(low, own_ref[b], sib_ref[b])
        second = jnp.where(low, sib_ref[b], own_ref[b])
        decay = jnp.exp2(rate * second[states:])
        out_ref[b, :states] = decay * first[:states] + second[:states]
        out_ref[b, states:] = first[states:] + second[states:]


def second_pass(
    core_ref, step_ref, sig_ref, gate_ref, into_ref, outof_ref, rate_ref, skip_ref, before_ref, pre_ref,
    *rest, earlier,
):
    sib_ref, *pair_refs = rest[: earlier + 1]
    mixed_ref, st4, v4, y4, into_b, outof_b, enter = rest[earlier + 1 :]
    states, channels = rate_ref.shape
    prompts = pre_ref.shape[0]
    turns = into_ref.shape[0]
    hop = turns * prompts
    spread(into_ref, into_b)
    spread(outof_ref, outof_b)
    split_lanes(step_ref, sig_ref, st4, v4)
    live = jnp.where(core_ref[0] > 0, 1.0, 0.0).astype(f32)
    for q in range(channels // LANES):
        lanes = slice(q * LANES, (q + 1) * LANES)
        rate_q = rate_ref[:, lanes] * -LOG2E
        rates = [jnp.broadcast_to(rate_q[n : n + 1], (SUBS, LANES)) for n in range(states)]
        for b in range(prompts):
            h0 = jnp.zeros((states, LANES), f32)
            for pair in pair_refs:
                h0 = jnp.exp2(rate_q * pair[b, states : states + 1, lanes]) * h0 + pair[b, :states, lanes]
            decay = jnp.exp2(rate_q * (sib_ref[b, states : states + 1, lanes] * live))
            enter[...] = decay * h0 + sib_ref[b, :states, lanes] * live
            pre = pre_ref[b, :, lanes]
            hs = tuple(
                before_ref[b, n, :, lanes]
                + jnp.exp2(rates[n] * pre) * jnp.broadcast_to(enter[n : n + 1], (SUBS, LANES))
                for n in range(states)
            )

            def turn(t, hs, q=q, b=b, rates=rates):
                rows = pl.ds(t * prompts + b, SUBS, stride=hop)
                st = st4[q, rows, :]
                v = v4[q, rows, :]
                new, sums = [], [None] * 4
                for n in range(states):
                    h = jnp.exp2(st * rates[n]) * hs[n] + v * into_b[t, b * states + n]
                    new.append(h)
                    term = h * outof_b[t, b * states + n]
                    sums[n % 4] = term if sums[n % 4] is None else sums[n % 4] + term
                y4[q, rows, :] = (sums[0] + sums[1]) + (sums[2] + sums[3])
                return tuple(new)

            lax.fori_loop(0, turns, turn, hs, unroll=UNROLL)
        sig = sig_ref[:, lanes].astype(f32)
        gate = gate_ref[:, lanes].astype(f32)
        y = y4[q] + skip_ref[:, lanes] * sig
        mixed_ref[:, lanes] = (y * (gate / (1.0 + jnp.exp(-gate)))).astype(bf16)


def project(coords_ref, mixed_ref, ids_ref, proj_hbm, *rest, sides):
    nx, nz = sides
    z_refs, x_refs = rest[:nz], rest[nz : nz + nx]
    ids_out, whole, proj, sem = rest[nz + nx :]
    _, half, width = z_refs[0].shape
    blocks, _, columns = proj.shape
    for c in range(blocks):
        pltpu.make_async_copy(proj_hbm.at[c], proj.at[c], sem.at[c]).start()
    for c in range(blocks):
        pltpu.make_async_copy(proj_hbm.at[c], proj.at[c], sem.at[c]).wait()
        part = jnp.dot(mixed_ref[...], proj[c], preferred_element_type=f32).astype(bf16)
        for i in range(columns // width):
            whole[c * (columns // width) + i] = part[:, i * width : (i + 1) * width]
    x, z = coords_ref[1], coords_ref[2]
    for d, out in enumerate(z_refs):
        for i in range(nx):
            out[i] = whole[i * nz + lax.rem(z + d, nz), :half]
    for d, out in enumerate(x_refs):
        for i in range(nz):
            out[i] = whole[lax.rem(x + d, nx) * nz + i, half:]
    ids_out[...] = ids_ref[...]


def fold(coords_ref, *rest, sides, ways):
    nx, nz = sides
    parts, outs = rest[: len(ways)], rest[len(ways) :]
    groups = [[p for p, (i, _) in zip(parts, ways) if i == group] for group in (0, 1)]
    x, z = coords_ref[1], coords_ref[2]
    for parts, outs, at, count in ((groups[0], outs[:nx], x, nx), (groups[1], outs[nx:], z, nz)):
        for d, out in enumerate(outs):
            block = lax.rem(at + d, count)
            total = parts[0][block].astype(f32)
            for p in parts[1:]:
                total = total + p[block].astype(f32)
            out[...] = total.astype(bf16)


def dispatch(*refs, ways):
    *recvs, hidden_ref, ids_ref, res_ref, slots_ref, pick = refs
    experts, slots, width = slots_ref.shape
    tokens = hidden_ref.shape[0]
    half = tokens // 2
    groups = [[p for p, (i, _) in zip(recvs, ways) if i == group] for group in (0, 1)]
    for rows, parts in ((slice(0, half), groups[0]), (slice(half, tokens), groups[1])):
        part = hidden_ref[rows].astype(f32)
        for p in parts:
            part = part + p[...].astype(f32)
        res_ref[rows] = part
    total = res_ref[...]
    expert = lax.broadcasted_iota(jnp.int32, (experts, tokens), 0)
    chosen = jnp.zeros((experts, tokens), f32)
    for k in range(ids_ref.shape[0]):
        chosen = jnp.where(ids_ref[k : k + 1, :] == expert, 1.0, chosen)
    row = lax.broadcasted_iota(jnp.int32, (tokens, tokens), 0)
    col = lax.broadcasted_iota(jnp.int32, (tokens, tokens), 1)
    earlier = jnp.where(row < col, 1.0, 0.0).astype(bf16)
    place = jnp.dot(chosen.astype(bf16), earlier, preferred_element_type=f32)
    place = jnp.where(chosen > 0.5, place, -1.0)
    slot = lax.broadcasted_iota(jnp.int32, (slots, tokens), 0).astype(f32)
    for e in range(experts):
        pick[e * slots : (e + 1) * slots] = jnp.where(place[e : e + 1] == slot, 1.0, 0.0).astype(bf16)
    rows = jnp.dot(pick[...], total.astype(bf16), preferred_element_type=f32).astype(bf16)
    slots_ref[...] = rows.reshape(experts, slots, width)


def normalize(recv_ref, gain_ref, out_ref):
    blocks, slots, width = recv_ref.shape
    square = jnp.zeros((slots, width), f32)
    for i in range(blocks):
        part = recv_ref[i].astype(f32)
        square = square + part * part
    mean = jnp.sum(square, axis=1, keepdims=True) / (blocks * width)
    scale = lax.rsqrt(mean + epsilon)
    for i in range(blocks):
        lanes = slice(i * width, (i + 1) * width)
        out_ref[:, lanes] = (recv_ref[i].astype(f32) * scale * gain_ref[:, lanes]).astype(bf16)


def load_weights(after_ref, *refs):
    count = (len(refs) - 2) // 2
    sources, targets, turn_out, sem = refs[:count], refs[count : 2 * count], refs[-2], refs[-1]
    copies = [pltpu.make_async_copy(s, t, sem.at[i]) for i, (s, t) in enumerate(zip(sources, targets))]
    for c in copies:
        c.start()
    turn_out[...] = after_ref[: turn_out.shape[0], : turn_out.shape[1]].astype(f32)
    for c in copies:
        c.wait()


def feed_forward(*refs, groups, cut):
    count = sum(sum(g) for g in groups)
    pieces, (w_gate, w_up, w_down, turn_ref) = refs[:count], refs[count : count + 4]
    *outs, turn_out, x, act = refs[count + 4 :]
    at = 0
    for p in pieces:
        x[at : at + p.shape[0]] = p[...]
        at += p.shape[0]
    blocks, rows, width = outs[0].shape
    size_out = blocks // cut
    wide = 2 * LANES
    hidden = w_gate.shape[1]
    for i in range(0, hidden, wide):
        size = min(wide, hidden - i)
        lanes = slice(i, i + size)
        both = jnp.concatenate([w_gate[:, lanes], w_up[:, lanes]], axis=1)
        part = jnp.dot(x[...], both, preferred_element_type=f32)
        g, u = part[:, :size], part[:, size:]
        act[:, lanes] = (g / (1.0 + jnp.exp(-g)) * u).astype(bf16)
    for i in range(blocks):
        part = jnp.dot(act[...], w_down[:, i * width : (i + 1) * width], preferred_element_type=f32)
        part = part.astype(bf16)
        for j in range(len(groups)):
            own, *others = outs[j * (cut + 1) : (j + 1) * (cut + 1)]
            own[i] = part[2 * j * rows : (2 * j + 1) * rows]
            others[i // size_out][i % size_out] = part[(2 * j + 1) * rows : (2 * j + 2) * rows]
    turn_out[...] = turn_ref[...]


def add_up(*refs, pieces):
    *parts, out_ref = refs
    for i in range(out_ref.shape[0]):
        total, at = None, 0
        for n in pieces:
            size = out_ref.shape[0] // n
            term = parts[at + i // size][i % size].astype(f32)
            total = term if total is None else total + term
            at += n
        out_ref[i] = total.astype(out_ref.dtype)


def combine(recv_ref, ids_ref, weight_ref, res_ref, out_ref):
    experts, slots, width = recv_ref.shape
    tokens, top = ids_ref.shape
    rows = recv_ref[...].reshape(experts * slots, width)
    expert = lax.broadcasted_iota(jnp.int32, (tokens, experts), 1)
    named = [ids_ref[:, k : k + 1] == expert for k in range(top)]
    chosen = jnp.zeros((tokens, experts), f32)
    for k in range(top):
        chosen = jnp.where(named[k], 1.0, chosen)
    row = lax.broadcasted_iota(jnp.int32, (tokens, tokens), 0)
    col = lax.broadcasted_iota(jnp.int32, (tokens, tokens), 1)
    earlier = jnp.where(col < row, 1.0, 0.0).astype(bf16)
    place = jnp.dot(earlier, chosen.astype(bf16), preferred_element_type=f32)
    place = place + (expert * slots).astype(f32)
    slot = lax.broadcasted_iota(jnp.int32, (tokens, experts * slots), 1)
    total = res_ref[...]
    for k in range(top):
        at = jnp.sum(jnp.where(named[k], place, 0.0), axis=1, keepdims=True).astype(jnp.int32)
        pick = jnp.where(slot == at, 1.0, 0.0).astype(bf16)
        total = total + weight_ref[:, k : k + 1] * jnp.dot(pick, rows, preferred_element_type=f32)
    out_ref[...] = total.astype(out_ref.dtype)


def scan_tables(table, turns):
    return table.reshape(SUBS, turns, -1).transpose(1, 0, 2)


def run_first(step, sig, into, rate, prompts):
    tokens, channels = step.shape
    states = rate.shape[0]
    turns = into.shape[0]
    tiles = channels // LANES
    return pl.pallas_call(
        first_pass,
        out_shape=(
            jax.ShapeDtypeStruct((prompts, states + 1, channels), f32),
            jax.ShapeDtypeStruct((prompts, states, SUBS, channels), f32),
            jax.ShapeDtypeStruct((prompts, SUBS, channels), f32),
        ),
        in_specs=[vmem()] * 4,
        out_specs=(vmem(),) * 3,
        scratch_shapes=[
            pltpu.VMEM((tiles, tokens, LANES), f32),
            pltpu.VMEM((tiles, tokens, LANES), f32),
            pltpu.VMEM((turns, prompts * states, SUBS, LANES), f32),
        ],
        compiler_params=params(24),
        name="scan_first",
    )(step, sig, into, rate)


def run_pair(core, own, sib, rate):
    return pl.pallas_call(
        pair_up,
        out_shape=jax.ShapeDtypeStruct(own.shape, f32),
        in_specs=[smem()] + [vmem()] * 3,
        out_specs=vmem(),
        compiler_params=params(8),
        name="pair_up",
    )(core, own, sib, rate)


def run_second(core, step, sig, gate, into, outof, rate, skip, before, pre, sib, pairs):
    tokens, channels = step.shape
    prompts, states = before.shape[:2]
    turns = into.shape[0]
    tiles = channels // LANES
    return pl.pallas_call(
        functools.partial(second_pass, earlier=len(pairs)),
        out_shape=jax.ShapeDtypeStruct((tokens, channels), bf16),
        in_specs=[smem()] + [vmem()] * (10 + len(pairs)),
        out_specs=vmem(),
        scratch_shapes=[
            pltpu.VMEM((tiles, tokens, LANES), f32),
            pltpu.VMEM((tiles, tokens, LANES), f32),
            pltpu.VMEM((tiles, tokens, LANES), f32),
            pltpu.VMEM((turns, prompts * states, SUBS, LANES), f32),
            pltpu.VMEM((turns, prompts * states, SUBS, LANES), f32),
            pltpu.VMEM((states, LANES), f32),
        ],
        compiler_params=params(16),
        cost_estimate=pl.CostEstimate(flops=2 * 10**9, bytes_accessed=2 * MIB, transcendentals=0),
        name="scan_second",
    )(core, step, sig, gate, into, outof, rate, skip, before, pre, sib, *pairs)


def run_project(coords, mixed, ids, proj, share, sides):
    tokens = mixed.shape[0]
    nx, nz = sides
    blocks = proj.shape[0] * proj.shape[2] // share
    return pl.pallas_call(
        functools.partial(project, sides=sides),
        out_shape=[jax.ShapeDtypeStruct((nx, tokens // 2, share), bf16)] * nz
        + [jax.ShapeDtypeStruct((nz, tokens // 2, share), bf16)] * nx
        + [jax.ShapeDtypeStruct(ids.shape, ids.dtype)],
        in_specs=[smem(), vmem(), vmem(), anywhere()],
        out_specs=[vmem()] * (nx + nz + 1),
        scratch_shapes=[
            pltpu.VMEM((blocks, tokens, share), bf16),
            pltpu.VMEM(proj.shape, bf16),
            pltpu.SemaphoreType.DMA((proj.shape[0],)),
        ],
        compiler_params=params(16),
        name="project",
    )(coords, mixed, ids, pltpu.with_memory_space_constraint(proj, pltpu.HBM))


def run_fold(coords, parts, sides, ways):
    nx, nz = sides
    _, half, share = parts[0].shape
    return pl.pallas_call(
        functools.partial(fold, sides=sides, ways=ways),
        out_shape=[jax.ShapeDtypeStruct((half, share), bf16)] * (nx + nz),
        in_specs=[smem()] + [vmem()] * (nx + nz),
        out_specs=[vmem()] * (nx + nz),
        compiler_params=params(8),
        name="fold",
    )(coords, *parts)


def run_dispatch(recvs, hidden, ids, experts, slots, ways):
    tokens, share = hidden.shape
    return pl.pallas_call(
        functools.partial(dispatch, ways=ways),
        out_shape=(
            jax.ShapeDtypeStruct((tokens, share), f32),
            jax.ShapeDtypeStruct((experts, slots, share), bf16),
        ),
        in_specs=[vmem()] * (len(recvs) + 2),
        out_specs=(vmem(),) * 2,
        scratch_shapes=[pltpu.VMEM((experts * slots, tokens), bf16)],
        compiler_params=params(8),
        name="dispatch",
    )(*recvs, hidden, ids)


def run_normalize(recv, gain):
    blocks, slots, width = recv.shape
    return pl.pallas_call(
        normalize,
        out_shape=jax.ShapeDtypeStruct((slots, blocks * width), bf16),
        in_specs=[vmem()] * 2,
        out_specs=vmem(),
        compiler_params=params(8),
        name="normalize",
    )(recv, gain)


def run_load(after, *weights):
    return pl.pallas_call(
        load_weights,
        out_shape=[pltpu.VMEM(w.shape, w.dtype) for w in weights] + [jax.ShapeDtypeStruct((8, LANES), f32)],
        in_specs=[vmem()] + [pl.BlockSpec(memory_space=pltpu.HBM)] * len(weights),
        out_specs=[vmem()] * (len(weights) + 1),
        scratch_shapes=[pltpu.SemaphoreType.DMA((len(weights),))],
        compiler_params=params(8),
        cost_estimate=pl.CostEstimate(flops=0, bytes_accessed=2 * sum(w.nbytes for w in weights), transcendentals=0),
        name="load_weights",
    )(after, *[pltpu.with_memory_space_constraint(w, pltpu.HBM) for w in weights])


def run_ffn(groups, weights, turn, share, cut=1):
    pieces = [p for own, other in groups for p in (*own, *other)]
    rows = sum(p.shape[0] for p in groups[0][0])
    depth, hidden = weights[0].shape
    total = 2 * rows * len(groups)
    part = jax.ShapeDtypeStruct((depth // share, rows, share), bf16)
    piece = jax.ShapeDtypeStruct((depth // share // cut, rows, share), bf16)
    weights = [pltpu.with_memory_space_constraint(w, pltpu.VMEM) for w in weights]
    return pl.pallas_call(
        functools.partial(feed_forward, groups=tuple((len(own), len(other)) for own, other in groups), cut=cut),
        out_shape=(part, *(piece,) * cut) * len(groups) + (jax.ShapeDtypeStruct(turn.shape, turn.dtype),),
        in_specs=[vmem()] * (len(pieces) + 4),
        out_specs=(vmem(),) * ((cut + 1) * len(groups) + 1),
        scratch_shapes=[pltpu.VMEM((total, depth), bf16), pltpu.VMEM((total, hidden), bf16)],
        compiler_params=params(12),
        cost_estimate=pl.CostEstimate(
            flops=6 * total * depth * hidden, bytes_accessed=4 * total * depth, transcendentals=0
        ),
        name="feed_forward",
    )(*pieces, *weights, turn)


def run_add(*parts, dtype=bf16, bytes_accessed=MIB):
    parts = [p if isinstance(p, list) else [p] for p in parts]
    flat = [piece for p in parts for piece in p]
    return pl.pallas_call(
        functools.partial(add_up, pieces=tuple(len(p) for p in parts)),
        out_shape=jax.ShapeDtypeStruct((sum(p.shape[0] for p in parts[0]), *flat[0].shape[1:]), dtype),
        in_specs=[vmem()] * len(flat),
        out_specs=vmem(),
        compiler_params=params(8),
        cost_estimate=pl.CostEstimate(flops=0, bytes_accessed=bytes_accessed, transcendentals=0),
        name="add_up",
    )(*flat)


def run_combine(recv, ids, weights, res):
    return pl.pallas_call(
        combine,
        out_shape=jax.ShapeDtypeStruct(res.shape, bf16),
        in_specs=[vmem()] * 4,
        out_specs=vmem(),
        compiler_params=params(16),
        name="combine",
    )(recv, ids, weights, res)


def on_device(
    mixer_input, gate_in, step_size, decay_rate, state_in, state_out, skip, out_proj, hidden_in, norm_gain,
    w_gate, w_up, w_down, route_ids, route_weight,
):
    slab_len, prompts, channels = mixer_input.shape
    tokens = slab_len * prompts
    share = hidden_in.shape[2]
    chips = lax.axis_size("y")
    ctx, exp = ("y", "core"), ("x", "z")
    experts = lax.axis_size(exp) * w_gate.shape[0]
    slots = 4 * tokens // experts
    turns = slab_len // SUBS

    def swap(value):
        return lax.ppermute(value, "core", [(0, 1), (1, 0)])

    def ring(value, d):
        return lax.ppermute(value, "y", [(i, (i + d) % chips) for i in range(chips)])

    proj = lax.all_gather(out_proj, ctx)
    sig = mixer_input.reshape(tokens, channels)
    step = step_size.reshape(tokens, channels)
    into = scan_tables(state_in, turns)
    end, before, pre = run_first(step, sig, into, decay_rate, prompts)
    coords = jnp.stack([lax.axis_index(a).astype(jnp.int32) for a in ("core", "x", "z")])
    sib = swap(end)
    pair = run_pair(coords, end, sib, decay_rate)
    gate_in, state_out, pair = lax.optimization_barrier((gate_in, state_out, pair))
    pairs = [
        lax.ppermute(pair, "y", [(i, i + d) for i in range(chips - d)]) for d in range(chips - 1, 0, -1)
    ]
    gate = gate_in.reshape(tokens, channels)
    outof = scan_tables(state_out, turns)
    mixed = run_second(
        coords, step, sig, gate, into, outof, decay_rate, skip.reshape(1, channels), before, pre, sib, pairs
    )
    sides = (lax.axis_size("x"), lax.axis_size("z"))

    def shift(value, axis, d):
        n = lax.axis_size(axis)
        return lax.ppermute(value, axis, [(i, (i + d) % n) for i in range(n)]) if d else value

    def spread_out(one, one_axis, two, two_axis):
        sides = ((one, one_axis), (two, two_axis))
        ways = [(i, d) for i, (parts, _) in enumerate(sides) for d in range(len(parts))]
        hops = {(i, d): min(d, len(sides[i][0]) - d) for i, d in ways}
        lead = (0, 1)
        ways = sorted(ways, key=lambda w: (w != lead, -hops[w], w[1], w[0]))
        return [shift(sides[i][0][d], sides[i][1], d) for i, d in ways], tuple(ways)

    nx, nz = sides
    ids = route_ids.reshape(tokens, -1)
    *parts, by_choice = run_project(coords, mixed, ids.T, proj, share, sides)
    hidden = hidden_in.reshape(tokens, share)
    parts, ways = spread_out(parts[:nz], "z", parts[nz:], "x")
    parts = run_fold(coords, parts, sides, ways)
    parts, ways = spread_out(parts[:nx], "x", parts[nx:], "z")
    residual, slot_rows = run_dispatch(parts, hidden, by_choice, experts, slots, ways)
    whole = lax.all_to_all(slot_rows, exp, 0, 0, tiled=True)
    own = run_normalize(whole, norm_gain.reshape(1, -1))

    half = slots // 2
    own_sib = swap(own)
    low = ring(own, 1)
    high = ring(own, -1)
    *weights, turn = run_load(own, w_gate[0], w_up[0], w_down[0])
    own_sib, turn = lax.optimization_barrier((own_sib, turn))
    mine0, other0, turn = run_ffn([([own], [own_sib])], weights, turn, share)
    low, high, turn = lax.optimization_barrier((low, high, turn))
    from0 = swap(other0)
    far_low, far_high = ring(low[:half], 1), ring(high[half:], -1)
    low_sib, high_sib = swap(low), swap(high)
    low_sib, from0 = lax.optimization_barrier((low_sib, from0))
    mine1, other1, mine3, other3, turn = run_ffn([([low], [low_sib]), ([high], [high_sib])], weights, turn, share)
    far_low, far_high, turn, other1, other3 = lax.optimization_barrier((far_low, far_high, turn, other1, other3))
    far_low_sib, far_high_sib = swap(far_low), swap(far_high)
    low_sum, high_sum = run_add(mine1, swap(other1)), run_add(mine3, swap(other3))
    low_sum, high_sum, turn = lax.optimization_barrier((low_sum, high_sum, turn))
    back1, back3 = ring(low_sum, -1), ring(high_sum, 1)
    mine2, other2, turn = run_ffn([([far_low, far_high], [far_low_sib, far_high_sib])], weights, turn, share)
    far_swap = swap(other2)
    back1, back3, far_swap = lax.optimization_barrier((back1, back3, far_swap))
    near = run_add(mine0, from0, back1, back3, dtype=f32)
    back2 = ring(run_add(mine2, far_swap), 2)
    returned = run_add(near, back2)

    back = lax.all_to_all(returned, exp, 0, 0, tiled=True)
    out = run_combine(back, ids, route_weight.reshape(tokens, -1), residual)
    return out.reshape(slab_len, prompts, share)


def solution(mesh):
    ctx, exp = ("y", "core"), ("x", "z")
    n_ctx, n_exp = mesh.devices.shape
    side = int(round(n_exp**0.5))
    mesh = Mesh(mesh.devices.reshape(n_ctx // 2, 2, side, n_exp // side), ctx + exp)
    placed = (
        P(ctx, None, exp),
        P(ctx, None, exp),
        P(ctx, None, exp),
        P(None, exp),
        P(ctx, None, None),
        P(ctx, None, None),
        P(exp),
        P(exp, ctx),
        P(ctx, None, exp),
        P(),
        P(exp, None, ctx),
        P(exp, None, ctx),
        P(exp, ctx, None),
        P(ctx, None, None),
        P(ctx, None, None),
    )
    return jax.shard_map(on_device, mesh=mesh, in_specs=placed, out_specs=P(ctx, None, exp), check_vma=False)
```
